32 devices in a mesh: gx: 16 (over z, x, core), gy: 2 (over y).
Axes of the slice: x: 2, y: 2, z: 4, core: 2. Of those that a mesh axis runs over, the one named last changes fastest.
Arguments:
- adjoint: bfloat16 [256, 256, 512], P('gx', 'gy'), may hold values from -6 to 6
- conduct_x: float32 [256, 256], P('gx', 'gy'), may hold values from 0.02 to 0.24
- conduct_y: float32 [256, 256], P('gx', 'gy'), may hold values from 0.02 to 0.24
- pick_weights: bfloat16 [64, 256, 256], P(None, 'gx', 'gy'), may hold values from -0.03125 to 0.03125
- owner_order: int32 [64], replicated, may hold values from 0 to 63, each once
Outputs:
- smoothed: bfloat16 [256, 256, 512], P('gx', 'gy')
- representer: float32 [64, 512], P(('gx', 'gy'))
The draws below stay inside these ranges and needn't reach their ends.
Inputs may be any that keep to these rules, and one draw needn't show every extreme that they name: `owner_order`: each of 0 to 63 appears once.
All inputs are finite; a program needn't handle non-finite values.
Results may differ from the reference program's by a relative error of at most 0.0029.
Values may be sent and summed in bfloat16 or wider, within the bound.
A program may use at most 64 MiB of HBM per device.

```python
import math
import jax
import jax.numpy as jnp

PANEL = 256
PANELS = 2
STEPS = 4
COLUMNS = 512
PICKS = 64
NX = 256
NY = 256


def raised(entries, stream_key, source, target, shards_of, factor):
    owner, partner = [(jnp.arange(entries.shape[axis_at]) // (entries.shape[axis_at] // shards_of)).reshape([-1 if axis == axis_at else 1 for axis in range(entries.ndim)]) for axis_at in (source, target)]
    chosen = jax.random.permutation(stream_key, shards_of)[partner]
    strong = (owner == chosen) | (owner == (partner + shards_of // 2) % shards_of)
    return jnp.where(strong, factor * entries, entries)


def shard_levels(stream_key, dims, shards, smallest, largest):
    level = 1.0
    for axis_at, shards_of in shards:
        steps = jax.random.uniform(jax.random.fold_in(jax.random.fold_in(stream_key, 6), axis_at), (shards_of,), jnp.float32, smallest / len(shards), largest / len(shards))
        level = level * jnp.repeat(jnp.exp(steps), dims[axis_at] // shards_of).reshape((-1,) + (1,) * (len(dims) - 1 - axis_at))
    return level


def normal_values(stream_key, extent, deviation, reach, split=(), kind=jnp.bfloat16):
    values = deviation * jax.random.normal(stream_key, extent, jnp.float32)
    if split:
        values = values * shard_levels(stream_key, extent, split, -0.22, 0.18)
    return jnp.clip(values, -reach, reach).astype(kind)


def bell_draw_with(rng, extent, deviation, reach, split, heavy, kind=jnp.bfloat16):
    drawn = deviation * jax.random.normal(rng, extent, jnp.float32)
    if split:
        drawn = drawn * shard_levels(rng, extent, split, -0.22, 0.18)
    return jnp.clip(raised(drawn, jax.random.fold_in(rng, 3), *heavy), -reach, reach).astype(kind)


def setup_inputs(seed: int = 0) -> dict:
    splits = jax.random.split(jax.random.key(seed), 6)
    return {
        "adjoint": normal_values(splits[0], (NX, NY, COLUMNS), 1.0, 6.0, ((0, 16), (1, 2))),
        "conduct_x": jnp.clip(jnp.exp(math.log(0.24) - 2.4849066 * jax.random.uniform(splits[1], (NX, NY), jnp.float32) ** shard_levels(splits[1], (NX, NY), ((0, 16), (1, 2)), -0.2, 0.2)), 0.02, 0.24),
        "conduct_y": jnp.clip(jnp.exp(math.log(0.24) - 2.4849066 * jax.random.uniform(splits[2], (NX, NY), jnp.float32) ** shard_levels(splits[2], (NX, NY), ((0, 16), (1, 2)), -0.2, 0.2)), 0.02, 0.24),
        "pick_weights": bell_draw_with(splits[3], (PICKS, NX, NY), (NX * NY) ** -0.5, 0.03125, ((1, 16), (2, 2)), (1, 0, 16, 2.0)),
        "owner_order": jax.random.permutation(splits[4], PICKS).astype(jnp.int32),
    }


def diffuse(field, conx, cony):
    centre = field[1:-1, 1:-1]
    above = field[:-2, 1:-1]
    below = field[2:, 1:-1]
    leftside = field[1:-1, :-2]
    rightside = field[1:-1, 2:]
    result = centre + conx[:-2, 1:-1, None] * (above - centre)
    result = result + conx[1:-1, 1:-1, None] * (below - centre)
    result = result + cony[1:-1, :-2, None] * (leftside - centre)
    result = result + cony[1:-1, 1:-1, None] * (rightside - centre)
    return result


def reference(adjoint, conduct_x, conduct_y, pick_weights, owner_order):
    rows_idx = jnp.arange(NX, dtype=jnp.int32)[:, None]
    cols_idx = jnp.arange(NY, dtype=jnp.int32)[None, :]
    conx = jnp.where(rows_idx < NX - 1, conduct_x, jnp.float32(0.0))
    cony = jnp.where(cols_idx < NY - 1, conduct_y, jnp.float32(0.0))
    conx_pad = jnp.pad(conx, 1)
    cony_pad = jnp.pad(cony, 1)
    flat_weights = pick_weights.reshape(PICKS, NX * NY)
    smooth_list = []
    repr_list = []
    for panel in range(PANELS):
        field = adjoint[:, :, panel * PANEL:(panel + 1) * PANEL].astype(jnp.float32)
        for step in range(STEPS):
            field = diffuse(jnp.pad(field, ((1, 1), (1, 1), (0, 0))), conx_pad, cony_pad)
        rounded = field.astype(jnp.bfloat16)
        smooth_list.append(rounded)
        partial_value = jnp.dot(flat_weights, rounded.reshape(NX * NY, PANEL), preferred_element_type=jnp.float32)
        repr_list.append(jnp.take(partial_value, owner_order, axis=0))
    return jnp.concatenate(smooth_list, axis=2), jnp.concatenate(repr_list, axis=1)
```

```python
import functools

import jax
import jax.numpy as jnp
from jax import lax
from jax.experimental import pallas as pl
from jax.experimental.pallas import tpu as pltpu
from jax.sharding import PartitionSpec as P

STEPS = 4
LANES = 128
SUB = 8
CHUNK = 128
MESH = pl.DeviceIdType.MESH
DIRS = ((0, 1), (0, -1), (1, 1), (1, -1), (-1, 1), (-1, -1), (1, 0), (-1, 0))
F32 = jnp.float32
BF16 = jnp.bfloat16
NEAR = [(a, b) for a in range(-2, 3) for b in range(-2, 3) if abs(a) + abs(b) <= 2]
FAR = [(a, b) for a in range(-4, 5) for b in range(-4, 5) if abs(a) + abs(b) <= 4]


def dir_id(dx, dy):
    return DIRS.index((dx, dy))


def centre(dx):
    return SUB * (dx + STEPS) + SUB


def kernel(
    nx, ny, adj, kx_hbm, ky_hbm, w_hbm, order_ref, out, rep,
    ub, xh, yb, y_rows, kk, shifted, coef, band, band_lo, fringe, acc,
    wv, w32, wt, ps, rbuf,
    own_sem, w_sem, k_load, a_send, a_recv, k_send, k_recv, r_send, r_recv,
):
    cx, cy, cols = adj.shape
    groups = cols // LANES
    chunks = cols // CHUNK
    ex = cx + 2 * STEPS
    picks = w_hbm.shape[0]
    n = nx * ny
    tile = ps.shape[0] // n
    kf = y_rows.shape[0]
    span = 2 * STEPS + 2
    gx = lax.axis_index("gx")
    gy = lax.axis_index("gy")
    me = gx * ny + gy

    def dev(t):
        return (t // ny, lax.rem(t, ny))

    barrier = pltpu.get_barrier_semaphore()

    @pl.loop(1, n)
    def _(k):
        pl.semaphore_signal(
            barrier, inc=1, device_id=dev(lax.rem(me + k, n)), device_id_type=MESH
        )

    own_rows, own_lanes = pl.ds(SUB, cx), pl.ds(LANES, LANES)
    k_loads = [
        pltpu.make_async_copy(src, kk.at[a, own_rows, own_lanes], k_load.at[a])
        for a, src in enumerate((kx_hbm, ky_hbm))
    ]
    own = pltpu.make_async_copy(adj, ub, own_sem)
    w_load = pltpu.make_async_copy(w_hbm, wv, w_sem)
    for c in k_loads + [w_load, own]:
        c.start()

    def present(dx, dy):
        ok = None
        for d, g, size in ((dx, gx, nx), (dy, gy, ny)):
            if d == 1:
                c = g < size - 1
            elif d == -1:
                c = g > 0
            else:
                continue
            ok = c if ok is None else jnp.logical_and(ok, c)
        return ok

    def k_region(sx, sy):
        rows = {-1: pl.ds(0, SUB), 0: own_rows, 1: pl.ds(SUB + cx, SUB)}[sx]
        return kk.at[:, rows, pl.ds(LANES * (1 + sy), LANES)]

    def a_region(sx, sy):
        if sy == 0:
            return xh.at[0 if sx == -1 else 1]
        rows = {-1: pl.ds(0, STEPS), 0: pl.ds(STEPS, cx), 1: pl.ds(STEPS + cx, STEPS)}[sx]
        return yb.at[0 if sy == 1 else 1, rows]

    def k_copy(dx, dy):
        rows = {1: pl.ds(cx, SUB), 0: own_rows, -1: pl.ds(SUB, SUB)}[dx]
        return pltpu.make_async_remote_copy(
            src_ref=kk.at[:, rows, own_lanes], dst_ref=k_region(-dx, -dy),
            send_sem=k_send.at[dir_id(dx, dy)], recv_sem=k_recv.at[dir_id(-dx, -dy)],
            device_id=(gx + dx, gy + dy), device_id_type=MESH,
        )

    def a_copies(dx, dy):
        slot, mine = dir_id(-dx, -dy), dir_id(dx, dy)
        src = adj
        if dx:
            src = src.at[pl.ds(cx - STEPS if dx == 1 else 0, STEPS)]
        if dy:
            src = src.at[:, pl.ds(cy - SUB if dy == 1 else 0, SUB)]
        dst = a_region(-dx, -dy)
        parts = [(src, dst)]
        if dy == 0:
            cut = [pl.ds(q * CHUNK, CHUNK) for q in range(chunks)]
            parts = [(src.at[:, :, c], dst.at[:, :, c]) for c in cut]
        return [
            pltpu.make_async_remote_copy(
                src_ref=s, dst_ref=d, send_sem=a_send.at[mine, q],
                recv_sem=a_recv.at[slot, q], device_id=(gx + dx, gy + dy),
                device_id_type=MESH,
            )
            for q, (s, d) in enumerate(parts)
        ]

    for dx, dy in DIRS:
        @pl.when(jnp.logical_not(present(dx, dy)))
        def _(dx=dx, dy=dy):
            k_part, a_part = k_region(dx, dy), a_region(dx, dy)
            k_part[...] = jnp.zeros(k_part.shape, F32)
            a_part[...] = jnp.zeros(a_part.shape, BF16)

    for c in k_loads:
        c.wait()
    pl.semaphore_wait(barrier, n - 1)

    for dx, dy in DIRS:
        @pl.when(present(dx, dy))
        def _(dx=dx, dy=dy):
            k_copy(dx, dy).start()

    for dx, dy in DIRS[:6]:
        @pl.when(present(dx, dy))
        def _(dx=dx, dy=dy):
            for c in a_copies(dx, dy):
                c.start()

    for q in range(chunks):
        for dx, dy in DIRS[6:]:
            @pl.when(present(dx, dy))
            def _(dx=dx, dy=dy, q=q):
                a_copies(dx, dy)[q].start()

    def wait_k(dx, dy):
        @pl.when(present(dx, dy))
        def _():
            part = k_region(dx, dy)
            pltpu.make_async_copy(part, part, k_recv.at[dir_id(dx, dy)]).wait()

    def wait_a(dx, dy, q=0):
        @pl.when(present(dx, dy))
        def _():
            part = a_region(dx, dy)
            if dy == 0:
                part = part.at[:, :, pl.ds(q * CHUNK, CHUNK)]
            pltpu.make_async_copy(part, part, a_recv.at[dir_id(dx, dy), q]).wait()

    w_load.wait()
    pick_ids = lax.broadcasted_iota(jnp.int32, (picks, picks), 0)
    chosen = jnp.where(pick_ids == order_ref[...], F32(1), F32(0)).astype(BF16)
    w32[...] = wv[...].astype(F32).reshape(picks * cx, LANES)
    for x in range(cx):
        row = w32[pl.ds(x, picks, stride=cx), :].astype(BF16)
        row = lax.dot_general(
            chosen, row, (((0,), (0,)), ((), ())), preferred_element_type=F32
        )
        wt[:, x * LANES : (x + 1) * LANES] = row.astype(BF16)

    zero_block = jnp.zeros((LANES, LANES), BF16)
    for x in range(cx):
        rows = slice(x * LANES, (x + 1) * LANES)
        r = 0 if x % 2 else span - 1
        band[rows, r * LANES : (r + 1) * LANES] = zero_block
        r = 0 if x % 2 else 3
        band_lo[rows, r * LANES : (r + 1) * LANES] = zero_block
    y_rows[...] = jnp.zeros(y_rows.shape, BF16)

    for d in DIRS:
        wait_k(*d)

    kx, ky = kk[0], kk[1]
    kx_at = lax.broadcasted_iota(jnp.int32, kx.shape, 0)
    ky_at = lax.broadcasted_iota(jnp.int32, ky.shape, 1)
    kx = jnp.where(jnp.logical_and(kx_at == SUB + cx - 1, gx == nx - 1), F32(0), kx)
    ky = jnp.where(jnp.logical_and(ky_at == 2 * LANES - 1, gy == ny - 1), F32(0), ky)
    high, wide = kx.shape

    def at(value, dx, dy):
        if dx:
            value = pltpu.roll(value, -dx % high, 0)
        if dy:
            value = pltpu.roll(value, -dy % wide, 1)
        return value

    xp, yp = kx, ky
    xm, ym = at(kx, -1, 0), at(ky, 0, -1)
    c = F32(1) - ((xm + xp) + (ym + yp))
    two = {
        (0, 0): c * c + ((xm * xm + xp * xp) + (ym * ym + yp * yp)),
        (1, 0): xp * (c + at(c, 1, 0)),
        (-1, 0): xm * (c + at(c, -1, 0)),
        (0, 1): yp * (c + at(c, 0, 1)),
        (0, -1): ym * (c + at(c, 0, -1)),
        (2, 0): xp * at(xp, 1, 0),
        (-2, 0): xm * at(xm, -1, 0),
        (0, 2): yp * at(yp, 0, 1),
        (0, -2): ym * at(ym, 0, -1),
        (1, 1): xp * at(yp, 1, 0) + yp * at(xp, 0, 1),
        (1, -1): xp * at(ym, 1, 0) + ym * at(xp, 0, -1),
        (-1, 1): xm * at(yp, -1, 0) + yp * at(xm, 0, 1),
        (-1, -1): xm * at(ym, -1, 0) + ym * at(xm, 0, -1),
    }
    for i, d in enumerate(NEAR):
        for dy in range(-2, 3):
            shifted[(dy + 2) * len(NEAR) + i] = at(two[d], 0, dy)[:, LANES : 2 * LANES]

    def near(d, dx, dy):
        return shifted[(dy + 2) * len(NEAR) + NEAR.index(d), SUB + dx : SUB + dx + cx]

    for fx, fy in FAR:
        total = None
        for dx, dy in NEAR:
            rest = (fx - dx, fy - dy)
            if rest in NEAR:
                term = near((dx, dy), 0, 0) * near(rest, dx, dy)
                total = term if total is None else total + term
        slot = centre(fx) + fy
        coef[slot * cx : (slot + 1) * cx, :] = total

    lane = lax.broadcasted_iota(jnp.int32, (LANES, LANES), 1)
    left_half = lax.broadcasted_iota(jnp.int32, (SUB, LANES), 1) < LANES // 2

    def low_part(value):
        high_part = value.astype(BF16)
        return high_part, (value - high_part.astype(F32)).astype(BF16)

    def build(x):
        table = coef[pl.ds(x, LANES, stride=cx), :].T
        rows = slice(x * LANES, (x + 1) * LANES)
        sides = [[None] * (kf // LANES) for _ in range(2)]
        for dx in range(-STEPS, STEPS + 1):
            reach = STEPS - abs(dx)
            mid = centre(dx)
            mask = jnp.logical_and(lane >= mid - reach, lane <= mid + reach)
            diag = pltpu.roll(
                jnp.where(mask, table, F32(0)), LANES - mid, 1, stride=1, stride_axis=0
            )
            top, bottom = diag[:SUB], diag[cy - SUB :]
            block = jnp.concatenate(
                [
                    jnp.where(left_half, top, F32(0)),
                    diag[SUB : cy - SUB],
                    jnp.where(left_half, F32(0), bottom),
                ],
                axis=0,
            )
            r = x % 2 + dx + STEPS
            big, small = low_part(block)
            band[rows, r * LANES : (r + 1) * LANES] = big
            if abs(dx) <= 1:
                r = x % 2 + dx + 1
                band_lo[rows, r * LANES : (r + 1) * LANES] = small
            if reach:
                e = x + dx + STEPS
                place, home = SUB * e % LANES, SUB * e // LANES
                before = jnp.where(left_half, F32(0), top)
                after = jnp.where(left_half, bottom, F32(0))
                for i, (part, by) in enumerate(((before, place + SUB), (after, place))):
                    if by % LANES:
                        part = pltpu.roll(part, by % LANES, 1)
                    old = sides[i][home]
                    sides[i][home] = part if old is None else old + part
        zero = jnp.zeros((SUB, LANES), F32)
        edge = jnp.concatenate(
            [
                jnp.concatenate([zero if p is None else p for p in side], axis=1)
                for side in sides
            ],
            axis=0,
        )
        big, small = low_part(edge)
        fringe[x * 2 * SUB : (x + 1) * 2 * SUB, :kf] = big
        fringe[x * 2 * SUB : (x + 1) * 2 * SUB, kf:] = small

    low_row = lax.broadcasted_iota(jnp.int32, (SUB, cols), 0) < STEPS

    def fill_fringe(lo, hi):
        for e in range(lo, hi, 2):
            pair = [
                jnp.where(low_row, yb[0, e + i].astype(F32), yb[1, e + i].astype(F32))
                for i in range(2)
            ]
            y_rows[e * SUB : (e + 2) * SUB, :] = jnp.concatenate(pair, axis=0).astype(BF16)

    def fringe_dot(lo, hi):
        rows = slice(lo * 2 * SUB, hi * 2 * SUB)
        y = y_rows[...]
        return jnp.dot(fringe[rows, :kf], y, preferred_element_type=F32) + jnp.dot(
            fringe[rows, kf:], y, preferred_element_type=F32
        )

    def own_dot(i, side):
        rows = slice(i * LANES, (i + 2) * LANES)
        value = None
        for mat, reach, ahead in ((band, STEPS, STEPS + 1), (band_lo, 1, 2)):
            lo, hi = max(i - reach, 0), min(i + ahead, cx - 1) + 1
            term = jnp.dot(
                mat[rows, (lo - i + reach) * LANES : (hi - i + reach) * LANES],
                ub[lo:hi].reshape((hi - lo) * cy, cols),
                preferred_element_type=F32,
            )
            value = term if value is None else value + term
        pieces = []
        for j in range(2):
            v = value[j * LANES : (j + 1) * LANES]
            s = side[j * 2 * SUB : (j + 1) * 2 * SUB]
            pieces += [v[:SUB] + s[:SUB], v[SUB : cy - SUB], v[cy - SUB :] + s[SUB:]]
        return jnp.concatenate(pieces, axis=0)

    inner = list(range(STEPS, cx - STEPS, 2))
    outer = [i for i in range(0, cx, 2) if i not in inner]
    for i in inner:
        build(i)
        build(i + 1)

    own.wait()
    for d in DIRS[:2]:
        wait_a(*d)
    fill_fringe(STEPS, STEPS + cx)
    sides = fringe_dot(STEPS, cx - STEPS)
    for j, i in enumerate(inner):
        value = own_dot(i, sides[j * 4 * SUB : (j + 1) * 4 * SUB])
        out[i : i + 2] = value.astype(BF16).reshape(2, cy, cols)
    for i in outer:
        build(i)
        build(i + 1)

    for d in DIRS[2:6]:
        wait_a(*d)
    fill_fringe(0, STEPS)
    fill_fringe(STEPS + cx, ex)
    sides = [fringe_dot(0, STEPS), fringe_dot(cx - STEPS, cx)]
    for j, i in enumerate(outer):
        s = sides[0 if i < STEPS else 1]
        k = i if i < STEPS else i - (cx - STEPS)
        acc[j * 2 * LANES : (j + 1) * 2 * LANES, :] = own_dot(
            i, s[k * 2 * SUB : (k + 2) * 2 * SUB]
        )

    def product(lo, hi, part):
        return jnp.dot(
            wt[:, lo * LANES : hi * LANES],
            out[lo:hi, :, part].reshape((hi - lo) * cy, part.stop - part.start),
            preferred_element_type=F32,
        )

    middle = product(STEPS, cx - STEPS, slice(0, cols))

    def halo_dot(i, part):
        rows = slice(i * LANES, (i + 2) * LANES)
        terms = []
        for mat, reach, ahead in ((band, STEPS, STEPS + 1), (band_lo, 1, 2)):
            if i < STEPS:
                lo, hi, source, base = i - reach, 0, 0, STEPS
            else:
                lo, hi, source, base = cx, i + ahead + 1, 1, -cx
            if lo >= hi:
                continue
            terms.append(
                jnp.dot(
                    mat[rows, (lo - i + reach) * LANES : (hi - i + reach) * LANES],
                    xh[source, lo + base : hi + base, :, part].reshape((hi - lo) * cy, CHUNK),
                    preferred_element_type=F32,
                )
            )
        return functools.reduce(jnp.add, terms)

    for q in range(chunks):
        part = slice(q * CHUNK, (q + 1) * CHUNK)
        for d in DIRS[6:]:
            wait_a(*d, q)
        for j, i in enumerate(outer):
            value = acc[j * 2 * LANES : (j + 1) * 2 * LANES, part] + halo_dot(i, part)
            out[i : i + 2, :, part] = value.astype(BF16).reshape(2, cy, CHUNK)
        total = middle[:, part] + product(0, STEPS, part) + product(cx - STEPS, cx, part)
        for g in range(CHUNK // LANES):
            at_group = q * (CHUNK // LANES) + g
            ps[pl.ds(at_group, picks, stride=groups), :] = total[:, g * LANES : (g + 1) * LANES]

    def reduce_copy(k):
        t = lax.rem(me + k, n)
        return pltpu.make_async_remote_copy(
            src_ref=ps.at[pl.ds(pl.multiple_of(t * tile, tile), tile)],
            dst_ref=rbuf.at[k - 1], send_sem=r_send.at[k - 1], recv_sem=r_recv.at[k - 1],
            device_id=dev(t), device_id_type=MESH,
        )

    @pl.loop(1, n)
    def _(k):
        reduce_copy(k).start()

    for dx, dy in DIRS:
        @pl.when(present(dx, dy))
        def _(dx=dx, dy=dy):
            k_copy(dx, dy).wait_send()
            for c in a_copies(dx, dy):
                c.wait_send()

    @pl.loop(1, n)
    def _(k):
        reduce_copy(k).wait()

    total = ps[pl.ds(pl.multiple_of(me * tile, tile), tile), :]
    total = total + jnp.sum(rbuf[...], axis=0)
    for r in range(tile // groups):
        for q in range(groups):
            rep[r : r + 1, q * LANES : (q + 1) * LANES] = total[
                r * groups + q : r * groups + q + 1
            ]


def store_kernel(field, owned, field_out, owned_out, sems):
    parts = sems.shape[0] - 1
    rows = field.shape[0] // parts
    copies = [pltpu.make_async_copy(owned, owned_out, sems.at[parts])]
    for p in range(parts):
        part = pl.ds(p * rows, rows)
        copies.append(pltpu.make_async_copy(field.at[part], field_out.at[part], sems.at[p]))
    for c in copies:
        c.start()
    for c in copies:
        c.wait()


def solution(mesh):
    nx, ny = mesh.shape["gx"], mesh.shape["gy"]
    n = nx * ny

    def per_device(adjoint, conduct_x, conduct_y, pick_weights, owner_order):
        cx, cy, cols = adjoint.shape
        picks = pick_weights.shape[0]
        groups = cols // LANES
        chunks = cols // CHUNK
        ex = cx + 2 * STEPS
        tile = picks // n * groups
        kf = -(-ex * SUB // LANES) * LANES
        vmem = pl.BlockSpec(memory_space=pltpu.VMEM)
        hbm = pl.BlockSpec(memory_space=pl.ANY)
        dma = pltpu.SemaphoreType.DMA
        span = 2 * STEPS + 2
        field, owned = pl.pallas_call(
            functools.partial(kernel, nx, ny),
            out_shape=(
                pltpu.VMEM((cx, cy, cols), BF16),
                pltpu.VMEM((picks // n, cols), F32),
            ),
            in_specs=[hbm] * 4 + [vmem],
            out_specs=(vmem, vmem),
            scratch_shapes=[
                pltpu.VMEM((cx, cy, cols), BF16),
                pltpu.VMEM((2, STEPS, cy, cols), BF16),
                pltpu.VMEM((2, ex, SUB, cols), BF16),
                pltpu.VMEM((kf, cols), BF16),
                pltpu.VMEM((2, cx + 2 * SUB, 3 * LANES), F32),
                pltpu.VMEM((5 * len(NEAR), cx + 2 * SUB, LANES), F32),
                pltpu.VMEM((LANES * cx, LANES), F32),
                pltpu.VMEM((cx * cy, span * LANES), BF16),
                pltpu.VMEM((cx * cy, 4 * LANES), BF16),
                pltpu.VMEM((cx * 2 * SUB, 2 * kf), BF16),
                pltpu.VMEM((2 * STEPS * cy, cols), F32),
                pltpu.VMEM((picks, cx, cy), BF16),
                pltpu.VMEM((picks * cx, LANES), F32),
                pltpu.VMEM((picks, cx * cy), BF16),
                pltpu.VMEM((picks * groups, LANES), F32),
                pltpu.VMEM((n - 1, tile, LANES), F32),
                dma,
                dma,
                dma((2,)),
                dma((len(DIRS), chunks)),
                dma((len(DIRS), chunks)),
                dma((len(DIRS),)),
                dma((len(DIRS),)),
                dma((n - 1,)),
                dma((n - 1,)),
            ],
            compiler_params=pltpu.CompilerParams(
                collective_id=0, has_side_effects=True, vmem_limit_bytes=56 << 20
            ),
        )(adjoint, conduct_x, conduct_y, pick_weights, owner_order.reshape(1, picks))
        return pl.pallas_call(
            store_kernel,
            out_shape=(
                jax.ShapeDtypeStruct((cx, cy, cols), BF16),
                jax.ShapeDtypeStruct((picks // n, cols), F32),
            ),
            in_specs=[vmem, vmem],
            out_specs=(hbm, hbm),
            scratch_shapes=[dma((5,))],
        )(field, owned)

    return jax.shard_map(
        per_device,
        mesh=mesh,
        in_specs=(P("gx", "gy", None), P("gx", "gy"), P("gx", "gy"), P(None, "gx", "gy"), P()),
        out_specs=(P("gx", "gy", None), P(("gx", "gy"), None)),
        check_vma=False,
    )
```

```python
import functools

import jax
import jax.numpy as jnp
from jax import lax
from jax.experimental import pallas as pl
from jax.experimental.pallas import tpu as pltpu
from jax.sharding import PartitionSpec as P

STEPS = 4
LANES = 128
SUB = 8
CHUNK = 256
PLANE = 4
MESH = pl.DeviceIdType.MESH
DIRS = ((0, 1), (0, -1), (1, 1), (1, -1), (-1, 1), (-1, -1), (1, 0), (-1, 0))
F32 = jnp.float32
BF16 = jnp.bfloat16
NEAR = [(a, b) for a in range(-2, 3) for b in range(-2, 3) if abs(a) + abs(b) <= 2]
FAR = [(a, b) for a in range(-4, 5) for b in range(-4, 5) if abs(a) + abs(b) <= 4]


def dir_id(dx, dy):
    return DIRS.index((dx, dy))


def centre(dx):
    return SUB * (dx + STEPS) + SUB


def kernel(
    nx, ny, adj, kx_hbm, ky_hbm, w_hbm, order_ref, out, rep,
    ub, xh, yb, y_rows, kk, shifted, coef, band, fringe, cells, acc,
    wv, w32, wt, ps, rbuf,
    own_sem, w_sem, k_load, a_send, a_recv, k_send, k_recv, r_send, r_recv, planes,
):
    cx, cy, cols = adj.shape
    groups = cols // LANES
    chunks = cols // CHUNK
    ex = cx + 2 * STEPS
    picks = w_hbm.shape[0]
    n = nx * ny
    tile = ps.shape[0] // n
    kf = y_rows.shape[0]
    span = 2 * STEPS + 4
    gx = lax.axis_index("gx")
    gy = lax.axis_index("gy")
    me = gx * ny + gy
    plane = nx if nx % PLANE else PLANE
    first = gx // plane * plane

    def ahead(i, j, lo, size):
        tx, ty = gx + i, gy + j
        tx = jnp.where(tx >= lo + size, tx - size, tx)
        return tx, jnp.where(ty >= ny, ty - ny, ty)

    def present(dx, dy):
        ok = None
        for d, g, size in ((dx, gx, nx), (dy, gy, ny)):
            if d == 1:
                c = g < size - 1
            elif d == -1:
                c = g > 0
            else:
                continue
            ok = c if ok is None else jnp.logical_and(ok, c)
        return ok

    barrier = pltpu.get_barrier_semaphore()

    def greet(semaphore, target):
        pl.semaphore_signal(semaphore, inc=1, device_id=target, device_id_type=MESH)

    for dx, dy in DIRS:
        if dx:
            @pl.when(present(dx, dy))
            def _(dx=dx, dy=dy):
                greet(barrier, (gx + dx, gy + dy))
    for i in range(plane):
        for j in range(ny):
            if i or j:
                greet(barrier, ahead(i, j, first, plane))
    others = range(plane, nx, plane)
    for i in others:
        greet(barrier, ahead(i, 0, 0, nx))

    own_rows, own_lanes = pl.ds(SUB, cx), pl.ds(LANES, LANES)
    k_loads = [
        pltpu.make_async_copy(src, kk.at[a, own_rows, own_lanes], k_load.at[a])
        for a, src in enumerate((kx_hbm, ky_hbm))
    ]
    own = pltpu.make_async_copy(adj, ub, own_sem)
    w_load = pltpu.make_async_copy(w_hbm, wv, w_sem)
    for c in k_loads + [w_load, own]:
        c.start()

    def k_region(sx, sy):
        rows = {-1: pl.ds(0, SUB), 0: own_rows, 1: pl.ds(SUB + cx, SUB)}[sx]
        return kk.at[:, rows, pl.ds(LANES * (1 + sy), LANES)]

    def a_region(sx, sy):
        if sy == 0:
            return xh.at[0 if sx == -1 else 1]
        rows = {-1: pl.ds(0, STEPS), 0: pl.ds(STEPS, cx), 1: pl.ds(STEPS + cx, STEPS)}[sx]
        return yb.at[0 if sy == 1 else 1, rows]

    def k_copy(dx, dy):
        rows = {1: pl.ds(cx, SUB), 0: own_rows, -1: pl.ds(SUB, SUB)}[dx]
        return pltpu.make_async_remote_copy(
            src_ref=kk.at[:, rows, own_lanes], dst_ref=k_region(-dx, -dy),
            send_sem=k_send.at[dir_id(dx, dy)], recv_sem=k_recv.at[dir_id(-dx, -dy)],
            device_id=(gx + dx, gy + dy), device_id_type=MESH,
        )

    def a_copies(dx, dy):
        slot, mine = dir_id(-dx, -dy), dir_id(dx, dy)
        src = adj
        if dx:
            src = src.at[pl.ds(cx - STEPS if dx == 1 else 0, STEPS)]
        if dy:
            src = src.at[:, pl.ds(cy - SUB if dy == 1 else 0, SUB)]
        dst = a_region(-dx, -dy)
        parts = [(src, dst)]
        if dy == 0:
            cut = [pl.ds(q * CHUNK, CHUNK) for q in range(chunks)]
            parts = [(src.at[:, :, c], dst.at[:, :, c]) for c in cut]
        return [
            pltpu.make_async_remote_copy(
                src_ref=s, dst_ref=d, send_sem=a_send.at[mine, q],
                recv_sem=a_recv.at[slot, q], device_id=(gx + dx, gy + dy),
                device_id_type=MESH,
            )
            for q, (s, d) in enumerate(parts)
        ]

    for dx, dy in DIRS:
        @pl.when(jnp.logical_not(present(dx, dy)))
        def _(dx=dx, dy=dy):
            k_part, a_part = k_region(dx, dy), a_region(dx, dy)
            k_part[...] = jnp.zeros(k_part.shape, F32)
            a_part[...] = jnp.zeros(a_part.shape, BF16)

    for c in k_loads:
        c.wait()
    count = plane * ny - 1 + len(others)
    for dx, dy in DIRS:
        if dx:
            count = count + jnp.where(present(dx, dy), 1, 0)
    pl.semaphore_wait(barrier, count)

    for dx, dy in DIRS:
        @pl.when(present(dx, dy))
        def _(dx=dx, dy=dy):
            k_copy(dx, dy).start()

    for dx, dy in DIRS[:6]:
        @pl.when(present(dx, dy))
        def _(dx=dx, dy=dy):
            for c in a_copies(dx, dy):
                c.start()

    for q in range(chunks):
        for dx, dy in DIRS[6:]:
            @pl.when(present(dx, dy))
            def _(dx=dx, dy=dy, q=q):
                a_copies(dx, dy)[q].start()

    for i in others:
        greet(planes, ahead(i, 0, 0, nx))

    def wait_k(dx, dy):
        @pl.when(present(dx, dy))
        def _():
            part = k_region(dx, dy)
            pltpu.make_async_copy(part, part, k_recv.at[dir_id(dx, dy)]).wait()

    def wait_a(dx, dy, q=0):
        @pl.when(present(dx, dy))
        def _():
            part = a_region(dx, dy)
            if dy == 0:
                part = part.at[:, :, pl.ds(q * CHUNK, CHUNK)]
            pltpu.make_async_copy(part, part, a_recv.at[dir_id(dx, dy), q]).wait()

    w_load.wait()
    pick_ids = lax.broadcasted_iota(jnp.int32, (picks, picks), 0)
    chosen = jnp.where(pick_ids == order_ref[...], F32(1), F32(0)).astype(BF16)
    w32[...] = wv[...].astype(F32).reshape(picks * cx, LANES)
    for x in range(cx):
        row = w32[pl.ds(x, picks, stride=cx), :].astype(BF16)
        row = lax.dot_general(
            chosen, row, (((0,), (0,)), ((), ())), preferred_element_type=F32
        )
        wt[:, x * LANES : (x + 1) * LANES] = row.astype(BF16)

    y_rows[...] = jnp.zeros(y_rows.shape, BF16)

    for d in DIRS:
        wait_k(*d)

    kx, ky = kk[0], kk[1]
    kx_at = lax.broadcasted_iota(jnp.int32, kx.shape, 0)
    ky_at = lax.broadcasted_iota(jnp.int32, ky.shape, 1)
    kx = jnp.where(jnp.logical_and(kx_at == SUB + cx - 1, gx == nx - 1), F32(0), kx)
    ky = jnp.where(jnp.logical_and(ky_at == 2 * LANES - 1, gy == ny - 1), F32(0), ky)
    high, wide = kx.shape

    def at(value, dx, dy):
        if dx:
            value = pltpu.roll(value, -dx % high, 0)
        if dy:
            value = pltpu.roll(value, -dy % wide, 1)
        return value

    xp, yp = kx, ky
    xm, ym = at(kx, -1, 0), at(ky, 0, -1)
    c = F32(1) - ((xm + xp) + (ym + yp))
    two = {
        (0, 0): c * c + ((xm * xm + xp * xp) + (ym * ym + yp * yp)),
        (1, 0): xp * (c + at(c, 1, 0)),
        (-1, 0): xm * (c + at(c, -1, 0)),
        (0, 1): yp * (c + at(c, 0, 1)),
        (0, -1): ym * (c + at(c, 0, -1)),
        (2, 0): xp * at(xp, 1, 0),
        (-2, 0): xm * at(xm, -1, 0),
        (0, 2): yp * at(yp, 0, 1),
        (0, -2): ym * at(ym, 0, -1),
        (1, 1): xp * at(yp, 1, 0) + yp * at(xp, 0, 1),
        (1, -1): xp * at(ym, 1, 0) + ym * at(xp, 0, -1),
        (-1, 1): xm * at(yp, -1, 0) + yp * at(xm, 0, 1),
        (-1, -1): xm * at(ym, -1, 0) + ym * at(xm, 0, -1),
    }
    for i, d in enumerate(NEAR):
        for dy in range(-2, 3):
            shifted[(dy + 2) * len(NEAR) + i] = at(two[d], 0, dy)[:, LANES : 2 * LANES]

    def near(d, dx, dy):
        return shifted[(dy + 2) * len(NEAR) + NEAR.index(d), SUB + dx : SUB + dx + cx]

    for fx, fy in FAR:
        total = None
        for dx, dy in NEAR:
            rest = (fx - dx, fy - dy)
            if rest in NEAR:
                term = near((dx, dy), 0, 0) * near(rest, dx, dy)
                total = term if total is None else total + term
        slot = centre(fx) + fy
        coef[slot * cx : (slot + 1) * cx, :] = total

    lane = lax.broadcasted_iota(jnp.int32, (LANES, LANES), 1)
    left_half = lax.broadcasted_iota(jnp.int32, (SUB, LANES), 1) < LANES // 2

    def low_part(value):
        high_part = value.astype(BF16)
        return high_part, (value - high_part.astype(F32)).astype(BF16)

    def build(x):
        table = coef[pl.ds(x, LANES, stride=cx), :].T
        rows = pl.ds(pl.multiple_of(x * LANES, LANES), LANES)
        before, after = [], []
        for dx in range(-STEPS, STEPS + 1):
            reach = STEPS - abs(dx)
            mid = centre(dx)
            mask = jnp.logical_and(lane >= mid - reach, lane <= mid + reach)
            diag = pltpu.roll(
                jnp.where(mask, table, F32(0)), LANES - mid, 1, stride=1, stride_axis=0
            )
            top, bottom = diag[:SUB], diag[cy - SUB :]
            block = jnp.concatenate(
                [
                    jnp.where(left_half, top, F32(0)),
                    diag[SUB : cy - SUB],
                    jnp.where(left_half, F32(0), bottom),
                ],
                axis=0,
            )
            big, small = low_part(block)
            r = dx + STEPS
            band[rows, r * LANES : (r + 1) * LANES] = big
            if abs(dx) <= 1:
                r = 2 * STEPS + 2 + dx
                band[rows, r * LANES : (r + 1) * LANES] = small
            if reach:
                place = SUB * (dx + STEPS)
                top, bottom = jnp.where(left_half, F32(0), top), jnp.where(left_half, bottom, F32(0))
                before.append(pltpu.roll(top, place + SUB, 1))
                after.append(pltpu.roll(bottom, place, 1))
        edge = jnp.concatenate(
            [functools.reduce(jnp.add, before), functools.reduce(jnp.add, after)], axis=0
        )
        edge = jnp.concatenate([edge] + [jnp.zeros_like(edge)] * (kf // LANES - 1), axis=1)
        big, small = low_part(pltpu.roll(edge, x * SUB, 1))
        rows = pl.ds(pl.multiple_of(x * 2 * SUB, 2 * SUB), 2 * SUB)
        fringe[rows, :kf] = big
        fringe[rows, kf:] = small

    low_row = lax.broadcasted_iota(jnp.int32, (SUB, cols), 0) < STEPS

    def fill_fringe(lo, hi):
        for e in range(lo, hi, 2):
            pair = [
                jnp.where(low_row, yb[0, e + i].astype(F32), yb[1, e + i].astype(F32))
                for i in range(2)
            ]
            y_rows[e * SUB : (e + 2) * SUB, :] = jnp.concatenate(pair, axis=0).astype(BF16)

    def band_dot(x, blocks, field):
        rows = slice(x * LANES, (x + 1) * LANES)
        left = [band[rows, lo * LANES : hi * LANES] for lo, hi in blocks]
        return jnp.dot(
            left[0] if len(left) == 1 else jnp.concatenate(left, axis=1),
            field[0] if len(field) == 1 else jnp.concatenate(field, axis=0),
            preferred_element_type=F32,
        )

    def own_dot(x):
        blocks, field = [], []
        for reach, base in ((STEPS, STEPS), (1, 2 * STEPS + 2)):
            lo, hi = max(x - reach, 0), min(x + reach, cx - 1) + 1
            blocks.append((lo - x + base, hi - x + base))
            field.append(ub[lo:hi].reshape((hi - lo) * cy, cols))
        if blocks[0][1] == blocks[1][0]:
            blocks = [(blocks[0][0], blocks[1][1])]
        return band_dot(x, blocks, field)

    @pl.loop(0, cx // 4)
    def _(p):
        for i in range(4):
            build(4 * p + i)

    inner = range(STEPS, cx - STEPS)
    outer = list(range(STEPS)) + list(range(cx - STEPS, cx))
    edge_rows = 2 * SUB
    own.wait()
    for x in inner:
        value = own_dot(x)
        out[x] = value.astype(BF16)
        base = x * 2 * edge_rows
        cells[base : base + edge_rows, :] = value[:edge_rows]
        cells[base + edge_rows : base + 2 * edge_rows, :] = value[cy - edge_rows :]
    for j, x in enumerate(outer):
        acc[j * LANES : (j + 1) * LANES, :] = own_dot(x)

    for d in DIRS[:6]:
        wait_a(*d)
    fill_fringe(0, ex)
    y = y_rows[...]
    side = jnp.dot(fringe[:, :kf], y, preferred_element_type=F32)
    side = side + jnp.dot(fringe[:, kf:], y, preferred_element_type=F32)
    for x in inner:
        base = x * 2 * edge_rows
        top = cells[base : base + edge_rows, :]
        bottom = cells[base + edge_rows : base + 2 * edge_rows, :]
        a, b = (side[(2 * x + i) * SUB : (2 * x + i + 1) * SUB] for i in range(2))
        top = jnp.concatenate([top[:SUB] + a, top[SUB:]], axis=0)
        bottom = jnp.concatenate([bottom[:SUB], bottom[SUB:] + b], axis=0)
        out[x, :edge_rows] = top.astype(BF16)
        out[x, cy - edge_rows :] = bottom.astype(BF16)
    for j, x in enumerate(outer):
        a, b = (side[(2 * x + i) * SUB : (2 * x + i + 1) * SUB] for i in range(2))
        acc[j * LANES : j * LANES + SUB, :] += a
        acc[(j + 1) * LANES - SUB : (j + 1) * LANES, :] += b

    def product(lo, hi, part):
        return jnp.dot(
            wt[:, lo * LANES : hi * LANES],
            out[lo:hi, :, part].reshape((hi - lo) * cy, part.stop - part.start),
            preferred_element_type=F32,
        )

    middle = product(STEPS, cx - STEPS, slice(0, cols))

    def halo_dot(x, part):
        blocks, field = [], []
        for reach, base in ((STEPS, STEPS), (1, 2 * STEPS + 2)):
            if x < STEPS:
                lo, hi, source, shift = x - reach, 0, 0, STEPS
            else:
                lo, hi, source, shift = cx, x + reach + 1, 1, -cx
            if lo < hi:
                blocks.append((lo - x + base, hi - x + base))
                field.append(
                    xh[source, lo + shift : hi + shift, :, part].reshape((hi - lo) * cy, CHUNK)
                )
        return band_dot(x, blocks, field)

    for q in range(chunks):
        part = slice(q * CHUNK, (q + 1) * CHUNK)
        for d in DIRS[6:]:
            wait_a(*d, q)
        for j, x in enumerate(outer):
            value = acc[j * LANES : (j + 1) * LANES, part] + halo_dot(x, part)
            out[x, :, part] = value.astype(BF16)
        total = middle[:, part] + product(0, STEPS, part) + product(cx - STEPS, cx, part)
        for g in range(CHUNK // LANES):
            at_group = q * (CHUNK // LANES) + g
            ps[pl.ds(at_group, picks, stride=groups), :] = total[:, g * LANES : (g + 1) * LANES]

    def reduce_copy(k, tx, ty):
        return pltpu.make_async_remote_copy(
            src_ref=ps.at[pl.ds(pl.multiple_of((tx * ny + ty) * tile, tile), tile)],
            dst_ref=rbuf.at[k - 1], send_sem=r_send, recv_sem=r_recv,
            device_id=(tx, ty), device_id_type=MESH,
        )

    if others:
        pl.semaphore_wait(planes, len(others))

    for j in range(ny):
        @pl.loop(0 if j else 1, nx)
        def _(i, j=j):
            reduce_copy(i * ny + j, *ahead(i, j, 0, nx)).start()

    for dx, dy in DIRS:
        @pl.when(present(dx, dy))
        def _(dx=dx, dy=dy):
            k_copy(dx, dy).wait_send()
            for c in a_copies(dx, dy):
                c.wait_send()

    pltpu.make_async_copy(rbuf, rbuf, r_recv).wait()
    pltpu.make_async_copy(rbuf, rbuf, r_send).wait()

    total = ps[pl.ds(pl.multiple_of(me * tile, tile), tile), :]
    total = total + jnp.sum(rbuf[...], axis=0)
    for r in range(tile // groups):
        for q in range(groups):
            rep[r : r + 1, q * LANES : (q + 1) * LANES] = total[
                r * groups + q : r * groups + q + 1
            ]


def store_kernel(field, owned, field_out, owned_out, sems):
    parts = sems.shape[0] - 1
    rows = field.shape[0] // parts
    copies = [pltpu.make_async_copy(owned, owned_out, sems.at[parts])]
    for p in range(parts):
        part = pl.ds(p * rows, rows)
        copies.append(pltpu.make_async_copy(field.at[part], field_out.at[part], sems.at[p]))
    for c in copies:
        c.start()
    for c in copies:
        c.wait()


def solution(mesh):
    nx, ny = mesh.shape["gx"], mesh.shape["gy"]
    n = nx * ny

    def per_device(adjoint, conduct_x, conduct_y, pick_weights, owner_order):
        cx, cy, cols = adjoint.shape
        picks = pick_weights.shape[0]
        groups = cols // LANES
        chunks = cols // CHUNK
        ex = cx + 2 * STEPS
        tile = picks // n * groups
        kf = -(-ex * SUB // LANES) * LANES
        vmem = pl.BlockSpec(memory_space=pltpu.VMEM)
        hbm = pl.BlockSpec(memory_space=pl.ANY)
        dma = pltpu.SemaphoreType.DMA
        span = 2 * STEPS + 4
        field, owned = pl.pallas_call(
            functools.partial(kernel, nx, ny),
            out_shape=(
                pltpu.VMEM((cx, cy, cols), BF16),
                pltpu.VMEM((picks // n, cols), F32),
            ),
            in_specs=[hbm] * 4 + [vmem],
            out_specs=(vmem, vmem),
            scratch_shapes=[
                pltpu.VMEM((cx, cy, cols), BF16),
                pltpu.VMEM((2, STEPS, cy, cols), BF16),
                pltpu.VMEM((2, ex, SUB, cols), BF16),
                pltpu.VMEM((kf, cols), BF16),
                pltpu.VMEM((2, cx + 2 * SUB, 3 * LANES), F32),
                pltpu.VMEM((5 * len(NEAR), cx + 2 * SUB, LANES), F32),
                pltpu.VMEM((LANES * cx, LANES), F32),
                pltpu.VMEM((cx * cy, span * LANES), BF16),
                pltpu.VMEM((cx * 2 * SUB, 2 * kf), BF16),
                pltpu.VMEM((cx * 4 * SUB, cols), F32),
                pltpu.VMEM((2 * STEPS * cy, cols), F32),
                pltpu.VMEM((picks, cx, cy), BF16),
                pltpu.VMEM((picks * cx, LANES), F32),
                pltpu.VMEM((picks, cx * cy), BF16),
                pltpu.VMEM((picks * groups, LANES), F32),
                pltpu.VMEM((n - 1, tile, LANES), F32),
                dma,
                dma,
                dma((2,)),
                dma((len(DIRS), chunks)),
                dma((len(DIRS), chunks)),
                dma((len(DIRS),)),
                dma((len(DIRS),)),
                dma,
                dma,
                pltpu.SemaphoreType.REGULAR,
            ],
            compiler_params=pltpu.CompilerParams(
                collective_id=0, has_side_effects=True, vmem_limit_bytes=56 << 20
            ),
        )(adjoint, conduct_x, conduct_y, pick_weights, owner_order.reshape(1, picks))
        return pl.pallas_call(
            store_kernel,
            out_shape=(
                jax.ShapeDtypeStruct((cx, cy, cols), BF16),
                jax.ShapeDtypeStruct((picks // n, cols), F32),
            ),
            in_specs=[vmem, vmem],
            out_specs=(hbm, hbm),
            scratch_shapes=[dma((9,))],
        )(*[pltpu.with_memory_space_constraint(v, pltpu.VMEM) for v in (field, owned)])

    return jax.shard_map(
        per_device,
        mesh=mesh,
        in_specs=(P("gx", "gy", None), P("gx", "gy"), P("gx", "gy"), P(None, "gx", "gy"), P()),
        out_specs=(P("gx", "gy", None), P(("gx", "gy"), None)),
        check_vma=False,
    )
```

```python
import functools

import jax
import jax.numpy as jnp
from jax import lax
from jax.experimental import pallas as pl
from jax.experimental.pallas import tpu as pltpu
from jax.sharding import PartitionSpec as P

STEPS = 4
LANES = 128
SUB = 8
CHUNK = 256
PLANE = 4
MESH = pl.DeviceIdType.MESH
DIRS = ((0, 1), (0, -1), (1, 1), (1, -1), (-1, 1), (-1, -1), (1, 0), (-1, 0))
F32 = jnp.float32
BF16 = jnp.bfloat16
NEAR = [(a, b) for a in range(-2, 3) for b in range(-2, 3) if abs(a) + abs(b) <= 2]
FAR = [(a, b) for a in range(-4, 5) for b in range(-4, 5) if abs(a) + abs(b) <= 4]


def dir_id(dx, dy):
    return DIRS.index((dx, dy))


def centre(dx):
    return SUB if dx == -STEPS else 2 * SUB * (dx + STEPS - 1)


def turn(dx):
    return 2 * SUB if dx == -STEPS else centre(dx)


def turned(dx, get):
    by = turn(dx)
    return [get(LANES - by, LANES), get(0, LANES - by)] if by else [get(0, LANES)]


def kernel(
    nx, ny, adj, kx_hbm, ky_hbm, w_hbm, order_ref, out, rep,
    ub, xh, yb, y_rows, kk, shifted, coef, masks, ends, band, fringe, cells, acc,
    wv, w32, wt, ps, rbuf,
    own_sem, w_sem, k_load, a_send, a_recv, k_send, k_recv, r_send, r_recv, planes,
):
    cx, cy, cols = adj.shape
    groups = cols // LANES
    chunks = cols // CHUNK
    ex = cx + 2 * STEPS
    picks = w_hbm.shape[0]
    n = nx * ny
    tile = ps.shape[0] // n
    kf = y_rows.shape[0]
    span = 2 * STEPS + 4
    gx = lax.axis_index("gx")
    gy = lax.axis_index("gy")
    me = gx * ny + gy
    plane = nx if nx % PLANE else PLANE
    first = gx // plane * plane

    def ahead(i, j, lo, size):
        tx, ty = gx + i, gy + j
        tx = jnp.where(tx >= lo + size, tx - size, tx)
        return tx, jnp.where(ty >= ny, ty - ny, ty)

    def present(dx, dy):
        ok = None
        for d, g, size in ((dx, gx, nx), (dy, gy, ny)):
            if d == 1:
                c = g < size - 1
            elif d == -1:
                c = g > 0
            else:
                continue
            ok = c if ok is None else jnp.logical_and(ok, c)
        return ok

    barrier = pltpu.get_barrier_semaphore()

    def greet(semaphore, target):
        pl.semaphore_signal(semaphore, inc=1, device_id=target, device_id_type=MESH)

    for dx, dy in DIRS:
        if dx:
            @pl.when(present(dx, dy))
            def _(dx=dx, dy=dy):
                greet(barrier, (gx + dx, gy + dy))
    for i in range(plane):
        for j in range(ny):
            if i or j:
                greet(barrier, ahead(i, j, first, plane))
    others = range(plane, nx, plane)
    for i in others:
        greet(barrier, ahead(i, 0, 0, nx))

    own_rows, own_lanes = pl.ds(SUB, cx), pl.ds(LANES, LANES)
    k_loads = [
        pltpu.make_async_copy(src, kk.at[a, own_rows, own_lanes], k_load.at[a])
        for a, src in enumerate((kx_hbm, ky_hbm))
    ]
    own = pltpu.make_async_copy(adj, ub, own_sem)
    w_load = pltpu.make_async_copy(w_hbm, wv, w_sem)
    for c in k_loads + [w_load, own]:
        c.start()

    def k_region(sx, sy):
        rows = {-1: pl.ds(0, SUB), 0: own_rows, 1: pl.ds(SUB + cx, SUB)}[sx]
        return kk.at[:, rows, pl.ds(LANES * (1 + sy), LANES)]

    def a_region(sx, sy):
        if sy == 0:
            return xh.at[0 if sx == -1 else 1]
        rows = {-1: pl.ds(0, STEPS), 0: pl.ds(STEPS, cx), 1: pl.ds(STEPS + cx, STEPS)}[sx]
        return yb.at[0 if sy == 1 else 1, rows]

    def k_copy(dx, dy):
        rows = {1: pl.ds(cx, SUB), 0: own_rows, -1: pl.ds(SUB, SUB)}[dx]
        return pltpu.make_async_remote_copy(
            src_ref=kk.at[:, rows, own_lanes], dst_ref=k_region(-dx, -dy),
            send_sem=k_send.at[dir_id(dx, dy)], recv_sem=k_recv.at[dir_id(-dx, -dy)],
            device_id=(gx + dx, gy + dy), device_id_type=MESH,
        )

    def a_copies(dx, dy):
        slot, mine = dir_id(-dx, -dy), dir_id(dx, dy)
        src = adj
        if dx:
            src = src.at[pl.ds(cx - STEPS if dx == 1 else 0, STEPS)]
        if dy:
            src = src.at[:, pl.ds(cy - SUB if dy == 1 else 0, SUB)]
        dst = a_region(-dx, -dy)
        parts = [(src, dst)]
        if dy == 0:
            cut = [pl.ds(q * CHUNK, CHUNK) for q in range(chunks)]
            parts = [(src.at[:, :, c], dst.at[:, :, c]) for c in cut]
        return [
            pltpu.make_async_remote_copy(
                src_ref=s, dst_ref=d, send_sem=a_send.at[mine, q],
                recv_sem=a_recv.at[slot, q], device_id=(gx + dx, gy + dy),
                device_id_type=MESH,
            )
            for q, (s, d) in enumerate(parts)
        ]

    for dx, dy in DIRS:
        @pl.when(jnp.logical_not(present(dx, dy)))
        def _(dx=dx, dy=dy):
            k_part, a_part = k_region(dx, dy), a_region(dx, dy)
            k_part[...] = jnp.zeros(k_part.shape, F32)
            a_part[...] = jnp.zeros(a_part.shape, BF16)

    for c in k_loads:
        c.wait()
    count = plane * ny - 1 + len(others)
    for dx, dy in DIRS:
        if dx:
            count = count + jnp.where(present(dx, dy), 1, 0)
    pl.semaphore_wait(barrier, count)

    for dx, dy in DIRS:
        @pl.when(present(dx, dy))
        def _(dx=dx, dy=dy):
            k_copy(dx, dy).start()

    for dx, dy in DIRS[:6]:
        @pl.when(present(dx, dy))
        def _(dx=dx, dy=dy):
            for c in a_copies(dx, dy):
                c.start()

    for q in range(chunks):
        for dx, dy in DIRS[6:]:
            @pl.when(present(dx, dy))
            def _(dx=dx, dy=dy, q=q):
                a_copies(dx, dy)[q].start()

    for i in others:
        greet(planes, ahead(i, 0, 0, nx))

    def wait_k(dx, dy):
        @pl.when(present(dx, dy))
        def _():
            part = k_region(dx, dy)
            pltpu.make_async_copy(part, part, k_recv.at[dir_id(dx, dy)]).wait()

    def wait_a(dx, dy, q=0):
        @pl.when(present(dx, dy))
        def _():
            part = a_region(dx, dy)
            if dy == 0:
                part = part.at[:, :, pl.ds(q * CHUNK, CHUNK)]
            pltpu.make_async_copy(part, part, a_recv.at[dir_id(dx, dy), q]).wait()

    w_load.wait()
    pick_ids = lax.broadcasted_iota(jnp.int32, (picks, picks), 0)
    chosen = jnp.where(pick_ids == order_ref[...], F32(1), F32(0)).astype(BF16)
    w32[...] = wv[...].astype(F32).reshape(picks * cx, LANES)
    for x in range(cx):
        row = w32[pl.ds(x, picks, stride=cx), :].astype(BF16)
        row = lax.dot_general(
            chosen, row, (((0,), (0,)), ((), ())), preferred_element_type=F32
        )
        wt[:, x * LANES : (x + 1) * LANES] = row.astype(BF16)

    coef[...] = jnp.zeros(coef.shape, F32)
    if kf > ex * 2 * SUB:
        y_rows[ex * 2 * SUB :, :] = jnp.zeros((kf - ex * 2 * SUB, cols), BF16)
    lane = lax.broadcasted_iota(jnp.int32, (LANES, LANES), 1)
    cell = lax.broadcasted_iota(jnp.int32, (LANES, LANES), 0)
    for dx in range(-STEPS, STEPS + 1):
        gap = ((lane - turn(dx)) & (LANES - 1)) - cell
        inside = jnp.abs(gap) <= STEPS - abs(dx)
        masks[dx + STEPS] = jnp.where(inside, F32(1), F32(0)).astype(BF16)
    lane, cell = lane[:SUB], cell[:SUB]
    before = after = jnp.zeros((SUB, LANES), F32)
    for dx in range(1 - STEPS, STEPS):
        reach = STEPS - abs(dx)
        place = ((lane - centre(dx) + LANES // 2) & (LANES - 1)) - LANES // 2
        left = (place < 0) & (place >= -STEPS) & (cell - place <= reach)
        right = (place >= 0) & (place < STEPS) & (place + SUB - cell <= reach)
        before = jnp.where(left, F32(1), before)
        after = jnp.where(right, F32(1), after)
    ends[:SUB], ends[SUB:] = before, after

    for d in DIRS:
        wait_k(*d)

    kx, ky = kk[0], kk[1]
    kx_at = lax.broadcasted_iota(jnp.int32, kx.shape, 0)
    ky_at = lax.broadcasted_iota(jnp.int32, ky.shape, 1)
    kx = jnp.where(jnp.logical_and(kx_at == SUB + cx - 1, gx == nx - 1), F32(0), kx)
    ky = jnp.where(jnp.logical_and(ky_at == 2 * LANES - 1, gy == ny - 1), F32(0), ky)
    high, wide = kx.shape

    def at(value, dx, dy):
        if dx:
            value = pltpu.roll(value, -dx % high, 0)
        if dy:
            value = pltpu.roll(value, -dy % wide, 1)
        return value

    xp, yp = kx, ky
    xm, ym = at(kx, -1, 0), at(ky, 0, -1)
    c = F32(1) - ((xm + xp) + (ym + yp))
    two = {
        (0, 0): c * c + ((xm * xm + xp * xp) + (ym * ym + yp * yp)),
        (1, 0): xp * (c + at(c, 1, 0)),
        (-1, 0): xm * (c + at(c, -1, 0)),
        (0, 1): yp * (c + at(c, 0, 1)),
        (0, -1): ym * (c + at(c, 0, -1)),
        (2, 0): xp * at(xp, 1, 0),
        (-2, 0): xm * at(xm, -1, 0),
        (0, 2): yp * at(yp, 0, 1),
        (0, -2): ym * at(ym, 0, -1),
        (1, 1): xp * at(yp, 1, 0) + yp * at(xp, 0, 1),
        (1, -1): xp * at(ym, 1, 0) + ym * at(xp, 0, -1),
        (-1, 1): xm * at(yp, -1, 0) + yp * at(xm, 0, 1),
        (-1, -1): xm * at(ym, -1, 0) + ym * at(xm, 0, -1),
    }
    for i, d in enumerate(NEAR):
        for dy in range(-2, 3):
            shifted[(dy + 2) * len(NEAR) + i] = at(two[d], 0, dy)[:, LANES : 2 * LANES]

    def near(d, dx, dy):
        return shifted[(dy + 2) * len(NEAR) + NEAR.index(d), SUB + dx : SUB + dx + cx]

    for fx, fy in FAR:
        total = None
        for dx, dy in NEAR:
            rest = (fx - dx, fy - dy)
            if rest in NEAR:
                term = near((dx, dy), 0, 0) * near(rest, dx, dy)
                total = term if total is None else total + term
        slot = (centre(fx) + fy) % LANES
        coef[slot * cx : (slot + 1) * cx, :] = total

    def low_part(value):
        high_part = value.astype(BF16)
        return high_part, (value - high_part.astype(F32)).astype(BF16)

    def build(x):
        table = pltpu.roll(
            coef[pl.ds(x, LANES, stride=cx), :].T, 0, 1, stride=1, stride_axis=0
        )
        rows = pl.ds(pl.multiple_of(x * LANES, LANES), LANES)
        big, small = low_part(table)
        for dx in range(-STEPS, STEPS + 1):
            r = dx + STEPS
            source = big
            if dx == -STEPS:
                source = pltpu.roll(table, SUB, 1).astype(BF16)
            band[rows, r * LANES : (r + 1) * LANES] = source * masks[r]
            if abs(dx) <= 1:
                k = 2 * STEPS + 2 + dx
                band[rows, k * LANES : (k + 1) * LANES] = small * masks[r]
        edge = jnp.concatenate([table[:SUB], table[cy - SUB :]], axis=0) * ends[...]
        edge = pltpu.roll(edge, SUB, 1)
        edge = jnp.concatenate([edge] + [jnp.zeros_like(edge)] * (kf // LANES - 1), axis=1)
        big, small = low_part(pltpu.roll(edge, (x + 1) * 2 * SUB, 1))
        rows = pl.ds(pl.multiple_of(x * 2 * SUB, 2 * SUB), 2 * SUB)
        fringe[rows, :kf] = big
        fringe[rows, kf:] = small

    def fill_fringe():
        for e in range(ex):
            pair = jnp.concatenate([yb[1, e].astype(F32), yb[0, e].astype(F32)], axis=0)
            y_rows[e * 2 * SUB : (e + 1) * 2 * SUB, :] = pair.astype(BF16)

    def band_dot(x, blocks, field):
        rows = slice(x * LANES, (x + 1) * LANES)
        left = [band[rows, lo * LANES : hi * LANES] for lo, hi in blocks]
        return jnp.dot(
            left[0] if len(left) == 1 else jnp.concatenate(left, axis=1),
            field[0] if len(field) == 1 else jnp.concatenate(field, axis=0),
            preferred_element_type=F32,
        )

    def own_dot(x):
        blocks, field = [], []
        for reach, base in ((STEPS, STEPS), (1, 2 * STEPS + 2)):
            lo, hi = max(x - reach, 0), min(x + reach, cx - 1) + 1
            blocks.append((lo - x + base, hi - x + base))
            for r in range(lo, hi):
                field += turned(r - x, lambda a, b, r=r: ub[r, a:b])
        if blocks[0][1] == blocks[1][0]:
            blocks = [(blocks[0][0], blocks[1][1])]
        return band_dot(x, blocks, field)

    @pl.loop(0, cx // 4)
    def _(p):
        for i in range(4):
            build(4 * p + i)

    inner = range(STEPS, cx - STEPS)
    outer = list(range(STEPS)) + list(range(cx - STEPS, cx))
    edge_rows = 2 * SUB
    own.wait()
    for x in inner:
        value = own_dot(x)
        out[x] = value.astype(BF16)
        base = x * 2 * edge_rows
        cells[base : base + edge_rows, :] = value[:edge_rows]
        cells[base + edge_rows : base + 2 * edge_rows, :] = value[cy - edge_rows :]
    for j, x in enumerate(outer):
        acc[j * LANES : (j + 1) * LANES, :] = own_dot(x)

    for d in DIRS[:6]:
        wait_a(*d)
    fill_fringe()
    y = y_rows[...]
    side = jnp.dot(fringe[:, :kf], y, preferred_element_type=F32)
    side = side + jnp.dot(fringe[:, kf:], y, preferred_element_type=F32)
    for x in inner:
        base = x * 2 * edge_rows
        top = cells[base : base + edge_rows, :]
        bottom = cells[base + edge_rows : base + 2 * edge_rows, :]
        a, b = (side[(2 * x + i) * SUB : (2 * x + i + 1) * SUB] for i in range(2))
        top = jnp.concatenate([top[:SUB] + a, top[SUB:]], axis=0)
        bottom = jnp.concatenate([bottom[:SUB], bottom[SUB:] + b], axis=0)
        out[x, :edge_rows] = top.astype(BF16)
        out[x, cy - edge_rows :] = bottom.astype(BF16)
    for j, x in enumerate(outer):
        a, b = (side[(2 * x + i) * SUB : (2 * x + i + 1) * SUB] for i in range(2))
        acc[j * LANES : j * LANES + SUB, :] += a
        acc[(j + 1) * LANES - SUB : (j + 1) * LANES, :] += b

    def product(lo, hi, part):
        return jnp.dot(
            wt[:, lo * LANES : hi * LANES],
            out[lo:hi, :, part].reshape((hi - lo) * cy, part.stop - part.start),
            preferred_element_type=F32,
        )

    middle = product(STEPS, cx - STEPS, slice(0, cols))

    def halo_dot(x, part):
        blocks, field = [], []
        for reach, base in ((STEPS, STEPS), (1, 2 * STEPS + 2)):
            if x < STEPS:
                lo, hi, source, shift = x - reach, 0, 0, STEPS
            else:
                lo, hi, source, shift = cx, x + reach + 1, 1, -cx
            if lo < hi:
                blocks.append((lo - x + base, hi - x + base))
                for r in range(lo, hi):
                    field += turned(
                        r - x, lambda a, b, r=r: xh[source, r + shift, a:b, part]
                    )
        return band_dot(x, blocks, field)

    for q in range(chunks):
        part = slice(q * CHUNK, (q + 1) * CHUNK)
        for d in DIRS[6:]:
            wait_a(*d, q)
        for j, x in enumerate(outer):
            value = acc[j * LANES : (j + 1) * LANES, part] + halo_dot(x, part)
            out[x, :, part] = value.astype(BF16)
        total = middle[:, part] + product(0, STEPS, part) + product(cx - STEPS, cx, part)
        for g in range(CHUNK // LANES):
            at_group = q * (CHUNK // LANES) + g
            ps[pl.ds(at_group, picks, stride=groups), :] = total[:, g * LANES : (g + 1) * LANES]

    def reduce_copy(k, tx, ty):
        return pltpu.make_async_remote_copy(
            src_ref=ps.at[pl.ds(pl.multiple_of((tx * ny + ty) * tile, tile), tile)],
            dst_ref=rbuf.at[k - 1], send_sem=r_send, recv_sem=r_recv,
            device_id=(tx, ty), device_id_type=MESH,
        )

    if others:
        pl.semaphore_wait(planes, len(others))

    for j in range(ny):
        @pl.loop(0 if j else 1, nx)
        def _(i, j=j):
            reduce_copy(i * ny + j, *ahead(i, j, 0, nx)).start()

    for dx, dy in DIRS:
        @pl.when(present(dx, dy))
        def _(dx=dx, dy=dy):
            k_copy(dx, dy).wait_send()
            for c in a_copies(dx, dy):
                c.wait_send()

    pltpu.make_async_copy(rbuf, rbuf, r_recv).wait()
    pltpu.make_async_copy(rbuf, rbuf, r_send).wait()

    total = ps[pl.ds(pl.multiple_of(me * tile, tile), tile), :]
    total = total + jnp.sum(rbuf[...], axis=0)
    for r in range(tile // groups):
        for q in range(groups):
            rep[r : r + 1, q * LANES : (q + 1) * LANES] = total[
                r * groups + q : r * groups + q + 1
            ]


def store_kernel(field, owned, field_out, owned_out, sems):
    parts = sems.shape[0] - 1
    rows = field.shape[0] // parts
    copies = [pltpu.make_async_copy(owned, owned_out, sems.at[parts])]
    for p in range(parts):
        part = pl.ds(p * rows, rows)
        copies.append(pltpu.make_async_copy(field.at[part], field_out.at[part], sems.at[p]))
    for c in copies:
        c.start()
    for c in copies:
        c.wait()


def solution(mesh):
    nx, ny = mesh.shape["gx"], mesh.shape["gy"]
    n = nx * ny

    def per_device(adjoint, conduct_x, conduct_y, pick_weights, owner_order):
        cx, cy, cols = adjoint.shape
        picks = pick_weights.shape[0]
        groups = cols // LANES
        chunks = cols // CHUNK
        ex = cx + 2 * STEPS
        tile = picks // n * groups
        kf = -(-ex * 2 * SUB // LANES) * LANES
        vmem = pl.BlockSpec(memory_space=pltpu.VMEM)
        hbm = pl.BlockSpec(memory_space=pl.ANY)
        dma = pltpu.SemaphoreType.DMA
        span = 2 * STEPS + 4
        field, owned = pl.pallas_call(
            functools.partial(kernel, nx, ny),
            out_shape=(
                pltpu.VMEM((cx, cy, cols), BF16),
                pltpu.VMEM((picks // n, cols), F32),
            ),
            in_specs=[hbm] * 4 + [vmem],
            out_specs=(vmem, vmem),
            scratch_shapes=[
                pltpu.VMEM((cx, cy, cols), BF16),
                pltpu.VMEM((2, STEPS, cy, cols), BF16),
                pltpu.VMEM((2, ex, SUB, cols), BF16),
                pltpu.VMEM((kf, cols), BF16),
                pltpu.VMEM((2, cx + 2 * SUB, 3 * LANES), F32),
                pltpu.VMEM((5 * len(NEAR), cx + 2 * SUB, LANES), F32),
                pltpu.VMEM((LANES * cx, LANES), F32),
                pltpu.VMEM((2 * STEPS + 1, LANES, LANES), BF16),
                pltpu.VMEM((2 * SUB, LANES), F32),
                pltpu.VMEM((cx * cy, span * LANES), BF16),
                pltpu.VMEM((cx * 2 * SUB, 2 * kf), BF16),
                pltpu.VMEM((cx * 4 * SUB, cols), F32),
                pltpu.VMEM((2 * STEPS * cy, cols), F32),
                pltpu.VMEM((picks, cx, cy), BF16),
                pltpu.VMEM((picks * cx, LANES), F32),
                pltpu.VMEM((picks, cx * cy), BF16),
                pltpu.VMEM((picks * groups, LANES), F32),
                pltpu.VMEM((n - 1, tile, LANES), F32),
                dma,
                dma,
                dma((2,)),
                dma((len(DIRS), chunks)),
                dma((len(DIRS), chunks)),
                dma((len(DIRS),)),
                dma((len(DIRS),)),
                dma,
                dma,
                pltpu.SemaphoreType.REGULAR,
            ],
            compiler_params=pltpu.CompilerParams(
                collective_id=0, has_side_effects=True, vmem_limit_bytes=56 << 20
            ),
        )(adjoint, conduct_x, conduct_y, pick_weights, owner_order.reshape(1, picks))
        return pl.pallas_call(
            store_kernel,
            out_shape=(
                jax.ShapeDtypeStruct((cx, cy, cols), BF16),
                jax.ShapeDtypeStruct((picks // n, cols), F32),
            ),
            in_specs=[vmem, vmem],
            out_specs=(hbm, hbm),
            scratch_shapes=[dma((9,))],
        )(*[pltpu.with_memory_space_constraint(v, pltpu.VMEM) for v in (field, owned)])

    return jax.shard_map(
        per_device,
        mesh=mesh,
        in_specs=(P("gx", "gy", None), P("gx", "gy"), P("gx", "gy"), P(None, "gx", "gy"), P()),
        out_specs=(P("gx", "gy", None), P(("gx", "gy"), None)),
        check_vma=False,
    )
```

```python
import functools

import jax
import jax.numpy as jnp
from jax import lax
from jax.experimental import pallas as pl
from jax.experimental.pallas import tpu as pltpu
from jax.sharding import PartitionSpec as P

STEPS = 4
LANES = 128
SUB = 8
CHUNK = 256
MESH = pl.DeviceIdType.MESH
DIRS = ((0, 1), (0, -1), (1, 1), (1, -1), (-1, 1), (-1, -1), (1, 0), (-1, 0))
F32 = jnp.float32
BF16 = jnp.bfloat16
NEAR = [(a, b) for a in range(-2, 3) for b in range(-2, 3) if abs(a) + abs(b) <= 2]
FAR = [(a, b) for a in range(-4, 5) for b in range(-4, 5) if abs(a) + abs(b) <= 4]


def dir_id(dx, dy):
    return DIRS.index((dx, dy))


def centre(dx):
    return SUB if dx == -STEPS else 2 * SUB * (dx + STEPS - 1)


def turn(dx):
    return 2 * SUB if dx == -STEPS else centre(dx)


def turned(dx, get):
    by = turn(dx)
    return [get(LANES - by, LANES), get(0, LANES - by)] if by else [get(0, LANES)]


def far_rounds(nx, ny):
    result = []
    for size, axis in ((nx, 0), (ny, 1)):
        reach = 1
        while reach < size - 1:
            result.append([(d, 0) if axis == 0 else (0, d) for d in (reach, -reach)])
            reach *= 2
    return result


def kernel(
    nx, ny, adj, kx_hbm, ky_hbm, w_hbm, order_ref, out, rep,
    ub, xh, yb, y_rows, kk, shifted, coef, masks, ends, band, fringe, cells, acc,
    wv, w32, wt, w_halo, ps, rbuf,
    own_sem, w_sem, k_load, a_send, a_recv, k_send, k_recv, w_send, w_recv, r_send, r_recv, known,
):
    cx, cy, cols = adj.shape
    groups = cols // LANES
    chunks = cols // CHUNK
    ex = cx + 2 * STEPS
    picks = w_hbm.shape[0]
    n = nx * ny
    tile = ps.shape[0] // n
    kf = y_rows.shape[0]
    span = 2 * STEPS + 4
    gx = lax.axis_index("gx")
    gy = lax.axis_index("gy")
    me = gx * ny + gy

    def around(i, j):
        tx, ty = gx + i, gy + j
        return jnp.where(tx >= nx, tx - nx, tx), jnp.where(ty >= ny, ty - ny, ty)

    def present(dx, dy):
        ok = None
        for d, g, size in ((dx, gx, nx), (dy, gy, ny)):
            if d == 0:
                continue
            c = g < size - d if d > 0 else g >= -d
            ok = c if ok is None else jnp.logical_and(ok, c)
        return ok

    barrier = pltpu.get_barrier_semaphore()
    rounds = far_rounds(nx, ny)

    def greet(semaphore, dx, dy):
        @pl.when(present(dx, dy))
        def _():
            pl.semaphore_signal(
                semaphore, inc=1, device_id=(gx + dx, gy + dy), device_id_type=MESH
            )

    def number(peers):
        return functools.reduce(jnp.add, [jnp.where(present(*d), 1, 0) for d in peers])

    for d in DIRS:
        greet(barrier, *d)

    def hear(i):
        pl.semaphore_wait(known.at[i], number(rounds[i]))

    def tell(i):
        for d in rounds[i]:
            greet(known.at[i], *d)

    own_rows, own_lanes = pl.ds(SUB, cx), pl.ds(LANES, LANES)
    k_loads = [
        pltpu.make_async_copy(src, kk.at[a, own_rows, own_lanes], k_load.at[a])
        for a, src in enumerate((kx_hbm, ky_hbm))
    ]
    own = pltpu.make_async_copy(adj, ub, own_sem)
    w_load = pltpu.make_async_copy(w_hbm, wv, w_sem)
    for c in k_loads + [w_load, own]:
        c.start()

    def k_region(sx, sy):
        rows = {-1: pl.ds(0, SUB), 0: own_rows, 1: pl.ds(SUB + cx, SUB)}[sx]
        return kk.at[:, rows, pl.ds(LANES * (1 + sy), LANES)]

    def a_region(sx, sy):
        if sy == 0:
            return xh.at[0 if sx == -1 else 1]
        rows = {-1: pl.ds(0, STEPS), 0: pl.ds(STEPS, cx), 1: pl.ds(STEPS + cx, STEPS)}[sx]
        return yb.at[0 if sy == 1 else 1, rows]

    def k_copy(dx, dy):
        rows = {1: pl.ds(cx, SUB), 0: own_rows, -1: pl.ds(SUB, SUB)}[dx]
        return pltpu.make_async_remote_copy(
            src_ref=kk.at[:, rows, own_lanes], dst_ref=k_region(-dx, -dy),
            send_sem=k_send.at[dir_id(dx, dy)], recv_sem=k_recv.at[dir_id(-dx, -dy)],
            device_id=(gx + dx, gy + dy), device_id_type=MESH,
        )

    def a_copies(dx, dy):
        slot, mine = dir_id(-dx, -dy), dir_id(dx, dy)
        src = adj
        if dx:
            src = src.at[pl.ds(cx - STEPS if dx == 1 else 0, STEPS)]
        if dy:
            src = src.at[:, pl.ds(cy - SUB if dy == 1 else 0, SUB)]
        dst = a_region(-dx, -dy)
        parts = [(src, dst)]
        if dy == 0:
            cut = [pl.ds(q * CHUNK, CHUNK) for q in range(chunks)]
            parts = [(src.at[:, :, c], dst.at[:, :, c]) for c in cut]
        return [
            pltpu.make_async_remote_copy(
                src_ref=s, dst_ref=d, send_sem=a_send.at[mine, q],
                recv_sem=a_recv.at[slot, q], device_id=(gx + dx, gy + dy),
                device_id_type=MESH,
            )
            for q, (s, d) in enumerate(parts)
        ]

    for dx, dy in DIRS:
        @pl.when(jnp.logical_not(present(dx, dy)))
        def _(dx=dx, dy=dy):
            k_part, a_part = k_region(dx, dy), a_region(dx, dy)
            k_part[...] = jnp.zeros(k_part.shape, F32)
            a_part[...] = jnp.zeros(a_part.shape, BF16)

    for c in k_loads:
        c.wait()
    pl.semaphore_wait(barrier, number(DIRS))

    for dx, dy in DIRS:
        @pl.when(present(dx, dy))
        def _(dx=dx, dy=dy):
            k_copy(dx, dy).start()

    for dx, dy in DIRS[:6]:
        @pl.when(present(dx, dy))
        def _(dx=dx, dy=dy):
            for c in a_copies(dx, dy):
                c.start()

    told = [0]

    def next_round():
        i = told[0]
        hear(i)
        if i + 1 < len(rounds):
            tell(i + 1)
        told[0] = i + 1

    tell(0)

    def wait_k(dx, dy):
        @pl.when(present(dx, dy))
        def _():
            part = k_region(dx, dy)
            pltpu.make_async_copy(part, part, k_recv.at[dir_id(dx, dy)]).wait()

    def wait_a(dx, dy, q=0):
        @pl.when(present(dx, dy))
        def _():
            part = a_region(dx, dy)
            if dy == 0:
                part = part.at[:, :, pl.ds(q * CHUNK, CHUNK)]
            pltpu.make_async_copy(part, part, a_recv.at[dir_id(dx, dy), q]).wait()

    def w_copy(dx):
        lo = (cx - STEPS) * LANES if dx == 1 else 0
        slot, mine = (0, 1) if dx == 1 else (1, 0)
        return pltpu.make_async_remote_copy(
            src_ref=wt.at[:, pl.ds(lo, STEPS * LANES)], dst_ref=w_halo.at[slot],
            send_sem=w_send.at[mine], recv_sem=w_recv.at[slot],
            device_id=(gx + dx, gy), device_id_type=MESH,
        )

    w_load.wait()
    pick_ids = lax.broadcasted_iota(jnp.int32, (picks, picks), 0)
    chosen = jnp.where(pick_ids == order_ref[...], F32(1), F32(0)).astype(BF16)
    w32[...] = wv[...].astype(F32).reshape(picks * cx, LANES)
    for x in range(cx):
        row = w32[pl.ds(x, picks, stride=cx), :].astype(BF16)
        row = lax.dot_general(
            chosen, row, (((0,), (0,)), ((), ())), preferred_element_type=F32
        )
        wt[:, x * LANES : (x + 1) * LANES] = row.astype(BF16)

    for dx in (1, -1):
        @pl.when(present(dx, 0))
        def _(dx=dx):
            w_copy(dx).start()

        @pl.when(jnp.logical_not(present(dx, 0)))
        def _(dx=dx):
            part = w_halo.at[1 if dx == 1 else 0]
            part[...] = jnp.zeros(part.shape, BF16)

    for q in range(chunks):
        for dx, dy in DIRS[6:]:
            @pl.when(present(dx, dy))
            def _(dx=dx, dy=dy, q=q):
                a_copies(dx, dy)[q].start()

    coef[...] = jnp.zeros(coef.shape, F32)
    if kf > ex * 2 * SUB:
        y_rows[ex * 2 * SUB :, :] = jnp.zeros((kf - ex * 2 * SUB, cols), BF16)
    lane = lax.broadcasted_iota(jnp.int32, (LANES, LANES), 1)
    cell = lax.broadcasted_iota(jnp.int32, (LANES, LANES), 0)
    for dx in range(-STEPS, STEPS + 1):
        gap = ((lane - turn(dx)) & (LANES - 1)) - cell
        inside = jnp.abs(gap) <= STEPS - abs(dx)
        masks[dx + STEPS] = jnp.where(inside, F32(1), F32(0)).astype(BF16)
    lane, cell = lane[:SUB], cell[:SUB]
    before = after = jnp.zeros((SUB, LANES), F32)
    for dx in range(1 - STEPS, STEPS):
        reach = STEPS - abs(dx)
        place = ((lane - centre(dx) + LANES // 2) & (LANES - 1)) - LANES // 2
        left = (place < 0) & (place >= -STEPS) & (cell - place <= reach)
        right = (place >= 0) & (place < STEPS) & (place + SUB - cell <= reach)
        before = jnp.where(left, F32(1), before)
        after = jnp.where(right, F32(1), after)
    ends[:SUB], ends[SUB:] = before, after

    for d in DIRS:
        wait_k(*d)
    next_round()

    kx, ky = kk[0], kk[1]
    kx_at = lax.broadcasted_iota(jnp.int32, kx.shape, 0)
    ky_at = lax.broadcasted_iota(jnp.int32, ky.shape, 1)
    kx = jnp.where(jnp.logical_and(kx_at == SUB + cx - 1, gx == nx - 1), F32(0), kx)
    ky = jnp.where(jnp.logical_and(ky_at == 2 * LANES - 1, gy == ny - 1), F32(0), ky)
    high, wide = kx.shape

    def at(value, dx, dy):
        if dx:
            value = pltpu.roll(value, -dx % high, 0)
        if dy:
            value = pltpu.roll(value, -dy % wide, 1)
        return value

    xp, yp = kx, ky
    xm, ym = at(kx, -1, 0), at(ky, 0, -1)
    c = F32(1) - ((xm + xp) + (ym + yp))
    two = {
        (0, 0): c * c + ((xm * xm + xp * xp) + (ym * ym + yp * yp)),
        (1, 0): xp * (c + at(c, 1, 0)),
        (-1, 0): xm * (c + at(c, -1, 0)),
        (0, 1): yp * (c + at(c, 0, 1)),
        (0, -1): ym * (c + at(c, 0, -1)),
        (2, 0): xp * at(xp, 1, 0),
        (-2, 0): xm * at(xm, -1, 0),
        (0, 2): yp * at(yp, 0, 1),
        (0, -2): ym * at(ym, 0, -1),
        (1, 1): xp * at(yp, 1, 0) + yp * at(xp, 0, 1),
        (1, -1): xp * at(ym, 1, 0) + ym * at(xp, 0, -1),
        (-1, 1): xm * at(yp, -1, 0) + yp * at(xm, 0, 1),
        (-1, -1): xm * at(ym, -1, 0) + ym * at(xm, 0, -1),
    }
    for i, d in enumerate(NEAR):
        for dy in range(-2, 3):
            shifted[(dy + 2) * len(NEAR) + i] = at(two[d], 0, dy)[:, LANES : 2 * LANES]

    def near(d, dx, dy):
        return shifted[(dy + 2) * len(NEAR) + NEAR.index(d), SUB + dx : SUB + dx + cx]

    for fx, fy in FAR:
        total = None
        for dx, dy in NEAR:
            rest = (fx - dx, fy - dy)
            if rest in NEAR:
                term = near((dx, dy), 0, 0) * near(rest, dx, dy)
                total = term if total is None else total + term
        slot = (centre(fx) + fy) % LANES
        coef[slot * cx : (slot + 1) * cx, :] = total

    def low_part(value):
        high_part = value.astype(BF16)
        return high_part, (value - high_part.astype(F32)).astype(BF16)

    def build(x):
        table = pltpu.roll(
            coef[pl.ds(x, LANES, stride=cx), :].T, 0, 1, stride=1, stride_axis=0
        )
        rows = pl.ds(pl.multiple_of(x * LANES, LANES), LANES)
        big, small = low_part(table)
        for dx in range(-STEPS, STEPS + 1):
            r = dx + STEPS
            source = big
            if dx == -STEPS:
                source = pltpu.roll(table, SUB, 1).astype(BF16)
            band[rows, r * LANES : (r + 1) * LANES] = source * masks[r]
            if abs(dx) <= 1:
                k = 2 * STEPS + 2 + dx
                band[rows, k * LANES : (k + 1) * LANES] = small * masks[r]
        edge = jnp.concatenate([table[:SUB], table[cy - SUB :]], axis=0) * ends[...]
        edge = pltpu.roll(edge, SUB, 1)
        edge = jnp.concatenate([edge] + [jnp.zeros_like(edge)] * (kf // LANES - 1), axis=1)
        big, small = low_part(pltpu.roll(edge, (x + 1) * 2 * SUB, 1))
        rows = pl.ds(pl.multiple_of(x * 2 * SUB, 2 * SUB), 2 * SUB)
        fringe[rows, :kf] = big
        fringe[rows, kf:] = small

    def fill_fringe():
        for e in range(ex):
            pair = jnp.concatenate([yb[1, e].astype(F32), yb[0, e].astype(F32)], axis=0)
            y_rows[e * 2 * SUB : (e + 1) * 2 * SUB, :] = pair.astype(BF16)

    def band_dot(x, blocks, field):
        rows = slice(x * LANES, (x + 1) * LANES)
        left = [band[rows, lo * LANES : hi * LANES] for lo, hi in blocks]
        return jnp.dot(
            left[0] if len(left) == 1 else jnp.concatenate(left, axis=1),
            field[0] if len(field) == 1 else jnp.concatenate(field, axis=0),
            preferred_element_type=F32,
        )

    def own_dot(x):
        blocks, field = [], []
        for reach, base in ((STEPS, STEPS), (1, 2 * STEPS + 2)):
            lo, hi = max(x - reach, 0), min(x + reach, cx - 1) + 1
            blocks.append((lo - x + base, hi - x + base))
            for r in range(lo, hi):
                field += turned(r - x, lambda a, b, r=r: ub[r, a:b])
        if blocks[0][1] == blocks[1][0]:
            blocks = [(blocks[0][0], blocks[1][1])]
        return band_dot(x, blocks, field)

    @pl.loop(0, cx // 4)
    def _(p):
        for i in range(4):
            build(4 * p + i)

    inner = range(STEPS, cx - STEPS)
    outer = list(range(STEPS)) + list(range(cx - STEPS, cx))
    edge_rows = 2 * SUB
    own.wait()
    next_round()
    for x in inner:
        value = own_dot(x)
        out[x] = value.astype(BF16)
        base = x * 2 * edge_rows
        cells[base : base + edge_rows, :] = value[:edge_rows]
        cells[base + edge_rows : base + 2 * edge_rows, :] = value[cy - edge_rows :]
    for j, x in enumerate(outer):
        acc[j * LANES : (j + 1) * LANES, :] = own_dot(x)

    for d in DIRS[:6]:
        wait_a(*d)
    next_round()
    fill_fringe()
    y = y_rows[...]
    side = jnp.dot(fringe[:, :kf], y, preferred_element_type=F32)
    side = side + jnp.dot(fringe[:, kf:], y, preferred_element_type=F32)
    for x in inner:
        base = x * 2 * edge_rows
        top = cells[base : base + edge_rows, :]
        bottom = cells[base + edge_rows : base + 2 * edge_rows, :]
        a, b = (side[(2 * x + i) * SUB : (2 * x + i + 1) * SUB] for i in range(2))
        top = jnp.concatenate([top[:SUB] + a, top[SUB:]], axis=0)
        bottom = jnp.concatenate([bottom[:SUB], bottom[SUB:] + b], axis=0)
        out[x, :edge_rows] = top.astype(BF16)
        out[x, cy - edge_rows :] = bottom.astype(BF16)
    for j, x in enumerate(outer):
        a, b = (side[(2 * x + i) * SUB : (2 * x + i + 1) * SUB] for i in range(2))
        acc[j * LANES : j * LANES + SUB, :] += a
        acc[(j + 1) * LANES - SUB : (j + 1) * LANES, :] += b

    for dx in (1, -1):
        @pl.when(present(dx, 0))
        def _(dx=dx):
            part = w_halo.at[1 if dx == 1 else 0]
            pltpu.make_async_copy(part, part, w_recv.at[1 if dx == 1 else 0]).wait()

    far = [
        [w_halo[side, :, h * LANES : (h + 1) * LANES].astype(F32) for h in range(STEPS)]
        for side in range(2)
    ]

    def spread(x):
        blocks, left = halo_blocks(x), []
        for lo, hi, base, source, shift in blocks:
            for r in range(lo, hi):
                w = far[source][r + shift]
                if turn(r - x):
                    w = pltpu.roll(w, turn(r - x), 1)
                left.append(w.astype(BF16))
        rows = slice(x * LANES, (x + 1) * LANES)
        right = [
            band[rows, (lo - x + base) * LANES : (hi - x + base) * LANES]
            for lo, hi, base, _, _ in blocks
        ]
        return lax.dot_general(
            jnp.concatenate(left, axis=1),
            right[0] if len(right) == 1 else jnp.concatenate(right, axis=1),
            (((1,), (1,)), ((), ())),
            preferred_element_type=F32,
        ).astype(BF16)

    def halo_blocks(x):
        result = []
        for reach, base in ((STEPS, STEPS), (1, 2 * STEPS + 2)):
            if x < STEPS:
                lo, hi, source, shift = x - reach, 0, 0, STEPS
            else:
                lo, hi, source, shift = cx, x + reach + 1, 1, -cx
            if lo < hi:
                result.append((lo, hi, base, source, shift))
        return result

    low, high_rows = STEPS * LANES, (cx - STEPS) * LANES
    total = jnp.dot(
        wt[:, low:high_rows],
        out[STEPS : cx - STEPS].reshape(high_rows - low, cols),
        preferred_element_type=F32,
    )
    total = total + jnp.dot(
        jnp.concatenate([wt[:, :low], wt[:, high_rows:]], axis=1),
        acc[...].astype(BF16),
        preferred_element_type=F32,
    )
    spread_rows = [spread(x) for x in outer]
    for side in range(2):
        total = total + jnp.dot(
            jnp.concatenate(spread_rows[side * STEPS : (side + 1) * STEPS], axis=1),
            ub[slice(0, STEPS) if side == 0 else slice(cx - STEPS, cx)].reshape(low, cols),
            preferred_element_type=F32,
        )
    for g in range(groups):
        ps[pl.ds(g, picks, stride=groups), :] = total[:, g * LANES : (g + 1) * LANES]

    def halo_dot(x, part):
        blocks, field = [], []
        for lo, hi, base, source, shift in halo_blocks(x):
            blocks.append((lo - x + base, hi - x + base))
            for r in range(lo, hi):
                field += turned(r - x, lambda a, b, r=r: xh[source, r + shift, a:b, part])
        return band_dot(x, blocks, field)

    def reduce_copy(k, tx, ty):
        return pltpu.make_async_remote_copy(
            src_ref=ps.at[pl.ds(pl.multiple_of((tx * ny + ty) * tile, tile), tile)],
            dst_ref=rbuf.at[k - 1], send_sem=r_send, recv_sem=r_recv,
            device_id=(tx, ty), device_id_type=MESH,
        )

    while told[0] < len(rounds):
        next_round()

    for j in range(ny):
        @pl.loop(0 if j else 1, nx)
        def _(i, j=j):
            reduce_copy(i * ny + j, *around(i, j)).start()

    for q in range(chunks):
        part = slice(q * CHUNK, (q + 1) * CHUNK)
        for d in DIRS[6:]:
            wait_a(*d, q)
        for j, x in enumerate(outer):
            value = acc[j * LANES : (j + 1) * LANES, part] + halo_dot(x, part)
            out[x, :, part] = value.astype(BF16)

    for dx in (1, -1):
        @pl.when(present(dx, 0))
        def _(dx=dx):
            w_copy(dx).wait_send()

    for dx, dy in DIRS:
        @pl.when(present(dx, dy))
        def _(dx=dx, dy=dy):
            k_copy(dx, dy).wait_send()
            for c in a_copies(dx, dy):
                c.wait_send()

    pltpu.make_async_copy(rbuf, rbuf, r_recv).wait()
    pltpu.make_async_copy(rbuf, rbuf, r_send).wait()

    total = ps[pl.ds(pl.multiple_of(me * tile, tile), tile), :]
    total = total + jnp.sum(rbuf[...], axis=0)
    for r in range(tile // groups):
        for q in range(groups):
            rep[r : r + 1, q * LANES : (q + 1) * LANES] = total[
                r * groups + q : r * groups + q + 1
            ]


def store_kernel(field, owned, field_out, owned_out, sems):
    parts = sems.shape[0] - 1
    rows = field.shape[0] // parts
    copies = [pltpu.make_async_copy(owned, owned_out, sems.at[parts])]
    for p in range(parts):
        part = pl.ds(p * rows, rows)
        copies.append(pltpu.make_async_copy(field.at[part], field_out.at[part], sems.at[p]))
    for c in copies:
        c.start()
    for c in copies:
        c.wait()


def solution(mesh):
    nx, ny = mesh.shape["gx"], mesh.shape["gy"]
    n = nx * ny

    def per_device(adjoint, conduct_x, conduct_y, pick_weights, owner_order):
        cx, cy, cols = adjoint.shape
        picks = pick_weights.shape[0]
        groups = cols // LANES
        chunks = cols // CHUNK
        ex = cx + 2 * STEPS
        tile = picks // n * groups
        kf = -(-ex * 2 * SUB // LANES) * LANES
        vmem = pl.BlockSpec(memory_space=pltpu.VMEM)
        hbm = pl.BlockSpec(memory_space=pl.ANY)
        dma = pltpu.SemaphoreType.DMA
        span = 2 * STEPS + 4
        field, owned = pl.pallas_call(
            functools.partial(kernel, nx, ny),
            out_shape=(
                pltpu.VMEM((cx, cy, cols), BF16),
                pltpu.VMEM((picks // n, cols), F32),
            ),
            in_specs=[hbm] * 4 + [vmem],
            out_specs=(vmem, vmem),
            scratch_shapes=[
                pltpu.VMEM((cx, cy, cols), BF16),
                pltpu.VMEM((2, STEPS, cy, cols), BF16),
                pltpu.VMEM((2, ex, SUB, cols), BF16),
                pltpu.VMEM((kf, cols), BF16),
                pltpu.VMEM((2, cx + 2 * SUB, 3 * LANES), F32),
                pltpu.VMEM((5 * len(NEAR), cx + 2 * SUB, LANES), F32),
                pltpu.VMEM((LANES * cx, LANES), F32),
                pltpu.VMEM((2 * STEPS + 1, LANES, LANES), BF16),
                pltpu.VMEM((2 * SUB, LANES), F32),
                pltpu.VMEM((cx * cy, span * LANES), BF16),
                pltpu.VMEM((cx * 2 * SUB, 2 * kf), BF16),
                pltpu.VMEM((cx * 4 * SUB, cols), F32),
                pltpu.VMEM((2 * STEPS * cy, cols), F32),
                pltpu.VMEM((picks, cx, cy), BF16),
                pltpu.VMEM((picks * cx, LANES), F32),
                pltpu.VMEM((picks, cx * cy), BF16),
                pltpu.VMEM((2, picks, STEPS * cy), BF16),
                pltpu.VMEM((picks * groups, LANES), F32),
                pltpu.VMEM((n - 1, tile, LANES), F32),
                dma,
                dma,
                dma((2,)),
                dma((len(DIRS), chunks)),
                dma((len(DIRS), chunks)),
                dma((len(DIRS),)),
                dma((len(DIRS),)),
                dma((2,)),
                dma((2,)),
                dma,
                dma,
                pltpu.SemaphoreType.REGULAR((len(far_rounds(nx, ny)),)),
            ],
            compiler_params=pltpu.CompilerParams(
                collective_id=0, has_side_effects=True, vmem_limit_bytes=56 << 20
            ),
        )(adjoint, conduct_x, conduct_y, pick_weights, owner_order.reshape(1, picks))
        return pl.pallas_call(
            store_kernel,
            out_shape=(
                jax.ShapeDtypeStruct((cx, cy, cols), BF16),
                jax.ShapeDtypeStruct((picks // n, cols), F32),
            ),
            in_specs=[vmem, vmem],
            out_specs=(hbm, hbm),
            scratch_shapes=[dma((9,))],
        )(*[pltpu.with_memory_space_constraint(v, pltpu.VMEM) for v in (field, owned)])

    return jax.shard_map(
        per_device,
        mesh=mesh,
        in_specs=(P("gx", "gy", None), P("gx", "gy"), P("gx", "gy"), P(None, "gx", "gy"), P()),
        out_specs=(P("gx", "gy", None), P(("gx", "gy"), None)),
        check_vma=False,
    )
```

```python
import functools

import jax
import jax.numpy as jnp
from jax import lax
from jax.experimental import pallas as pl
from jax.experimental.pallas import tpu as pltpu
from jax.sharding import PartitionSpec as P

STEPS = 4
LANES = 128
SUB = 8
CHUNK = 256
MESH = pl.DeviceIdType.MESH
DIRS = ((0, 1), (0, -1), (1, 1), (1, -1), (-1, 1), (-1, -1), (1, 0), (-1, 0))
F32 = jnp.float32
BF16 = jnp.bfloat16
NEAR = [(a, b) for a in range(-2, 3) for b in range(-2, 3) if abs(a) + abs(b) <= 2]
FAR = [(a, b) for a in range(-4, 5) for b in range(-4, 5) if abs(a) + abs(b) <= 4]


def dir_id(dx, dy):
    return DIRS.index((dx, dy))


def centre(dx):
    return SUB if dx == -STEPS else 2 * SUB * (dx + STEPS - 1)


def turn(dx):
    return 2 * SUB if dx == -STEPS else centre(dx)


def turned(dx, get):
    by = turn(dx)
    return [get(LANES - by, LANES), get(0, LANES - by)] if by else [get(0, LANES)]


def far_rounds(nx, ny):
    result = []
    for size, axis in ((nx, 0), (ny, 1)):
        reach = 1
        while reach < size - 1:
            result.append([(d, 0) if axis == 0 else (0, d) for d in (reach, -reach)])
            reach *= 2
    return result


def kernel(
    nx, ny, adj, kx_hbm, ky_hbm, w_hbm, order_hbm, out, rep,
    ub, xh, yb, y_rows, kk, shifted, coef, masks, ends, band, fringe, cells, acc,
    order_ref, wv, w32, wt, w_halo, ps, rbuf,
    own_sem, w_sem, order_sem, k_load, a_send, a_recv, k_send, k_recv, w_send, w_recv, r_send, r_recv, known,
):
    cx, cy, cols = adj.shape
    groups = cols // LANES
    chunks = cols // CHUNK
    ex = cx + 2 * STEPS
    picks = w_hbm.shape[0]
    n = nx * ny
    tile = ps.shape[0] // n
    kf = y_rows.shape[0]
    span = 2 * STEPS + 4
    gx = lax.axis_index("gx")
    gy = lax.axis_index("gy")
    me = gx * ny + gy

    def around(i, j):
        tx, ty = gx + i, gy + j
        return jnp.where(tx >= nx, tx - nx, tx), jnp.where(ty >= ny, ty - ny, ty)

    def present(dx, dy):
        ok = None
        for d, g, size in ((dx, gx, nx), (dy, gy, ny)):
            if d == 0:
                continue
            c = g < size - d if d > 0 else g >= -d
            ok = c if ok is None else jnp.logical_and(ok, c)
        return ok

    own_rows, own_lanes = pl.ds(SUB, cx), pl.ds(LANES, LANES)
    k_loads = [
        pltpu.make_async_copy(src, kk.at[a, own_rows, own_lanes], k_load.at[a])
        for a, src in enumerate((kx_hbm, ky_hbm))
    ]
    for c in k_loads:
        c.start()

    barrier = pltpu.get_barrier_semaphore()
    rounds = far_rounds(nx, ny)

    def greet(semaphore, dx, dy):
        @pl.when(present(dx, dy))
        def _():
            pl.semaphore_signal(
                semaphore, inc=1, device_id=(gx + dx, gy + dy), device_id_type=MESH
            )

    def number(peers):
        return functools.reduce(jnp.add, [jnp.where(present(*d), 1, 0) for d in peers])

    for d in DIRS:
        greet(barrier, *d)

    def hear(i):
        pl.semaphore_wait(known.at[i], number(rounds[i]))

    def tell(i):
        for d in rounds[i]:
            greet(known.at[i], *d)

    own = pltpu.make_async_copy(adj, ub, own_sem)
    w_load = pltpu.make_async_copy(w_hbm, wv, w_sem)
    order_load = pltpu.make_async_copy(order_hbm, order_ref, order_sem)
    for c in [w_load, order_load, own]:
        c.start()

    def k_region(sx, sy):
        rows = {-1: pl.ds(0, SUB), 0: own_rows, 1: pl.ds(SUB + cx, SUB)}[sx]
        return kk.at[:, rows, pl.ds(LANES * (1 + sy), LANES)]

    def a_region(sx, sy):
        if sy == 0:
            return xh.at[0 if sx == -1 else 1]
        rows = {-1: pl.ds(1, STEPS - 1), 0: pl.ds(STEPS, cx), 1: pl.ds(STEPS + cx, STEPS - 1)}[sx]
        return yb.at[0 if sy == 1 else 1, rows]

    def k_copy(dx, dy):
        rows = {1: pl.ds(cx, SUB), 0: own_rows, -1: pl.ds(SUB, SUB)}[dx]
        return pltpu.make_async_remote_copy(
            src_ref=kk.at[:, rows, own_lanes], dst_ref=k_region(-dx, -dy),
            send_sem=k_send.at[dir_id(dx, dy)], recv_sem=k_recv.at[dir_id(-dx, -dy)],
            device_id=(gx + dx, gy + dy), device_id_type=MESH,
        )

    def a_copies(dx, dy):
        slot, mine = dir_id(-dx, -dy), dir_id(dx, dy)
        src = adj
        if dx:
            count = STEPS - 1 if dy else STEPS
            src = src.at[pl.ds(cx - count if dx == 1 else 0, count)]
        if dy:
            src = src.at[:, pl.ds(cy - SUB if dy == 1 else 0, SUB)]
        dst = a_region(-dx, -dy)
        parts = [(src, dst)]
        if dy == 0:
            cut = [pl.ds(q * CHUNK, CHUNK) for q in range(chunks)]
            parts = [(src.at[:, :, c], dst.at[:, :, c]) for c in cut]
        return [
            pltpu.make_async_remote_copy(
                src_ref=s, dst_ref=d, send_sem=a_send.at[mine, q],
                recv_sem=a_recv.at[slot, q], device_id=(gx + dx, gy + dy),
                device_id_type=MESH,
            )
            for q, (s, d) in enumerate(parts)
        ]

    for e in (0, ex - 1):
        yb[:, e] = jnp.zeros((2, SUB, cols), BF16)
    for dx, dy in DIRS:
        @pl.when(jnp.logical_not(present(dx, dy)))
        def _(dx=dx, dy=dy):
            k_part, a_part = k_region(dx, dy), a_region(dx, dy)
            k_part[...] = jnp.zeros(k_part.shape, F32)
            a_part[...] = jnp.zeros(a_part.shape, BF16)

    for c in k_loads:
        c.wait()
    pl.semaphore_wait(barrier, number(DIRS))

    for dx, dy in DIRS:
        @pl.when(present(dx, dy))
        def _(dx=dx, dy=dy):
            k_copy(dx, dy).start()

    for dx, dy in DIRS[:6]:
        @pl.when(present(dx, dy))
        def _(dx=dx, dy=dy):
            for c in a_copies(dx, dy):
                c.start()

    told = [0]

    def next_round():
        i = told[0]
        hear(i)
        if i + 1 < len(rounds):
            tell(i + 1)
        told[0] = i + 1

    tell(0)

    def wait_k(dx, dy):
        @pl.when(present(dx, dy))
        def _():
            part = k_region(dx, dy)
            pltpu.make_async_copy(part, part, k_recv.at[dir_id(dx, dy)]).wait()

    def wait_a(dx, dy, q=0):
        @pl.when(present(dx, dy))
        def _():
            part = a_region(dx, dy)
            if dy == 0:
                part = part.at[:, :, pl.ds(q * CHUNK, CHUNK)]
            pltpu.make_async_copy(part, part, a_recv.at[dir_id(dx, dy), q]).wait()

    def w_copy(dx):
        lo = (cx - STEPS) * LANES if dx == 1 else 0
        slot, mine = (0, 1) if dx == 1 else (1, 0)
        return pltpu.make_async_remote_copy(
            src_ref=wt.at[:, pl.ds(lo, STEPS * LANES)], dst_ref=w_halo.at[slot],
            send_sem=w_send.at[mine], recv_sem=w_recv.at[slot],
            device_id=(gx + dx, gy), device_id_type=MESH,
        )

    w_load.wait()
    order_load.wait()
    pick_ids = lax.broadcasted_iota(jnp.int32, (picks, picks), 0)
    chosen = jnp.where(pick_ids == order_ref[...], F32(1), F32(0)).astype(BF16)
    w32[...] = wv[...].astype(F32).reshape(picks * cx, LANES)
    for x in range(cx):
        row = w32[pl.ds(x, picks, stride=cx), :].astype(BF16)
        row = lax.dot_general(
            chosen, row, (((0,), (0,)), ((), ())), preferred_element_type=F32
        )
        wt[:, x * LANES : (x + 1) * LANES] = row.astype(BF16)

    for dx in (1, -1):
        @pl.when(present(dx, 0))
        def _(dx=dx):
            w_copy(dx).start()

        @pl.when(jnp.logical_not(present(dx, 0)))
        def _(dx=dx):
            part = w_halo.at[1 if dx == 1 else 0]
            part[...] = jnp.zeros(part.shape, BF16)

    for q in range(chunks):
        for dx, dy in DIRS[6:]:
            @pl.when(present(dx, dy))
            def _(dx=dx, dy=dy, q=q):
                a_copies(dx, dy)[q].start()

    coef[...] = jnp.zeros(coef.shape, F32)
    if kf > ex * 2 * SUB:
        y_rows[ex * 2 * SUB :, :] = jnp.zeros((kf - ex * 2 * SUB, cols), BF16)
    lane = lax.broadcasted_iota(jnp.int32, (LANES, LANES), 1)
    cell = lax.broadcasted_iota(jnp.int32, (LANES, LANES), 0)
    for dx in range(-STEPS, STEPS + 1):
        gap = ((lane - turn(dx)) & (LANES - 1)) - cell
        inside = jnp.abs(gap) <= STEPS - abs(dx)
        masks[dx + STEPS] = jnp.where(inside, F32(1), F32(0)).astype(BF16)
    lane, cell = lane[:SUB], cell[:SUB]
    before = after = jnp.zeros((SUB, LANES), F32)
    for dx in range(1 - STEPS, STEPS):
        reach = STEPS - abs(dx)
        place = ((lane - centre(dx) + LANES // 2) & (LANES - 1)) - LANES // 2
        left = (place < 0) & (place >= -STEPS) & (cell - place <= reach)
        right = (place >= 0) & (place < STEPS) & (place + SUB - cell <= reach)
        before = jnp.where(left, F32(1), before)
        after = jnp.where(right, F32(1), after)
    ends[:SUB], ends[SUB:] = before, after

    for d in DIRS:
        wait_k(*d)
    next_round()

    near_end = lax.broadcasted_iota(jnp.int32, (cx + 2 * SUB, LANES), 1) < LANES // 2

    def folded(k):
        past = jnp.where(near_end, k[:, 2 * LANES :], k[:, :LANES])
        return jnp.concatenate([k[:, LANES : 2 * LANES], past], axis=1)

    kx, ky = folded(kk[0]), folded(kk[1])
    kx_at = lax.broadcasted_iota(jnp.int32, kx.shape, 0)
    ky_at = lax.broadcasted_iota(jnp.int32, ky.shape, 1)
    kx = jnp.where(jnp.logical_and(kx_at == SUB + cx - 1, gx == nx - 1), F32(0), kx)
    ky = jnp.where(jnp.logical_and(ky_at == LANES - 1, gy == ny - 1), F32(0), ky)
    high, wide = kx.shape

    def at(value, dx, dy):
        if dx:
            value = pltpu.roll(value, -dx % high, 0)
        if dy:
            value = pltpu.roll(value, -dy % wide, 1)
        return value

    xp, yp = kx, ky
    xm, ym = at(kx, -1, 0), at(ky, 0, -1)
    c = F32(1) - ((xm + xp) + (ym + yp))
    two = {
        (0, 0): c * c + ((xm * xm + xp * xp) + (ym * ym + yp * yp)),
        (1, 0): xp * (c + at(c, 1, 0)),
        (-1, 0): xm * (c + at(c, -1, 0)),
        (0, 1): yp * (c + at(c, 0, 1)),
        (0, -1): ym * (c + at(c, 0, -1)),
        (2, 0): xp * at(xp, 1, 0),
        (-2, 0): xm * at(xm, -1, 0),
        (0, 2): yp * at(yp, 0, 1),
        (0, -2): ym * at(ym, 0, -1),
        (1, 1): xp * at(yp, 1, 0) + yp * at(xp, 0, 1),
        (1, -1): xp * at(ym, 1, 0) + ym * at(xp, 0, -1),
        (-1, 1): xm * at(yp, -1, 0) + yp * at(xm, 0, 1),
        (-1, -1): xm * at(ym, -1, 0) + ym * at(xm, 0, -1),
    }
    for i, d in enumerate(NEAR):
        for dy in range(-2, 3):
            shifted[(dy + 2) * len(NEAR) + i] = at(two[d], 0, dy)[:, :LANES]

    def near(d, dx, dy):
        return shifted[(dy + 2) * len(NEAR) + NEAR.index(d), SUB + dx : SUB + dx + cx]

    for fx, fy in FAR:
        total = None
        for dx, dy in NEAR:
            rest = (fx - dx, fy - dy)
            if rest in NEAR:
                term = near((dx, dy), 0, 0) * near(rest, dx, dy)
                total = term if total is None else total + term
        slot = (centre(fx) + fy) % LANES
        coef[slot * cx : (slot + 1) * cx, :] = total

    def low_part(value):
        high_part = value.astype(BF16)
        return high_part, (value - high_part.astype(F32)).astype(BF16)

    def build(x):
        table = pltpu.roll(
            coef[pl.ds(x, LANES, stride=cx), :].T, 0, 1, stride=1, stride_axis=0
        )
        rows = pl.ds(pl.multiple_of(x * LANES, LANES), LANES)
        big, small = low_part(table)
        for dx in range(-STEPS, STEPS + 1):
            r = dx + STEPS
            source = big
            if dx == -STEPS:
                source = pltpu.roll(table, SUB, 1).astype(BF16)
            band[rows, r * LANES : (r + 1) * LANES] = source * masks[r]
            if abs(dx) <= 1:
                k = 2 * STEPS + 2 + dx
                band[rows, k * LANES : (k + 1) * LANES] = small * masks[r]
        edge = jnp.concatenate([table[:SUB], table[cy - SUB :]], axis=0) * ends[...]
        edge = pltpu.roll(edge, SUB, 1)
        edge = jnp.concatenate([edge] + [jnp.zeros_like(edge)] * (kf // LANES - 1), axis=1)
        big, small = low_part(pltpu.roll(edge, (x + 1) * 2 * SUB, 1))
        rows = pl.ds(pl.multiple_of(x * 2 * SUB, 2 * SUB), 2 * SUB)
        fringe[rows, :kf] = big
        fringe[rows, kf:] = small

    def fill_fringe():
        for e in range(ex):
            pair = jnp.concatenate([yb[1, e].astype(F32), yb[0, e].astype(F32)], axis=0)
            y_rows[e * 2 * SUB : (e + 1) * 2 * SUB, :] = pair.astype(BF16)

    def band_dot(x, blocks, field):
        rows = slice(x * LANES, (x + 1) * LANES)
        left = [band[rows, lo * LANES : hi * LANES] for lo, hi in blocks]
        return jnp.dot(
            left[0] if len(left) == 1 else jnp.concatenate(left, axis=1),
            field[0] if len(field) == 1 else jnp.concatenate(field, axis=0),
            preferred_element_type=F32,
        )

    def own_dot(x):
        blocks, field = [], []
        for reach, base in ((STEPS, STEPS), (1, 2 * STEPS + 2)):
            lo, hi = max(x - reach, 0), min(x + reach, cx - 1) + 1
            blocks.append((lo - x + base, hi - x + base))
            for r in range(lo, hi):
                field += turned(r - x, lambda a, b, r=r: ub[r, a:b])
        if blocks[0][1] == blocks[1][0]:
            blocks = [(blocks[0][0], blocks[1][1])]
        return band_dot(x, blocks, field)

    @pl.loop(0, cx // 4)
    def _(p):
        for i in range(4):
            build(4 * p + i)

    inner = range(STEPS, cx - STEPS)
    outer = list(range(STEPS)) + list(range(cx - STEPS, cx))
    edge_rows = 2 * SUB
    own.wait()
    next_round()
    for x in inner:
        value = own_dot(x)
        out[x] = value.astype(BF16)
        base = x * 2 * edge_rows
        cells[base : base + edge_rows, :] = value[:edge_rows]
        cells[base + edge_rows : base + 2 * edge_rows, :] = value[cy - edge_rows :]
    for j, x in enumerate(outer):
        acc[j * LANES : (j + 1) * LANES, :] = own_dot(x)

    for d in DIRS[:6]:
        wait_a(*d)
    next_round()
    fill_fringe()
    y = y_rows[...]
    side = jnp.dot(fringe[:, :kf], y, preferred_element_type=F32)
    side = side + jnp.dot(fringe[:, kf:], y, preferred_element_type=F32)
    for x in inner:
        base = x * 2 * edge_rows
        top = cells[base : base + edge_rows, :]
        bottom = cells[base + edge_rows : base + 2 * edge_rows, :]
        a, b = (side[(2 * x + i) * SUB : (2 * x + i + 1) * SUB] for i in range(2))
        top = jnp.concatenate([top[:SUB] + a, top[SUB:]], axis=0)
        bottom = jnp.concatenate([bottom[:SUB], bottom[SUB:] + b], axis=0)
        out[x, :edge_rows] = top.astype(BF16)
        out[x, cy - edge_rows :] = bottom.astype(BF16)
    for j, x in enumerate(outer):
        a, b = (side[(2 * x + i) * SUB : (2 * x + i + 1) * SUB] for i in range(2))
        acc[j * LANES : j * LANES + SUB, :] += a
        acc[(j + 1) * LANES - SUB : (j + 1) * LANES, :] += b

    for dx in (1, -1):
        @pl.when(present(dx, 0))
        def _(dx=dx):
            part = w_halo.at[1 if dx == 1 else 0]
            pltpu.make_async_copy(part, part, w_recv.at[1 if dx == 1 else 0]).wait()

    far = [
        [w_halo[side, :, h * LANES : (h + 1) * LANES].astype(F32) for h in range(STEPS)]
        for side in range(2)
    ]

    def spread(x):
        blocks, left = halo_blocks(x), []
        for lo, hi, base, source, shift in blocks:
            for r in range(lo, hi):
                w = far[source][r + shift]
                if turn(r - x):
                    w = pltpu.roll(w, turn(r - x), 1)
                left.append(w.astype(BF16))
        rows = slice(x * LANES, (x + 1) * LANES)
        right = [
            band[rows, (lo - x + base) * LANES : (hi - x + base) * LANES]
            for lo, hi, base, _, _ in blocks
        ]
        return lax.dot_general(
            jnp.concatenate(left, axis=1),
            right[0] if len(right) == 1 else jnp.concatenate(right, axis=1),
            (((1,), (1,)), ((), ())),
            preferred_element_type=F32,
        ).astype(BF16)

    def halo_blocks(x):
        result = []
        for reach, base in ((STEPS, STEPS), (1, 2 * STEPS + 2)):
            if x < STEPS:
                lo, hi, source, shift = x - reach, 0, 0, STEPS
            else:
                lo, hi, source, shift = cx, x + reach + 1, 1, -cx
            if lo < hi:
                result.append((lo, hi, base, source, shift))
        return result

    low, high_rows = STEPS * LANES, (cx - STEPS) * LANES
    total = jnp.dot(
        wt[:, low:high_rows],
        out[STEPS : cx - STEPS].reshape(high_rows - low, cols),
        preferred_element_type=F32,
    )
    total = total + jnp.dot(
        jnp.concatenate([wt[:, :low], wt[:, high_rows:]], axis=1),
        acc[...].astype(BF16),
        preferred_element_type=F32,
    )
    spread_rows = [spread(x) for x in outer]
    for side in range(2):
        total = total + jnp.dot(
            jnp.concatenate(spread_rows[side * STEPS : (side + 1) * STEPS], axis=1),
            ub[slice(0, STEPS) if side == 0 else slice(cx - STEPS, cx)].reshape(low, cols),
            preferred_element_type=F32,
        )
    for g in range(groups):
        ps[pl.ds(g, picks, stride=groups), :] = total[:, g * LANES : (g + 1) * LANES]

    def halo_dot(x, part):
        blocks, field = [], []
        for lo, hi, base, source, shift in halo_blocks(x):
            blocks.append((lo - x + base, hi - x + base))
            for r in range(lo, hi):
                field += turned(r - x, lambda a, b, r=r: xh[source, r + shift, a:b, part])
        return band_dot(x, blocks, field)

    def reduce_copy(k, tx, ty):
        return pltpu.make_async_remote_copy(
            src_ref=ps.at[pl.ds(pl.multiple_of((tx * ny + ty) * tile, tile), tile)],
            dst_ref=rbuf.at[k - 1], send_sem=r_send, recv_sem=r_recv,
            device_id=(tx, ty), device_id_type=MESH,
        )

    while told[0] < len(rounds):
        next_round()

    for j in range(ny):
        @pl.loop(0 if j else 1, nx)
        def _(i, j=j):
            reduce_copy(i * ny + j, *around(i, j)).start()

    for q in range(chunks):
        part = slice(q * CHUNK, (q + 1) * CHUNK)
        for d in DIRS[6:]:
            wait_a(*d, q)
        for j, x in enumerate(outer):
            value = acc[j * LANES : (j + 1) * LANES, part] + halo_dot(x, part)
            out[x, :, part] = value.astype(BF16)

    for dx in (1, -1):
        @pl.when(present(dx, 0))
        def _(dx=dx):
            w_copy(dx).wait_send()

    for dx, dy in DIRS:
        @pl.when(present(dx, dy))
        def _(dx=dx, dy=dy):
            k_copy(dx, dy).wait_send()
            for c in a_copies(dx, dy):
                c.wait_send()

    pltpu.make_async_copy(rbuf, rbuf, r_recv).wait()
    pltpu.make_async_copy(rbuf, rbuf, r_send).wait()

    total = ps[pl.ds(pl.multiple_of(me * tile, tile), tile), :]
    total = total + jnp.sum(rbuf[...], axis=0)
    for r in range(tile // groups):
        for q in range(groups):
            rep[r : r + 1, q * LANES : (q + 1) * LANES] = total[
                r * groups + q : r * groups + q + 1
            ]


def store_kernel(field, owned, field_out, owned_out, sems):
    parts = sems.shape[0] - 1
    rows = field.shape[0] // parts
    copies = [pltpu.make_async_copy(owned, owned_out, sems.at[parts])]
    for p in range(parts):
        part = pl.ds(p * rows, rows)
        copies.append(pltpu.make_async_copy(field.at[part], field_out.at[part], sems.at[p]))
    for c in copies:
        c.start()
    for c in copies:
        c.wait()


def solution(mesh):
    nx, ny = mesh.shape["gx"], mesh.shape["gy"]
    n = nx * ny

    def per_device(adjoint, conduct_x, conduct_y, pick_weights, owner_order):
        cx, cy, cols = adjoint.shape
        picks = pick_weights.shape[0]
        groups = cols // LANES
        chunks = cols // CHUNK
        ex = cx + 2 * STEPS
        tile = picks // n * groups
        kf = -(-ex * 2 * SUB // LANES) * LANES
        vmem = pl.BlockSpec(memory_space=pltpu.VMEM)
        hbm = pl.BlockSpec(memory_space=pl.ANY)
        dma = pltpu.SemaphoreType.DMA
        span = 2 * STEPS + 4
        field, owned = pl.pallas_call(
            functools.partial(kernel, nx, ny),
            out_shape=(
                pltpu.VMEM((cx, cy, cols), BF16),
                pltpu.VMEM((picks // n, cols), F32),
            ),
            in_specs=[hbm] * 5,
            out_specs=(vmem, vmem),
            scratch_shapes=[
                pltpu.VMEM((cx, cy, cols), BF16),
                pltpu.VMEM((2, STEPS, cy, cols), BF16),
                pltpu.VMEM((2, ex, SUB, cols), BF16),
                pltpu.VMEM((kf, cols), BF16),
                pltpu.VMEM((2, cx + 2 * SUB, 3 * LANES), F32),
                pltpu.VMEM((5 * len(NEAR), cx + 2 * SUB, LANES), F32),
                pltpu.VMEM((LANES * cx, LANES), F32),
                pltpu.VMEM((2 * STEPS + 1, LANES, LANES), BF16),
                pltpu.VMEM((2 * SUB, LANES), F32),
                pltpu.VMEM((cx * cy, span * LANES), BF16),
                pltpu.VMEM((cx * 2 * SUB, 2 * kf), BF16),
                pltpu.VMEM((cx * 4 * SUB, cols), F32),
                pltpu.VMEM((2 * STEPS * cy, cols), F32),
                pltpu.VMEM((1, picks), jnp.int32),
                pltpu.VMEM((picks, cx, cy), BF16),
                pltpu.VMEM((picks * cx, LANES), F32),
                pltpu.VMEM((picks, cx * cy), BF16),
                pltpu.VMEM((2, picks, STEPS * cy), BF16),
                pltpu.VMEM((picks * groups, LANES), F32),
                pltpu.VMEM((n - 1, tile, LANES), F32),
                dma,
                dma,
                dma,
                dma((2,)),
                dma((len(DIRS), chunks)),
                dma((len(DIRS), chunks)),
                dma((len(DIRS),)),
                dma((len(DIRS),)),
                dma((2,)),
                dma((2,)),
                dma,
                dma,
                pltpu.SemaphoreType.REGULAR((len(far_rounds(nx, ny)),)),
            ],
            compiler_params=pltpu.CompilerParams(
                collective_id=0, has_side_effects=True, vmem_limit_bytes=56 << 20
            ),
        )(adjoint, conduct_x, conduct_y, pick_weights, owner_order.reshape(1, picks))
        return pl.pallas_call(
            store_kernel,
            out_shape=(
                jax.ShapeDtypeStruct((cx, cy, cols), BF16),
                jax.ShapeDtypeStruct((picks // n, cols), F32),
            ),
            in_specs=[vmem, vmem],
            out_specs=(hbm, hbm),
            scratch_shapes=[dma((3,))],
        )(*[pltpu.with_memory_space_constraint(v, pltpu.VMEM) for v in (field, owned)])

    return jax.shard_map(
        per_device,
        mesh=mesh,
        in_specs=(P("gx", "gy", None), P("gx", "gy"), P("gx", "gy"), P(None, "gx", "gy"), P()),
        out_specs=(P("gx", "gy", None), P(("gx", "gy"), None)),
        check_vma=False,
    )
```

```python
import functools

import jax
import jax.numpy as jnp
from jax import lax
from jax.experimental import pallas as pl
from jax.experimental.pallas import tpu as pltpu
from jax.sharding import PartitionSpec as P

STEPS = 4
LANES = 128
SUB = 8
CHUNK = 256
MESH = pl.DeviceIdType.MESH
DIRS = ((0, 1), (0, -1), (1, 1), (1, -1), (-1, 1), (-1, -1), (1, 0), (-1, 0))
F32 = jnp.float32
BF16 = jnp.bfloat16
NEAR = [(a, b) for a in range(-2, 3) for b in range(-2, 3) if abs(a) + abs(b) <= 2]
FAR = [(a, b) for a in range(-4, 5) for b in range(-4, 5) if abs(a) + abs(b) <= 4]


def dir_id(dx, dy):
    return DIRS.index((dx, dy))


def centre(dx):
    return SUB if dx == -STEPS else 2 * SUB * (dx + STEPS - 1)


def turn(dx):
    return 2 * SUB if dx == -STEPS else centre(dx)


def turned(dx, get):
    by = turn(dx)
    return [get(LANES - by, LANES), get(0, LANES - by)] if by else [get(0, LANES)]


def far_rounds(nx, ny):
    result = []
    for size, axis in ((nx, 0), (ny, 1)):
        reach = 1
        while reach < size - 1:
            result.append([(d, 0) if axis == 0 else (0, d) for d in (reach, -reach)])
            reach *= 2
    return result


def kernel(
    nx, ny, adj, kx_hbm, ky_hbm, w_hbm, order_hbm, out, rep,
    ub, xh, yb, y_rows, kk, shifted, coef, masks, ends, band, fringe, cells, acc,
    order_ref, wv, w32, wt, w_halo, ps, rbuf,
    own_sem, w_sem, order_sem, k_load, a_send, a_recv, k_send, k_recv, w_send, w_recv, r_send, r_recv, known,
):
    cx, cy, cols = adj.shape
    groups = cols // LANES
    chunks = cols // CHUNK
    ex = cx + 2 * STEPS
    picks = w_hbm.shape[0]
    n = nx * ny
    tile = ps.shape[0] // n
    kf = y_rows.shape[0]
    span = 2 * STEPS + 4
    gx = lax.axis_index("gx")
    gy = lax.axis_index("gy")
    me = gx * ny + gy

    def around(i, j):
        tx, ty = gx + i, gy + j
        return jnp.where(tx >= nx, tx - nx, tx), jnp.where(ty >= ny, ty - ny, ty)

    def present(dx, dy):
        ok = None
        for d, g, size in ((dx, gx, nx), (dy, gy, ny)):
            if d == 0:
                continue
            c = g < size - d if d > 0 else g >= -d
            ok = c if ok is None else jnp.logical_and(ok, c)
        return ok

    own_rows, own_lanes = pl.ds(SUB, cx), pl.ds(LANES, LANES)
    k_loads = [
        pltpu.make_async_copy(src, kk.at[a, own_rows, own_lanes], k_load.at[a])
        for a, src in enumerate((kx_hbm, ky_hbm))
    ]
    for c in k_loads:
        c.start()

    barrier = pltpu.get_barrier_semaphore()
    rounds = far_rounds(nx, ny)

    def greet(semaphore, dx, dy):
        @pl.when(present(dx, dy))
        def _():
            pl.semaphore_signal(
                semaphore, inc=1, device_id=(gx + dx, gy + dy), device_id_type=MESH
            )

    def number(peers):
        return functools.reduce(jnp.add, [jnp.where(present(*d), 1, 0) for d in peers])

    for d in DIRS:
        greet(barrier, *d)

    def hear(i):
        pl.semaphore_wait(known.at[i], number(rounds[i]))

    def tell(i):
        for d in rounds[i]:
            greet(known.at[i], *d)

    own = pltpu.make_async_copy(adj, ub, own_sem)
    w_load = pltpu.make_async_copy(w_hbm, wv, w_sem)
    order_load = pltpu.make_async_copy(order_hbm, order_ref, order_sem)
    for c in [w_load, order_load, own]:
        c.start()

    def k_region(sx, sy):
        rows = {-1: pl.ds(0, SUB), 0: own_rows, 1: pl.ds(SUB + cx, SUB)}[sx]
        return kk.at[:, rows, pl.ds(LANES * (1 + sy), LANES)]

    def a_region(sx, sy):
        if sy == 0:
            return xh.at[0 if sx == -1 else 1]
        rows = {-1: pl.ds(1, STEPS - 1), 0: pl.ds(STEPS, cx), 1: pl.ds(STEPS + cx, STEPS - 1)}[sx]
        return yb.at[0 if sy == 1 else 1, rows]

    def k_copy(dx, dy):
        rows = {1: pl.ds(cx, SUB), 0: own_rows, -1: pl.ds(SUB, SUB)}[dx]
        return pltpu.make_async_remote_copy(
            src_ref=kk.at[:, rows, own_lanes], dst_ref=k_region(-dx, -dy),
            send_sem=k_send.at[dir_id(dx, dy)], recv_sem=k_recv.at[dir_id(-dx, -dy)],
            device_id=(gx + dx, gy + dy), device_id_type=MESH,
        )

    def a_copies(dx, dy):
        slot, mine = dir_id(-dx, -dy), dir_id(dx, dy)
        src = adj
        if dx:
            count = STEPS - 1 if dy else STEPS
            src = src.at[pl.ds(cx - count if dx == 1 else 0, count)]
        if dy:
            src = src.at[:, pl.ds(cy - SUB if dy == 1 else 0, SUB)]
        dst = a_region(-dx, -dy)
        parts = [(src, dst)]
        if dy == 0:
            cut = [pl.ds(q * CHUNK, CHUNK) for q in range(chunks)]
            parts = [(src.at[:, :, c], dst.at[:, :, c]) for c in cut]
        return [
            pltpu.make_async_remote_copy(
                src_ref=s, dst_ref=d, send_sem=a_send.at[mine, q],
                recv_sem=a_recv.at[slot, q], device_id=(gx + dx, gy + dy),
                device_id_type=MESH,
            )
            for q, (s, d) in enumerate(parts)
        ]

    for e in (0, ex - 1):
        yb[:, e] = jnp.zeros((2, SUB, cols), BF16)
    for dx, dy in DIRS:
        @pl.when(jnp.logical_not(present(dx, dy)))
        def _(dx=dx, dy=dy):
            k_part, a_part = k_region(dx, dy), a_region(dx, dy)
            k_part[...] = jnp.zeros(k_part.shape, F32)
            a_part[...] = jnp.zeros(a_part.shape, BF16)

    coef[...] = jnp.zeros(coef.shape, F32)
    if kf > ex * 2 * SUB:
        y_rows[ex * 2 * SUB :, :] = jnp.zeros((kf - ex * 2 * SUB, cols), BF16)
    lane = lax.broadcasted_iota(jnp.int32, (LANES, LANES), 1)
    cell = lax.broadcasted_iota(jnp.int32, (LANES, LANES), 0)
    for dx in range(-STEPS, STEPS + 1):
        gap = ((lane - turn(dx)) & (LANES - 1)) - cell
        inside = jnp.abs(gap) <= STEPS - abs(dx)
        masks[dx + STEPS] = jnp.where(inside, F32(1), F32(0)).astype(BF16)
    lane, cell = lane[:SUB], cell[:SUB]
    before = after = jnp.zeros((SUB, LANES), F32)
    for dx in range(1 - STEPS, STEPS):
        reach = STEPS - abs(dx)
        place = ((lane - centre(dx) + LANES // 2) & (LANES - 1)) - LANES // 2
        left = (place < 0) & (place >= -STEPS) & (cell - place <= reach)
        right = (place >= 0) & (place < STEPS) & (place + SUB - cell <= reach)
        before = jnp.where(left, F32(1), before)
        after = jnp.where(right, F32(1), after)
    ends[:SUB], ends[SUB:] = before, after

    for c in k_loads:
        c.wait()
    pl.semaphore_wait(barrier, number(DIRS))

    for dx, dy in DIRS:
        @pl.when(present(dx, dy))
        def _(dx=dx, dy=dy):
            k_copy(dx, dy).start()

    for dx, dy in DIRS[:6]:
        @pl.when(present(dx, dy))
        def _(dx=dx, dy=dy):
            for c in a_copies(dx, dy):
                c.start()

    told = [0]

    def next_round():
        i = told[0]
        hear(i)
        if i + 1 < len(rounds):
            tell(i + 1)
        told[0] = i + 1

    tell(0)

    def wait_k(dx, dy):
        @pl.when(present(dx, dy))
        def _():
            part = k_region(dx, dy)
            pltpu.make_async_copy(part, part, k_recv.at[dir_id(dx, dy)]).wait()

    def wait_a(dx, dy, q=0):
        @pl.when(present(dx, dy))
        def _():
            part = a_region(dx, dy)
            if dy == 0:
                part = part.at[:, :, pl.ds(q * CHUNK, CHUNK)]
            pltpu.make_async_copy(part, part, a_recv.at[dir_id(dx, dy), q]).wait()

    def w_copy(dx):
        lo = (cx - STEPS) * LANES if dx == 1 else 0
        slot, mine = (0, 1) if dx == 1 else (1, 0)
        return pltpu.make_async_remote_copy(
            src_ref=wt.at[:, pl.ds(lo, STEPS * LANES)], dst_ref=w_halo.at[slot],
            send_sem=w_send.at[mine], recv_sem=w_recv.at[slot],
            device_id=(gx + dx, gy), device_id_type=MESH,
        )

    w_load.wait()
    order_load.wait()
    pick_ids = lax.broadcasted_iota(jnp.int32, (picks, picks), 0)
    chosen = jnp.where(pick_ids == order_ref[...], F32(1), F32(0)).astype(BF16)
    w32[...] = wv[...].astype(F32).reshape(picks * cx, LANES)
    for x in range(cx):
        row = w32[pl.ds(x, picks, stride=cx), :].astype(BF16)
        row = lax.dot_general(
            chosen, row, (((0,), (0,)), ((), ())), preferred_element_type=F32
        )
        wt[:, x * LANES : (x + 1) * LANES] = row.astype(BF16)

    for dx in (1, -1):
        @pl.when(present(dx, 0))
        def _(dx=dx):
            w_copy(dx).start()

        @pl.when(jnp.logical_not(present(dx, 0)))
        def _(dx=dx):
            part = w_halo.at[1 if dx == 1 else 0]
            part[...] = jnp.zeros(part.shape, BF16)

    for d in DIRS:
        wait_k(*d)
    for q in range(chunks):
        for dx, dy in DIRS[6:]:
            @pl.when(present(dx, dy))
            def _(dx=dx, dy=dy, q=q):
                a_copies(dx, dy)[q].start()

    next_round()

    near_end = lax.broadcasted_iota(jnp.int32, (cx + 2 * SUB, LANES), 1) < LANES // 2

    def folded(k):
        past = jnp.where(near_end, k[:, 2 * LANES :], k[:, :LANES])
        return jnp.concatenate([k[:, LANES : 2 * LANES], past], axis=1)

    kx, ky = folded(kk[0]), folded(kk[1])
    kx_at = lax.broadcasted_iota(jnp.int32, kx.shape, 0)
    ky_at = lax.broadcasted_iota(jnp.int32, ky.shape, 1)
    kx = jnp.where(jnp.logical_and(kx_at == SUB + cx - 1, gx == nx - 1), F32(0), kx)
    ky = jnp.where(jnp.logical_and(ky_at == LANES - 1, gy == ny - 1), F32(0), ky)
    high, wide = kx.shape

    def at(value, dx, dy):
        if dx:
            value = pltpu.roll(value, -dx % high, 0)
        if dy:
            value = pltpu.roll(value, -dy % wide, 1)
        return value

    xp, yp = kx, ky
    xm, ym = at(kx, -1, 0), at(ky, 0, -1)
    c = F32(1) - ((xm + xp) + (ym + yp))
    two = {
        (0, 0): c * c + ((xm * xm + xp * xp) + (ym * ym + yp * yp)),
        (1, 0): xp * (c + at(c, 1, 0)),
        (-1, 0): xm * (c + at(c, -1, 0)),
        (0, 1): yp * (c + at(c, 0, 1)),
        (0, -1): ym * (c + at(c, 0, -1)),
        (2, 0): xp * at(xp, 1, 0),
        (-2, 0): xm * at(xm, -1, 0),
        (0, 2): yp * at(yp, 0, 1),
        (0, -2): ym * at(ym, 0, -1),
        (1, 1): xp * at(yp, 1, 0) + yp * at(xp, 0, 1),
        (1, -1): xp * at(ym, 1, 0) + ym * at(xp, 0, -1),
        (-1, 1): xm * at(yp, -1, 0) + yp * at(xm, 0, 1),
        (-1, -1): xm * at(ym, -1, 0) + ym * at(xm, 0, -1),
    }
    for i, d in enumerate(NEAR):
        for dy in range(-2, 3):
            shifted[(dy + 2) * len(NEAR) + i] = at(two[d], 0, dy)[:, :LANES]

    def near(d, dx, dy):
        return shifted[(dy + 2) * len(NEAR) + NEAR.index(d), SUB + dx : SUB + dx + cx]

    for fx, fy in FAR:
        total = None
        for dx, dy in NEAR:
            rest = (fx - dx, fy - dy)
            if rest in NEAR:
                term = near((dx, dy), 0, 0) * near(rest, dx, dy)
                total = term if total is None else total + term
        slot = (centre(fx) + fy) % LANES
        coef[slot * cx : (slot + 1) * cx, :] = total

    def low_part(value):
        high_part = value.astype(BF16)
        return high_part, (value - high_part.astype(F32)).astype(BF16)

    def build(x):
        table = pltpu.roll(
            coef[pl.ds(x, LANES, stride=cx), :].T, 0, 1, stride=1, stride_axis=0
        )
        rows = pl.ds(pl.multiple_of(x * LANES, LANES), LANES)
        big, small = low_part(table)
        for dx in range(-STEPS, STEPS + 1):
            r = dx + STEPS
            source = big
            if dx == -STEPS:
                source = pltpu.roll(table, SUB, 1).astype(BF16)
            band[rows, r * LANES : (r + 1) * LANES] = source * masks[r]
            if abs(dx) <= 1:
                k = 2 * STEPS + 2 + dx
                band[rows, k * LANES : (k + 1) * LANES] = small * masks[r]
        edge = jnp.concatenate([table[:SUB], table[cy - SUB :]], axis=0) * ends[...]
        edge = pltpu.roll(edge, SUB, 1)
        edge = jnp.concatenate([edge] + [jnp.zeros_like(edge)] * (kf // LANES - 1), axis=1)
        big, small = low_part(pltpu.roll(edge, (x + 1) * 2 * SUB, 1))
        rows = pl.ds(pl.multiple_of(x * 2 * SUB, 2 * SUB), 2 * SUB)
        fringe[rows, :kf] = big
        fringe[rows, kf:] = small

    def fill_fringe():
        for e in range(ex):
            pair = jnp.concatenate([yb[1, e].astype(F32), yb[0, e].astype(F32)], axis=0)
            y_rows[e * 2 * SUB : (e + 1) * 2 * SUB, :] = pair.astype(BF16)

    def band_dot(x, blocks, field):
        rows = slice(x * LANES, (x + 1) * LANES)
        left = [band[rows, lo * LANES : hi * LANES] for lo, hi in blocks]
        return jnp.dot(
            left[0] if len(left) == 1 else jnp.concatenate(left, axis=1),
            field[0] if len(field) == 1 else jnp.concatenate(field, axis=0),
            preferred_element_type=F32,
        )

    def own_dot(x):
        blocks, field = [], []
        for reach, base in ((STEPS, STEPS), (1, 2 * STEPS + 2)):
            lo, hi = max(x - reach, 0), min(x + reach, cx - 1) + 1
            blocks.append((lo - x + base, hi - x + base))
            for r in range(lo, hi):
                field += turned(r - x, lambda a, b, r=r: ub[r, a:b])
        if blocks[0][1] == blocks[1][0]:
            blocks = [(blocks[0][0], blocks[1][1])]
        return band_dot(x, blocks, field)

    @pl.loop(0, cx // 4)
    def _(p):
        for i in range(4):
            build(4 * p + i)

    inner = range(STEPS, cx - STEPS)
    outer = list(range(STEPS)) + list(range(cx - STEPS, cx))
    edge_rows = 2 * SUB
    own.wait()
    next_round()
    for x in inner:
        value = own_dot(x)
        out[x] = value.astype(BF16)
        base = x * 2 * edge_rows
        cells[base : base + edge_rows, :] = value[:edge_rows]
        cells[base + edge_rows : base + 2 * edge_rows, :] = value[cy - edge_rows :]
    for j, x in enumerate(outer):
        acc[j * LANES : (j + 1) * LANES, :] = own_dot(x)

    for d in DIRS[:6]:
        wait_a(*d)
    next_round()
    fill_fringe()
    y = y_rows[...]
    side = jnp.dot(fringe[:, :kf], y, preferred_element_type=F32)
    side = side + jnp.dot(fringe[:, kf:], y, preferred_element_type=F32)
    for x in inner:
        base = x * 2 * edge_rows
        top = cells[base : base + edge_rows, :]
        bottom = cells[base + edge_rows : base + 2 * edge_rows, :]
        a, b = (side[(2 * x + i) * SUB : (2 * x + i + 1) * SUB] for i in range(2))
        top = jnp.concatenate([top[:SUB] + a, top[SUB:]], axis=0)
        bottom = jnp.concatenate([bottom[:SUB], bottom[SUB:] + b], axis=0)
        out[x, :edge_rows] = top.astype(BF16)
        out[x, cy - edge_rows :] = bottom.astype(BF16)
    for j, x in enumerate(outer):
        a, b = (side[(2 * x + i) * SUB : (2 * x + i + 1) * SUB] for i in range(2))
        acc[j * LANES : j * LANES + SUB, :] += a
        acc[(j + 1) * LANES - SUB : (j + 1) * LANES, :] += b

    for dx in (1, -1):
        @pl.when(present(dx, 0))
        def _(dx=dx):
            part = w_halo.at[1 if dx == 1 else 0]
            pltpu.make_async_copy(part, part, w_recv.at[1 if dx == 1 else 0]).wait()

    far = [
        [w_halo[side, :, h * LANES : (h + 1) * LANES].astype(F32) for h in range(STEPS)]
        for side in range(2)
    ]

    def spread(x):
        blocks, left = halo_blocks(x), []
        for lo, hi, base, source, shift in blocks:
            for r in range(lo, hi):
                w = far[source][r + shift]
                if turn(r - x):
                    w = pltpu.roll(w, turn(r - x), 1)
                left.append(w.astype(BF16))
        rows = slice(x * LANES, (x + 1) * LANES)
        right = [
            band[rows, (lo - x + base) * LANES : (hi - x + base) * LANES]
            for lo, hi, base, _, _ in blocks
        ]
        return lax.dot_general(
            jnp.concatenate(left, axis=1),
            right[0] if len(right) == 1 else jnp.concatenate(right, axis=1),
            (((1,), (1,)), ((), ())),
            preferred_element_type=F32,
        ).astype(BF16)

    def halo_blocks(x):
        result = []
        for reach, base in ((STEPS, STEPS), (1, 2 * STEPS + 2)):
            if x < STEPS:
                lo, hi, source, shift = x - reach, 0, 0, STEPS
            else:
                lo, hi, source, shift = cx, x + reach + 1, 1, -cx
            if lo < hi:
                result.append((lo, hi, base, source, shift))
        return result

    low, high_rows = STEPS * LANES, (cx - STEPS) * LANES
    total = jnp.dot(
        wt[:, low:high_rows],
        out[STEPS : cx - STEPS].reshape(high_rows - low, cols),
        preferred_element_type=F32,
    )
    total = total + jnp.dot(
        jnp.concatenate([wt[:, :low], wt[:, high_rows:]], axis=1),
        acc[...].astype(BF16),
        preferred_element_type=F32,
    )
    spread_rows = [spread(x) for x in outer]
    for side in range(2):
        total = total + jnp.dot(
            jnp.concatenate(spread_rows[side * STEPS : (side + 1) * STEPS], axis=1),
            ub[slice(0, STEPS) if side == 0 else slice(cx - STEPS, cx)].reshape(low, cols),
            preferred_element_type=F32,
        )
    for g in range(groups):
        ps[pl.ds(g, picks, stride=groups), :] = total[:, g * LANES : (g + 1) * LANES]

    def halo_dot(x, part):
        blocks, field = [], []
        for lo, hi, base, source, shift in halo_blocks(x):
            blocks.append((lo - x + base, hi - x + base))
            for r in range(lo, hi):
                field += turned(r - x, lambda a, b, r=r: xh[source, r + shift, a:b, part])
        return band_dot(x, blocks, field)

    def reduce_copy(k, tx, ty):
        return pltpu.make_async_remote_copy(
            src_ref=ps.at[pl.ds(pl.multiple_of((tx * ny + ty) * tile, tile), tile)],
            dst_ref=rbuf.at[k - 1], send_sem=r_send, recv_sem=r_recv,
            device_id=(tx, ty), device_id_type=MESH,
        )

    while told[0] < len(rounds):
        next_round()

    near = nx // 4
    for lo, hi in ((near, nx - near + 1), (1, near), (nx - near + 1, nx)):
        @pl.loop(lo, hi)
        def _(i):
            for j in range(ny):
                reduce_copy(i * ny + j, *around(i, j)).start()

    for j in range(1, ny):
        reduce_copy(j, *around(0, j)).start()

    for q in range(chunks):
        part = slice(q * CHUNK, (q + 1) * CHUNK)
        for d in DIRS[6:]:
            wait_a(*d, q)
        for j, x in enumerate(outer):
            value = acc[j * LANES : (j + 1) * LANES, part] + halo_dot(x, part)
            out[x, :, part] = value.astype(BF16)

    for dx in (1, -1):
        @pl.when(present(dx, 0))
        def _(dx=dx):
            w_copy(dx).wait_send()

    for dx, dy in DIRS:
        @pl.when(present(dx, dy))
        def _(dx=dx, dy=dy):
            k_copy(dx, dy).wait_send()
            for c in a_copies(dx, dy):
                c.wait_send()

    pltpu.make_async_copy(rbuf, rbuf, r_recv).wait()
    pltpu.make_async_copy(rbuf, rbuf, r_send).wait()

    total = ps[pl.ds(pl.multiple_of(me * tile, tile), tile), :]
    total = total + jnp.sum(rbuf[...], axis=0)
    for r in range(tile // groups):
        for q in range(groups):
            rep[r : r + 1, q * LANES : (q + 1) * LANES] = total[
                r * groups + q : r * groups + q + 1
            ]


def store_kernel(field, owned, field_out, owned_out, sems):
    parts = sems.shape[0] - 1
    rows = field.shape[0] // parts
    copies = [pltpu.make_async_copy(owned, owned_out, sems.at[parts])]
    for p in range(parts):
        part = pl.ds(p * rows, rows)
        copies.append(pltpu.make_async_copy(field.at[part], field_out.at[part], sems.at[p]))
    for c in copies:
        c.start()
    for c in copies:
        c.wait()


def solution(mesh):
    nx, ny = mesh.shape["gx"], mesh.shape["gy"]
    n = nx * ny

    def per_device(adjoint, conduct_x, conduct_y, pick_weights, owner_order):
        cx, cy, cols = adjoint.shape
        picks = pick_weights.shape[0]
        groups = cols // LANES
        chunks = cols // CHUNK
        ex = cx + 2 * STEPS
        tile = picks // n * groups
        kf = -(-ex * 2 * SUB // LANES) * LANES
        vmem = pl.BlockSpec(memory_space=pltpu.VMEM)
        hbm = pl.BlockSpec(memory_space=pl.ANY)
        dma = pltpu.SemaphoreType.DMA
        span = 2 * STEPS + 4
        field, owned = pl.pallas_call(
            functools.partial(kernel, nx, ny),
            out_shape=(
                pltpu.VMEM((cx, cy, cols), BF16),
                pltpu.VMEM((picks // n, cols), F32),
            ),
            in_specs=[hbm] * 5,
            out_specs=(vmem, vmem),
            scratch_shapes=[
                pltpu.VMEM((cx, cy, cols), BF16),
                pltpu.VMEM((2, STEPS, cy, cols), BF16),
                pltpu.VMEM((2, ex, SUB, cols), BF16),
                pltpu.VMEM((kf, cols), BF16),
                pltpu.VMEM((2, cx + 2 * SUB, 3 * LANES), F32),
                pltpu.VMEM((5 * len(NEAR), cx + 2 * SUB, LANES), F32),
                pltpu.VMEM((LANES * cx, LANES), F32),
                pltpu.VMEM((2 * STEPS + 1, LANES, LANES), BF16),
                pltpu.VMEM((2 * SUB, LANES), F32),
                pltpu.VMEM((cx * cy, span * LANES), BF16),
                pltpu.VMEM((cx * 2 * SUB, 2 * kf), BF16),
                pltpu.VMEM((cx * 4 * SUB, cols), F32),
                pltpu.VMEM((2 * STEPS * cy, cols), F32),
                pltpu.VMEM((1, picks), jnp.int32),
                pltpu.VMEM((picks, cx, cy), BF16),
                pltpu.VMEM((picks * cx, LANES), F32),
                pltpu.VMEM((picks, cx * cy), BF16),
                pltpu.VMEM((2, picks, STEPS * cy), BF16),
                pltpu.VMEM((picks * groups, LANES), F32),
                pltpu.VMEM((n - 1, tile, LANES), F32),
                dma,
                dma,
                dma,
                dma((2,)),
                dma((len(DIRS), chunks)),
                dma((len(DIRS), chunks)),
                dma((len(DIRS),)),
                dma((len(DIRS),)),
                dma((2,)),
                dma((2,)),
                dma,
                dma,
                pltpu.SemaphoreType.REGULAR((len(far_rounds(nx, ny)),)),
            ],
            compiler_params=pltpu.CompilerParams(
                collective_id=0, has_side_effects=True, vmem_limit_bytes=56 << 20
            ),
        )(adjoint, conduct_x, conduct_y, pick_weights, owner_order.reshape(1, picks))
        return pl.pallas_call(
            store_kernel,
            out_shape=(
                jax.ShapeDtypeStruct((cx, cy, cols), BF16),
                jax.ShapeDtypeStruct((picks // n, cols), F32),
            ),
            in_specs=[vmem, vmem],
            out_specs=(hbm, hbm),
            scratch_shapes=[dma((3,))],
        )(*[pltpu.with_memory_space_constraint(v, pltpu.VMEM) for v in (field, owned)])

    return jax.shard_map(
        per_device,
        mesh=mesh,
        in_specs=(P("gx", "gy", None), P("gx", "gy"), P("gx", "gy"), P(None, "gx", "gy"), P()),
        out_specs=(P("gx", "gy", None), P(("gx", "gy"), None)),
        check_vma=False,
    )
```

```python
import functools

import jax
import jax.numpy as jnp
from jax import lax
from jax.experimental import pallas as pl
from jax.experimental.pallas import tpu as pltpu
from jax.sharding import PartitionSpec as P

STEPS = 4
LANES = 128
SUB = 8
CHUNK = 256
MESH = pl.DeviceIdType.MESH
DIRS = ((0, 1), (0, -1), (1, 1), (1, -1), (-1, 1), (-1, -1), (1, 0), (-1, 0))
F32 = jnp.float32
BF16 = jnp.bfloat16
NEAR = [(a, b) for a in range(-2, 3) for b in range(-2, 3) if abs(a) + abs(b) <= 2]
FAR = [(a, b) for a in range(-4, 5) for b in range(-4, 5) if abs(a) + abs(b) <= 4]


def dir_id(dx, dy):
    return DIRS.index((dx, dy))


def centre(dx):
    return SUB if dx == -STEPS else 2 * SUB * (dx + STEPS - 1)


def turn(dx):
    return 2 * SUB if dx == -STEPS else centre(dx)


def turned(dx, get):
    by = turn(dx)
    return [get(LANES - by, LANES), get(0, LANES - by)] if by else [get(0, LANES)]


def far_rounds(nx, ny):
    result = []
    for size, axis in ((nx, 0), (ny, 1)):
        reach = 1
        while reach < size - 1:
            result.append([(d, 0) if axis == 0 else (0, d) for d in (reach, -reach)])
            reach *= 2
    return result


def kernel(
    nx, ny, adj, kx_hbm, ky_hbm, w_hbm, order_hbm, out, rep,
    ub, xh, yb, y_rows, kk, shifted, coef, masks, ends, band, fringe, acc,
    order_ref, wv, w32, wt, w_halo, w_rim, spread, ps, rbuf,
    own_sem, w_sem, order_sem, k_load, a_send, a_recv, k_send, k_recv, w_send, w_recv, r_send, r_recv, known,
):
    cx, cy, cols = adj.shape
    groups = cols // LANES
    chunks = cols // CHUNK
    ex = cx + 2 * STEPS
    picks = w_hbm.shape[0]
    n = nx * ny
    tile = ps.shape[0] // n
    kf = y_rows.shape[0]
    span = 2 * STEPS + 4
    gx = lax.axis_index("gx")
    gy = lax.axis_index("gy")
    me = gx * ny + gy

    def around(i, j):
        tx, ty = gx + i, gy + j
        return jnp.where(tx >= nx, tx - nx, tx), jnp.where(ty >= ny, ty - ny, ty)

    def present(dx, dy):
        ok = None
        for d, g, size in ((dx, gx, nx), (dy, gy, ny)):
            if d == 0:
                continue
            c = g < size - d if d > 0 else g >= -d
            ok = c if ok is None else jnp.logical_and(ok, c)
        return ok

    own_rows, own_lanes = pl.ds(SUB, cx), pl.ds(LANES, LANES)
    k_loads = [
        pltpu.make_async_copy(src, kk.at[a, own_rows, own_lanes], k_load.at[a])
        for a, src in enumerate((kx_hbm, ky_hbm))
    ]
    for c in k_loads:
        c.start()

    barrier = pltpu.get_barrier_semaphore()
    rounds = far_rounds(nx, ny)

    def greet(semaphore, dx, dy):
        @pl.when(present(dx, dy))
        def _():
            pl.semaphore_signal(
                semaphore, inc=1, device_id=(gx + dx, gy + dy), device_id_type=MESH
            )

    def number(peers):
        return functools.reduce(jnp.add, [jnp.where(present(*d), 1, 0) for d in peers])

    for d in DIRS:
        greet(barrier, *d)

    def hear(i):
        pl.semaphore_wait(known.at[i], number(rounds[i]))

    def tell(i):
        for d in rounds[i]:
            greet(known.at[i], *d)

    own = pltpu.make_async_copy(adj, ub, own_sem)
    w_load = pltpu.make_async_copy(w_hbm, wv, w_sem)
    order_load = pltpu.make_async_copy(order_hbm, order_ref, order_sem)
    for c in [w_load, order_load, own]:
        c.start()

    def k_region(sx, sy):
        rows = {-1: pl.ds(0, SUB), 0: own_rows, 1: pl.ds(SUB + cx, SUB)}[sx]
        return kk.at[:, rows, pl.ds(LANES * (1 + sy), LANES)]

    def a_region(sx, sy):
        if sy == 0:
            return xh.at[0 if sx == -1 else 1]
        rows = {-1: pl.ds(1, STEPS - 1), 0: pl.ds(STEPS, cx), 1: pl.ds(STEPS + cx, STEPS - 1)}[sx]
        return yb.at[0 if sy == 1 else 1, rows]

    def k_copy(dx, dy):
        rows = {1: pl.ds(cx, SUB), 0: own_rows, -1: pl.ds(SUB, SUB)}[dx]
        return pltpu.make_async_remote_copy(
            src_ref=kk.at[:, rows, own_lanes], dst_ref=k_region(-dx, -dy),
            send_sem=k_send.at[dir_id(dx, dy)], recv_sem=k_recv.at[dir_id(-dx, -dy)],
            device_id=(gx + dx, gy + dy), device_id_type=MESH,
        )

    def a_copies(dx, dy):
        slot, mine = dir_id(-dx, -dy), dir_id(dx, dy)
        src = adj
        if dx:
            count = STEPS - 1 if dy else STEPS
            src = src.at[pl.ds(cx - count if dx == 1 else 0, count)]
        if dy:
            src = src.at[:, pl.ds(cy - SUB if dy == 1 else 0, SUB)]
        dst = a_region(-dx, -dy)
        parts = [(src, dst)]
        if dy == 0:
            cut = [pl.ds(q * CHUNK, CHUNK) for q in range(chunks)]
            parts = [(src.at[:, :, c], dst.at[:, :, c]) for c in cut]
        return [
            pltpu.make_async_remote_copy(
                src_ref=s, dst_ref=d, send_sem=a_send.at[mine, q],
                recv_sem=a_recv.at[slot, q], device_id=(gx + dx, gy + dy),
                device_id_type=MESH,
            )
            for q, (s, d) in enumerate(parts)
        ]

    for e in (0, ex - 1):
        yb[:, e] = jnp.zeros((2, SUB, cols), BF16)
    for dx, dy in DIRS:
        @pl.when(jnp.logical_not(present(dx, dy)))
        def _(dx=dx, dy=dy):
            k_part, a_part = k_region(dx, dy), a_region(dx, dy)
            k_part[...] = jnp.zeros(k_part.shape, F32)
            a_part[...] = jnp.zeros(a_part.shape, BF16)

    for c in k_loads:
        c.wait()
    pl.semaphore_wait(barrier, number(DIRS))

    for dx, dy in DIRS:
        @pl.when(present(dx, dy))
        def _(dx=dx, dy=dy):
            k_copy(dx, dy).start()

    for dx, dy in DIRS[:6]:
        @pl.when(present(dx, dy))
        def _(dx=dx, dy=dy):
            for c in a_copies(dx, dy):
                c.start()

    told = [0]

    def next_round():
        i = told[0]
        hear(i)
        if i + 1 < len(rounds):
            tell(i + 1)
        told[0] = i + 1

    tell(0)

    def wait_k(dx, dy):
        @pl.when(present(dx, dy))
        def _():
            part = k_region(dx, dy)
            pltpu.make_async_copy(part, part, k_recv.at[dir_id(dx, dy)]).wait()

    def wait_a(dx, dy, q=0):
        @pl.when(present(dx, dy))
        def _():
            part = a_region(dx, dy)
            if dy == 0:
                part = part.at[:, :, pl.ds(q * CHUNK, CHUNK)]
            pltpu.make_async_copy(part, part, a_recv.at[dir_id(dx, dy), q]).wait()

    def w_copy(dx):
        lo = (cx - STEPS) * LANES if dx == 1 else 0
        slot, mine = (0, 1) if dx == 1 else (1, 0)
        return pltpu.make_async_remote_copy(
            src_ref=wt.at[:, pl.ds(lo, STEPS * LANES)], dst_ref=w_halo.at[slot],
            send_sem=w_send.at[mine], recv_sem=w_recv.at[slot],
            device_id=(gx + dx, gy), device_id_type=MESH,
        )

    w_load.wait()
    order_load.wait()
    pick_ids = lax.broadcasted_iota(jnp.int32, (picks, picks), 0)
    chosen = jnp.where(pick_ids == order_ref[...], F32(1), F32(0)).astype(BF16)
    some = w32.shape[0] // cx
    for b in range(0, picks, some):
        w32[...] = wv[b : b + some].astype(F32).reshape(some * cx, LANES)
        for x in range(cx):
            row = w32[pl.ds(x, some, stride=cx), :]
            wt[b : b + some, x * LANES : (x + 1) * LANES] = row.astype(BF16)
    for x in range(cx):
        at_x = slice(x * LANES, (x + 1) * LANES)
        row = lax.dot_general(
            chosen, wt[:, at_x], (((0,), (0,)), ((), ())), preferred_element_type=F32
        )
        wt[:, at_x] = row.astype(BF16)

    for dx in (1, -1):
        @pl.when(present(dx, 0))
        def _(dx=dx):
            w_copy(dx).start()

        @pl.when(jnp.logical_not(present(dx, 0)))
        def _(dx=dx):
            part = w_halo.at[1 if dx == 1 else 0]
            part[...] = jnp.zeros(part.shape, BF16)

    pick_lane = lax.broadcasted_iota(jnp.int32, (picks, LANES), 1)
    rim = []
    for x in range(cx):
        first = x * 2 * SUB % LANES
        row = wt[:, x * LANES : (x + 1) * LANES].astype(F32)
        row = pltpu.roll(row, (first + SUB) % LANES, 1)
        inside = (pick_lane >= first) & (pick_lane < first + 2 * SUB)
        mine = jnp.where(inside, row, F32(0))
        if first == 0:
            rim.append(mine)
        else:
            rim[-1] = rim[-1] + mine
    for i, value in enumerate(rim):
        w_rim[:, i * LANES : (i + 1) * LANES] = value.astype(BF16)
    coef[...] = jnp.zeros(coef.shape, F32)
    if kf > ex * 2 * SUB:
        y_rows[ex * 2 * SUB :, :] = jnp.zeros((kf - ex * 2 * SUB, cols), BF16)
    lane = lax.broadcasted_iota(jnp.int32, (LANES, LANES), 1)
    cell = lax.broadcasted_iota(jnp.int32, (LANES, LANES), 0)
    for dx in range(-STEPS, STEPS + 1):
        gap = ((lane - turn(dx)) & (LANES - 1)) - cell
        inside = jnp.abs(gap) <= STEPS - abs(dx)
        masks[dx + STEPS] = jnp.where(inside, F32(1), F32(0)).astype(BF16)
    lane, cell = lane[:SUB], cell[:SUB]
    before = after = jnp.zeros((SUB, LANES), F32)
    for dx in range(1 - STEPS, STEPS):
        reach = STEPS - abs(dx)
        place = ((lane - centre(dx) + LANES // 2) & (LANES - 1)) - LANES // 2
        left = (place < 0) & (place >= -STEPS) & (cell - place <= reach)
        right = (place >= 0) & (place < STEPS) & (place + SUB - cell <= reach)
        before = jnp.where(left, F32(1), before)
        after = jnp.where(right, F32(1), after)
    ends[:SUB], ends[SUB:] = after, before

    for d in DIRS:
        wait_k(*d)
    for q in range(chunks):
        for dx, dy in DIRS[6:]:
            @pl.when(present(dx, dy))
            def _(dx=dx, dy=dy, q=q):
                a_copies(dx, dy)[q].start()

    next_round()

    near_end = lax.broadcasted_iota(jnp.int32, (cx + 2 * SUB, LANES), 1) < LANES // 2

    def folded(k):
        past = jnp.where(near_end, k[:, 2 * LANES :], k[:, :LANES])
        return jnp.concatenate([k[:, LANES : 2 * LANES], past], axis=1)

    kx, ky = folded(kk[0]), folded(kk[1])
    kx_at = lax.broadcasted_iota(jnp.int32, kx.shape, 0)
    ky_at = lax.broadcasted_iota(jnp.int32, ky.shape, 1)
    kx = jnp.where(jnp.logical_and(kx_at == SUB + cx - 1, gx == nx - 1), F32(0), kx)
    ky = jnp.where(jnp.logical_and(ky_at == LANES - 1, gy == ny - 1), F32(0), ky)
    high, wide = kx.shape

    def at(value, dx, dy):
        if dx:
            value = pltpu.roll(value, -dx % high, 0)
        if dy:
            value = pltpu.roll(value, -dy % wide, 1)
        return value

    xp, yp = kx, ky
    xm, ym = at(kx, -1, 0), at(ky, 0, -1)
    c = F32(1) - ((xm + xp) + (ym + yp))
    two = {
        (0, 0): c * c + ((xm * xm + xp * xp) + (ym * ym + yp * yp)),
        (1, 0): xp * (c + at(c, 1, 0)),
        (-1, 0): xm * (c + at(c, -1, 0)),
        (0, 1): yp * (c + at(c, 0, 1)),
        (0, -1): ym * (c + at(c, 0, -1)),
        (2, 0): xp * at(xp, 1, 0),
        (-2, 0): xm * at(xm, -1, 0),
        (0, 2): yp * at(yp, 0, 1),
        (0, -2): ym * at(ym, 0, -1),
        (1, 1): xp * at(yp, 1, 0) + yp * at(xp, 0, 1),
        (1, -1): xp * at(ym, 1, 0) + ym * at(xp, 0, -1),
        (-1, 1): xm * at(yp, -1, 0) + yp * at(xm, 0, 1),
        (-1, -1): xm * at(ym, -1, 0) + ym * at(xm, 0, -1),
    }
    for i, d in enumerate(NEAR):
        for dy in range(-2, 3):
            shifted[(dy + 2) * len(NEAR) + i] = at(two[d], 0, dy)[:, :LANES]

    def near(d, dx, dy):
        return shifted[(dy + 2) * len(NEAR) + NEAR.index(d), SUB + dx : SUB + dx + cx]

    for fx, fy in FAR:
        total = None
        for dx, dy in NEAR:
            rest = (fx - dx, fy - dy)
            if rest in NEAR:
                term = near((dx, dy), 0, 0) * near(rest, dx, dy)
                total = term if total is None else total + term
        slot = (centre(fx) + fy) % LANES
        coef[slot * cx : (slot + 1) * cx, :] = total

    def low_part(value):
        high_part = value.astype(BF16)
        return high_part, (value - high_part.astype(F32)).astype(BF16)

    def build(x):
        table = pltpu.roll(
            coef[pl.ds(x, LANES, stride=cx), :].T, 0, 1, stride=1, stride_axis=0
        )
        rows = pl.ds(pl.multiple_of(x * LANES, LANES), LANES)
        big, small = low_part(table)
        for dx in range(-STEPS, STEPS + 1):
            r = dx + STEPS
            source = big
            if dx == -STEPS:
                source = pltpu.roll(table, SUB, 1).astype(BF16)
            band[rows, r * LANES : (r + 1) * LANES] = source * masks[r]
            if abs(dx) <= 1:
                k = 2 * STEPS + 2 + dx
                band[rows, k * LANES : (k + 1) * LANES] = small * masks[r]
        edge = jnp.concatenate([table[cy - SUB :], table[:SUB]], axis=0) * ends[...]
        edge = pltpu.roll(edge, SUB, 1)
        edge = jnp.concatenate([edge] + [jnp.zeros_like(edge)] * (kf // LANES - 1), axis=1)
        big, small = low_part(pltpu.roll(edge, (x + 1) * 2 * SUB, 1))
        rows = pl.ds(pl.multiple_of(x * 2 * SUB, 2 * SUB), 2 * SUB)
        fringe[rows, :kf] = big
        fringe[rows, kf:] = small

    def fill_fringe():
        for e in range(ex):
            pair = jnp.concatenate([yb[1, e].astype(F32), yb[0, e].astype(F32)], axis=0)
            y_rows[e * 2 * SUB : (e + 1) * 2 * SUB, :] = pair.astype(BF16)

    def band_dot(x, blocks, field):
        rows = slice(x * LANES, (x + 1) * LANES)
        left = [band[rows, lo * LANES : hi * LANES] for lo, hi in blocks]
        return jnp.dot(
            left[0] if len(left) == 1 else jnp.concatenate(left, axis=1),
            field[0] if len(field) == 1 else jnp.concatenate(field, axis=0),
            preferred_element_type=F32,
        )

    def own_dot(x):
        blocks, field = [], []
        for reach, base in ((STEPS, STEPS), (1, 2 * STEPS + 2)):
            lo, hi = max(x - reach, 0), min(x + reach, cx - 1) + 1
            blocks.append((lo - x + base, hi - x + base))
            for r in range(lo, hi):
                field += turned(r - x, lambda a, b, r=r: ub[r, a:b])
        if blocks[0][1] == blocks[1][0]:
            blocks = [(blocks[0][0], blocks[1][1])]
        return band_dot(x, blocks, field)

    @pl.loop(0, cx // 4)
    def _(p):
        for i in range(4):
            build(4 * p + i)

    inner = range(STEPS, cx - STEPS)
    outer = list(range(STEPS)) + list(range(cx - STEPS, cx))
    next_round()

    for dx in (1, -1):
        @pl.when(present(dx, 0))
        def _(dx=dx):
            part = w_halo.at[1 if dx == 1 else 0]
            pltpu.make_async_copy(part, part, w_recv.at[1 if dx == 1 else 0]).wait()

    next_round()

    def weights(r):
        if r < 0:
            return w_halo[0, :, (r + STEPS) * LANES : (r + STEPS + 1) * LANES]
        if r >= cx:
            return w_halo[1, :, (r - cx) * LANES : (r - cx + 1) * LANES]
        return wt[:, r * LANES : (r + 1) * LANES]

    for x in range(cx):
        left = []
        for dx in range(-STEPS, STEPS + 1):
            w = weights(x + dx)
            if turn(dx):
                w = pltpu.roll(w.astype(F32), turn(dx), 1).astype(BF16)
            left.append(w)
        value = lax.dot_general(
            jnp.concatenate(left + left[STEPS - 1 : STEPS + 2], axis=1),
            band[x * LANES : (x + 1) * LANES, :],
            (((1,), (1,)), ((), ())),
            preferred_element_type=F32,
        )
        big, small = low_part(value)
        spread[:picks, x * LANES : (x + 1) * LANES] = big
        spread[picks:, x * LANES : (x + 1) * LANES] = small

    own.wait()
    total = jnp.dot(
        spread[...], ub[...].reshape(cx * cy, cols), preferred_element_type=F32
    )
    total = total[:picks] + total[picks:]

    for d in DIRS[:6]:
        wait_a(*d)
    fill_fringe()
    y = y_rows[...]
    side = jnp.dot(fringe[:, :kf], y, preferred_element_type=F32)
    side = side + jnp.dot(fringe[:, kf:], y, preferred_element_type=F32)
    total = total + jnp.dot(w_rim[...], side.astype(BF16), preferred_element_type=F32)
    for g in range(groups):
        ps[pl.ds(g, picks, stride=groups), :] = total[:, g * LANES : (g + 1) * LANES]

    def halo_blocks(x):
        result = []
        for reach, base in ((STEPS, STEPS), (1, 2 * STEPS + 2)):
            if x < STEPS:
                lo, hi, source, shift = x - reach, 0, 0, STEPS
            else:
                lo, hi, source, shift = cx, x + reach + 1, 1, -cx
            if lo < hi:
                result.append((lo, hi, base, source, shift))
        return result

    def halo_dot(x, part):
        blocks, field = [], []
        for lo, hi, base, source, shift in halo_blocks(x):
            blocks.append((lo - x + base, hi - x + base))
            for r in range(lo, hi):
                field += turned(r - x, lambda a, b, r=r: xh[source, r + shift, a:b, part])
        return band_dot(x, blocks, field)

    def reduce_copy(k, tx, ty):
        return pltpu.make_async_remote_copy(
            src_ref=ps.at[pl.ds(pl.multiple_of((tx * ny + ty) * tile, tile), tile)],
            dst_ref=rbuf.at[k - 1], send_sem=r_send, recv_sem=r_recv,
            device_id=(tx, ty), device_id_type=MESH,
        )

    while told[0] < len(rounds):
        next_round()

    near = nx // 4
    for lo, hi in ((near, nx - near + 1), (1, near), (nx - near + 1, nx)):
        @pl.loop(lo, hi)
        def _(i):
            for j in range(ny):
                reduce_copy(i * ny + j, *around(i, j)).start()

    for j in range(1, ny):
        reduce_copy(j, *around(0, j)).start()

    def with_side(x):
        value = own_dot(x)
        bottom, top = (side[(2 * x + i) * SUB : (2 * x + i + 1) * SUB] for i in range(2))
        return jnp.concatenate(
            [value[:SUB] + top, value[SUB : cy - SUB], value[cy - SUB :] + bottom], axis=0
        )

    for x in inner:
        out[x] = with_side(x).astype(BF16)
    for j, x in enumerate(outer):
        acc[j * LANES : (j + 1) * LANES, :] = with_side(x)

    for q in range(chunks):
        part = slice(q * CHUNK, (q + 1) * CHUNK)
        for d in DIRS[6:]:
            wait_a(*d, q)
        for j, x in enumerate(outer):
            value = acc[j * LANES : (j + 1) * LANES, part] + halo_dot(x, part)
            out[x, :, part] = value.astype(BF16)

    for dx in (1, -1):
        @pl.when(present(dx, 0))
        def _(dx=dx):
            w_copy(dx).wait_send()

    for dx, dy in DIRS:
        @pl.when(present(dx, dy))
        def _(dx=dx, dy=dy):
            k_copy(dx, dy).wait_send()
            for c in a_copies(dx, dy):
                c.wait_send()

    pltpu.make_async_copy(rbuf, rbuf, r_recv).wait()
    pltpu.make_async_copy(rbuf, rbuf, r_send).wait()

    total = ps[pl.ds(pl.multiple_of(me * tile, tile), tile), :]
    total = total + jnp.sum(rbuf[...], axis=0)
    for r in range(tile // groups):
        for q in range(groups):
            rep[r : r + 1, q * LANES : (q + 1) * LANES] = total[
                r * groups + q : r * groups + q + 1
            ]


def store_kernel(field, owned, field_out, owned_out, sems):
    parts = sems.shape[0] - 1
    rows = field.shape[0] // parts
    copies = [pltpu.make_async_copy(owned, owned_out, sems.at[parts])]
    for p in range(parts):
        part = pl.ds(p * rows, rows)
        copies.append(pltpu.make_async_copy(field.at[part], field_out.at[part], sems.at[p]))
    for c in copies:
        c.start()
    for c in copies:
        c.wait()


def solution(mesh):
    nx, ny = mesh.shape["gx"], mesh.shape["gy"]
    n = nx * ny

    def per_device(adjoint, conduct_x, conduct_y, pick_weights, owner_order):
        cx, cy, cols = adjoint.shape
        picks = pick_weights.shape[0]
        groups = cols // LANES
        chunks = cols // CHUNK
        ex = cx + 2 * STEPS
        tile = picks // n * groups
        kf = -(-ex * 2 * SUB // LANES) * LANES
        vmem = pl.BlockSpec(memory_space=pltpu.VMEM)
        hbm = pl.BlockSpec(memory_space=pl.ANY)
        dma = pltpu.SemaphoreType.DMA
        span = 2 * STEPS + 4
        field, owned = pl.pallas_call(
            functools.partial(kernel, nx, ny),
            out_shape=(
                pltpu.VMEM((cx, cy, cols), BF16),
                pltpu.VMEM((picks // n, cols), F32),
            ),
            in_specs=[hbm] * 5,
            out_specs=(vmem, vmem),
            scratch_shapes=[
                pltpu.VMEM((cx, cy, cols), BF16),
                pltpu.VMEM((2, STEPS, cy, cols), BF16),
                pltpu.VMEM((2, ex, SUB, cols), BF16),
                pltpu.VMEM((kf, cols), BF16),
                pltpu.VMEM((2, cx + 2 * SUB, 3 * LANES), F32),
                pltpu.VMEM((5 * len(NEAR), cx + 2 * SUB, LANES), F32),
                pltpu.VMEM((LANES * cx, LANES), F32),
                pltpu.VMEM((2 * STEPS + 1, LANES, LANES), BF16),
                pltpu.VMEM((2 * SUB, LANES), F32),
                pltpu.VMEM((cx * cy, span * LANES), BF16),
                pltpu.VMEM((cx * 2 * SUB, 2 * kf), BF16),
                pltpu.VMEM((2 * STEPS * cy, cols), F32),
                pltpu.VMEM((1, picks), jnp.int32),
                pltpu.VMEM((picks, cx, cy), BF16),
                pltpu.VMEM((min(picks, LANES) * cx, LANES), F32),
                pltpu.VMEM((picks, cx * cy), BF16),
                pltpu.VMEM((2, picks, STEPS * cy), BF16),
                pltpu.VMEM((picks, -(-cx * 2 * SUB // LANES) * LANES), BF16),
                pltpu.VMEM((2 * picks, cx * cy), BF16),
                pltpu.VMEM((picks * groups, LANES), F32),
                pltpu.VMEM((n - 1, tile, LANES), F32),
                dma,
                dma,
                dma,
                dma((2,)),
                dma((len(DIRS), chunks)),
                dma((len(DIRS), chunks)),
                dma((len(DIRS),)),
                dma((len(DIRS),)),
                dma((2,)),
                dma((2,)),
                dma,
                dma,
                pltpu.SemaphoreType.REGULAR((len(far_rounds(nx, ny)),)),
            ],
            compiler_params=pltpu.CompilerParams(
                collective_id=0, has_side_effects=True, vmem_limit_bytes=56 << 20
            ),
        )(adjoint, conduct_x, conduct_y, pick_weights, owner_order.reshape(1, picks))
        return pl.pallas_call(
            store_kernel,
            out_shape=(
                jax.ShapeDtypeStruct((cx, cy, cols), BF16),
                jax.ShapeDtypeStruct((picks // n, cols), F32),
            ),
            in_specs=[vmem, vmem],
            out_specs=(hbm, hbm),
            scratch_shapes=[dma((3,))],
        )(*[pltpu.with_memory_space_constraint(v, pltpu.VMEM) for v in (field, owned)])

    return jax.shard_map(
        per_device,
        mesh=mesh,
        in_specs=(P("gx", "gy", None), P("gx", "gy"), P("gx", "gy"), P(None, "gx", "gy"), P()),
        out_specs=(P("gx", "gy", None), P(("gx", "gy"), None)),
        check_vma=False,
    )
```

```python
import functools

import jax
import jax.numpy as jnp
from jax import lax
from jax.experimental import pallas as pl
from jax.experimental.pallas import tpu as pltpu
from jax.sharding import PartitionSpec as P

STEPS = 4
LANES = 128
SUB = 8
CHUNK = 256
MESH = pl.DeviceIdType.MESH
DIRS = ((0, 1), (0, -1), (1, 1), (1, -1), (-1, 1), (-1, -1), (1, 0), (-1, 0))
F32 = jnp.float32
BF16 = jnp.bfloat16
NEAR = [(a, b) for a in range(-2, 3) for b in range(-2, 3) if abs(a) + abs(b) <= 2]
FAR = [(a, b) for a in range(-4, 5) for b in range(-4, 5) if abs(a) + abs(b) <= 4]


def dir_id(dx, dy):
    return DIRS.index((dx, dy))


def centre(dx):
    return SUB if dx == -STEPS else 2 * SUB * (dx + STEPS - 1)


def turn(dx):
    return 2 * SUB if dx == -STEPS else centre(dx)


def turned(dx, get):
    by = turn(dx)
    return [get(LANES - by, LANES), get(0, LANES - by)] if by else [get(0, LANES)]


def far_rounds(nx, ny):
    result = []
    for size, axis in ((nx, 0), (ny, 1)):
        reach = 1
        while reach < size - 1:
            result.append([(d, 0) if axis == 0 else (0, d) for d in (reach, -reach)])
            reach *= 2
    return result


def kernel(
    nx, ny, adj, kx_hbm, ky_hbm, w_hbm, order_hbm, out, rep,
    ub, xh, yb, y_rows, kk, shifted, coef, masks, ends, band, fringe, cells, acc,
    order_ref, wv, w32, wt, w_halo, ps, rbuf,
    own_sem, w_sem, order_sem, k_load, a_send, a_recv, k_send, k_recv, w_send, w_recv, r_send, r_recv, known,
):
    cx, cy, cols = adj.shape
    groups = cols // LANES
    chunks = cols // CHUNK
    ex = cx + 2 * STEPS
    picks = w_hbm.shape[0]
    n = nx * ny
    tile = ps.shape[0] // n
    kf = y_rows.shape[0]
    span = 2 * STEPS + 4
    gx = lax.axis_index("gx")
    gy = lax.axis_index("gy")
    me = gx * ny + gy

    def around(i, j):
        tx, ty = gx + i, gy + j
        return jnp.where(tx >= nx, tx - nx, tx), jnp.where(ty >= ny, ty - ny, ty)

    def present(dx, dy):
        ok = None
        for d, g, size in ((dx, gx, nx), (dy, gy, ny)):
            if d == 0:
                continue
            c = g < size - d if d > 0 else g >= -d
            ok = c if ok is None else jnp.logical_and(ok, c)
        return ok

    own_rows, own_lanes = pl.ds(SUB, cx), pl.ds(LANES, LANES)
    k_loads = [
        pltpu.make_async_copy(src, kk.at[a, own_rows, own_lanes], k_load.at[a])
        for a, src in enumerate((kx_hbm, ky_hbm))
    ]
    for c in k_loads:
        c.start()

    barrier = pltpu.get_barrier_semaphore()
    rounds = far_rounds(nx, ny)

    def greet(semaphore, dx, dy):
        @pl.when(present(dx, dy))
        def _():
            pl.semaphore_signal(
                semaphore, inc=1, device_id=(gx + dx, gy + dy), device_id_type=MESH
            )

    def number(peers):
        return functools.reduce(jnp.add, [jnp.where(present(*d), 1, 0) for d in peers])

    for d in DIRS:
        greet(barrier, *d)

    def hear(i):
        pl.semaphore_wait(known.at[i], number(rounds[i]))

    def tell(i):
        for d in rounds[i]:
            greet(known.at[i], *d)

    own = pltpu.make_async_copy(adj, ub, own_sem)
    w_load = pltpu.make_async_copy(w_hbm, wv, w_sem)
    order_load = pltpu.make_async_copy(order_hbm, order_ref, order_sem)
    for c in [w_load, order_load, own]:
        c.start()

    def k_region(sx, sy):
        rows = {-1: pl.ds(0, SUB), 0: own_rows, 1: pl.ds(SUB + cx, SUB)}[sx]
        return kk.at[:, rows, pl.ds(LANES * (1 + sy), LANES)]

    def a_region(sx, sy):
        if sy == 0:
            return xh.at[0 if sx == -1 else 1]
        rows = {-1: pl.ds(1, STEPS - 1), 0: pl.ds(STEPS, cx), 1: pl.ds(STEPS + cx, STEPS - 1)}[sx]
        return yb.at[0 if sy == 1 else 1, rows]

    def k_copy(dx, dy):
        rows = {1: pl.ds(cx, SUB), 0: own_rows, -1: pl.ds(SUB, SUB)}[dx]
        return pltpu.make_async_remote_copy(
            src_ref=kk.at[:, rows, own_lanes], dst_ref=k_region(-dx, -dy),
            send_sem=k_send.at[dir_id(dx, dy)], recv_sem=k_recv.at[dir_id(-dx, -dy)],
            device_id=(gx + dx, gy + dy), device_id_type=MESH,
        )

    def a_copies(dx, dy):
        slot, mine = dir_id(-dx, -dy), dir_id(dx, dy)
        src = adj if dy else ub
        if dx:
            count = STEPS - 1 if dy else STEPS
            src = src.at[pl.ds(cx - count if dx == 1 else 0, count)]
        if dy:
            src = src.at[:, pl.ds(cy - SUB if dy == 1 else 0, SUB)]
        dst = a_region(-dx, -dy)
        parts = [(src, dst)]
        if dy == 0:
            cut = [pl.ds(q * CHUNK, CHUNK) for q in range(chunks)]
            parts = [(src.at[:, :, c], dst.at[:, :, c]) for c in cut]
        return [
            pltpu.make_async_remote_copy(
                src_ref=s, dst_ref=d, send_sem=a_send.at[mine, q],
                recv_sem=a_recv.at[slot, q], device_id=(gx + dx, gy + dy),
                device_id_type=MESH,
            )
            for q, (s, d) in enumerate(parts)
        ]

    for e in (0, ex - 1):
        yb[:, e] = jnp.zeros((2, SUB, cols), BF16)
    for dx, dy in DIRS:
        @pl.when(jnp.logical_not(present(dx, dy)))
        def _(dx=dx, dy=dy):
            k_part, a_part = k_region(dx, dy), a_region(dx, dy)
            k_part[...] = jnp.zeros(k_part.shape, F32)
            a_part[...] = jnp.zeros(a_part.shape, BF16)

    coef[...] = jnp.zeros(coef.shape, F32)
    if kf > ex * 2 * SUB:
        y_rows[ex * 2 * SUB :, :] = jnp.zeros((kf - ex * 2 * SUB, cols), BF16)
    lane = lax.broadcasted_iota(jnp.int32, (LANES, LANES), 1)
    cell = lax.broadcasted_iota(jnp.int32, (LANES, LANES), 0)
    for dx in range(-STEPS, STEPS + 1):
        gap = ((lane - turn(dx)) & (LANES - 1)) - cell
        inside = jnp.abs(gap) <= STEPS - abs(dx)
        masks[dx + STEPS] = jnp.where(inside, F32(1), F32(0)).astype(BF16)
    lane, cell = lane[:SUB], cell[:SUB]
    before = after = jnp.zeros((SUB, LANES), F32)
    for dx in range(1 - STEPS, STEPS):
        reach = STEPS - abs(dx)
        place = ((lane - centre(dx) + LANES // 2) & (LANES - 1)) - LANES // 2
        left = (place < 0) & (place >= -STEPS) & (cell - place <= reach)
        right = (place >= 0) & (place < STEPS) & (place + SUB - cell <= reach)
        before = jnp.where(left, F32(1), before)
        after = jnp.where(right, F32(1), after)
    ends[:SUB], ends[SUB:] = before, after

    for c in k_loads:
        c.wait()
    pl.semaphore_wait(barrier, number(DIRS))

    for dx, dy in DIRS:
        @pl.when(present(dx, dy))
        def _(dx=dx, dy=dy):
            k_copy(dx, dy).start()

    for dx, dy in DIRS[:6]:
        @pl.when(present(dx, dy))
        def _(dx=dx, dy=dy):
            for c in a_copies(dx, dy):
                c.start()

    told = [0]

    def next_round():
        i = told[0]
        hear(i)
        if i + 1 < len(rounds):
            tell(i + 1)
        told[0] = i + 1

    tell(0)

    def wait_k(dx, dy):
        @pl.when(present(dx, dy))
        def _():
            part = k_region(dx, dy)
            pltpu.make_async_copy(part, part, k_recv.at[dir_id(dx, dy)]).wait()

    def wait_a(dx, dy, q=0):
        @pl.when(present(dx, dy))
        def _():
            part = a_region(dx, dy)
            if dy == 0:
                part = part.at[:, :, pl.ds(q * CHUNK, CHUNK)]
            pltpu.make_async_copy(part, part, a_recv.at[dir_id(dx, dy), q]).wait()

    def w_copy(dx):
        lo = (cx - STEPS) * LANES if dx == 1 else 0
        slot, mine = (0, 1) if dx == 1 else (1, 0)
        return pltpu.make_async_remote_copy(
            src_ref=wt.at[:, pl.ds(lo, STEPS * LANES)], dst_ref=w_halo.at[slot],
            send_sem=w_send.at[mine], recv_sem=w_recv.at[slot],
            device_id=(gx + dx, gy), device_id_type=MESH,
        )

    w_load.wait()
    order_load.wait()
    pick_ids = lax.broadcasted_iota(jnp.int32, (picks, picks), 0)
    chosen = jnp.where(pick_ids == order_ref[...], F32(1), F32(0)).astype(BF16)
    w32[...] = wv[...].astype(F32).reshape(picks * cx, LANES)
    for x in range(cx):
        row = w32[pl.ds(x, picks, stride=cx), :].astype(BF16)
        row = lax.dot_general(
            chosen, row, (((0,), (0,)), ((), ())), preferred_element_type=F32
        )
        wt[:, x * LANES : (x + 1) * LANES] = row.astype(BF16)

    for dx in (1, -1):
        @pl.when(present(dx, 0))
        def _(dx=dx):
            w_copy(dx).start()

        @pl.when(jnp.logical_not(present(dx, 0)))
        def _(dx=dx):
            part = w_halo.at[1 if dx == 1 else 0]
            part[...] = jnp.zeros(part.shape, BF16)

    for d in DIRS:
        wait_k(*d)
    own.wait()
    for q in range(chunks):
        for dx, dy in DIRS[6:]:
            @pl.when(present(dx, dy))
            def _(dx=dx, dy=dy, q=q):
                a_copies(dx, dy)[q].start()

    next_round()

    near_end = lax.broadcasted_iota(jnp.int32, (cx + 2 * SUB, LANES), 1) < LANES // 2

    def folded(k):
        past = jnp.where(near_end, k[:, 2 * LANES :], k[:, :LANES])
        return jnp.concatenate([k[:, LANES : 2 * LANES], past], axis=1)

    kx, ky = folded(kk[0]), folded(kk[1])
    kx_at = lax.broadcasted_iota(jnp.int32, kx.shape, 0)
    ky_at = lax.broadcasted_iota(jnp.int32, ky.shape, 1)
    kx = jnp.where(jnp.logical_and(kx_at == SUB + cx - 1, gx == nx - 1), F32(0), kx)
    ky = jnp.where(jnp.logical_and(ky_at == LANES - 1, gy == ny - 1), F32(0), ky)
    high, wide = kx.shape

    def at(value, dx, dy):
        if dx:
            value = pltpu.roll(value, -dx % high, 0)
        if dy:
            value = pltpu.roll(value, -dy % wide, 1)
        return value

    xp, yp = kx, ky
    xm, ym = at(kx, -1, 0), at(ky, 0, -1)
    c = F32(1) - ((xm + xp) + (ym + yp))
    two = {
        (0, 0): c * c + ((xm * xm + xp * xp) + (ym * ym + yp * yp)),
        (1, 0): xp * (c + at(c, 1, 0)),
        (-1, 0): xm * (c + at(c, -1, 0)),
        (0, 1): yp * (c + at(c, 0, 1)),
        (0, -1): ym * (c + at(c, 0, -1)),
        (2, 0): xp * at(xp, 1, 0),
        (-2, 0): xm * at(xm, -1, 0),
        (0, 2): yp * at(yp, 0, 1),
        (0, -2): ym * at(ym, 0, -1),
        (1, 1): xp * at(yp, 1, 0) + yp * at(xp, 0, 1),
        (1, -1): xp * at(ym, 1, 0) + ym * at(xp, 0, -1),
        (-1, 1): xm * at(yp, -1, 0) + yp * at(xm, 0, 1),
        (-1, -1): xm * at(ym, -1, 0) + ym * at(xm, 0, -1),
    }
    for i, d in enumerate(NEAR):
        for dy in range(-2, 3):
            shifted[(dy + 2) * len(NEAR) + i] = at(two[d], 0, dy)[:, :LANES]

    def near(d, dx, dy):
        return shifted[(dy + 2) * len(NEAR) + NEAR.index(d), SUB + dx : SUB + dx + cx]

    for fx, fy in FAR:
        total = None
        for dx, dy in NEAR:
            rest = (fx - dx, fy - dy)
            if rest in NEAR:
                term = near((dx, dy), 0, 0) * near(rest, dx, dy)
                total = term if total is None else total + term
        slot = (centre(fx) + fy) % LANES
        coef[slot * cx : (slot + 1) * cx, :] = total

    def low_part(value):
        high_part = value.astype(BF16)
        return high_part, (value - high_part.astype(F32)).astype(BF16)

    def build(x):
        table = pltpu.roll(
            coef[pl.ds(x, LANES, stride=cx), :].T, 0, 1, stride=1, stride_axis=0
        )
        rows = pl.ds(pl.multiple_of(x * LANES, LANES), LANES)
        big, small = low_part(table)
        for dx in range(-STEPS, STEPS + 1):
            r = dx + STEPS
            source = big
            if dx == -STEPS:
                source = pltpu.roll(table, SUB, 1).astype(BF16)
            band[rows, r * LANES : (r + 1) * LANES] = source * masks[r]
            if abs(dx) <= 1:
                k = 2 * STEPS + 2 + dx
                band[rows, k * LANES : (k + 1) * LANES] = small * masks[r]
        edge = jnp.concatenate([table[:SUB], table[cy - SUB :]], axis=0) * ends[...]
        edge = pltpu.roll(edge, SUB, 1)
        edge = jnp.concatenate([edge] + [jnp.zeros_like(edge)] * (kf // LANES - 1), axis=1)
        big, small = low_part(pltpu.roll(edge, (x + 1) * 2 * SUB, 1))
        rows = pl.ds(pl.multiple_of(x * 2 * SUB, 2 * SUB), 2 * SUB)
        fringe[rows, :kf] = big
        fringe[rows, kf:] = small

    def fill_fringe():
        for e in range(ex):
            pair = jnp.concatenate([yb[1, e].astype(F32), yb[0, e].astype(F32)], axis=0)
            y_rows[e * 2 * SUB : (e + 1) * 2 * SUB, :] = pair.astype(BF16)

    def band_dot(x, blocks, field):
        rows = slice(x * LANES, (x + 1) * LANES)
        left = [band[rows, lo * LANES : hi * LANES] for lo, hi in blocks]
        return jnp.dot(
            left[0] if len(left) == 1 else jnp.concatenate(left, axis=1),
            field[0] if len(field) == 1 else jnp.concatenate(field, axis=0),
            preferred_element_type=F32,
        )

    def own_dot(x):
        blocks, field = [], []
        for reach, base in ((STEPS, STEPS), (1, 2 * STEPS + 2)):
            lo, hi = max(x - reach, 0), min(x + reach, cx - 1) + 1
            blocks.append((lo - x + base, hi - x + base))
            for r in range(lo, hi):
                field += turned(r - x, lambda a, b, r=r: ub[r, a:b])
        if blocks[0][1] == blocks[1][0]:
            blocks = [(blocks[0][0], blocks[1][1])]
        return band_dot(x, blocks, field)

    @pl.loop(0, cx // 4)
    def _(p):
        for i in range(4):
            build(4 * p + i)

    inner = range(STEPS, cx - STEPS)
    outer = list(range(STEPS)) + list(range(cx - STEPS, cx))
    edge_rows = 2 * SUB
    next_round()
    for x in inner:
        value = own_dot(x)
        out[x] = value.astype(BF16)
        base = x * 2 * edge_rows
        cells[base : base + edge_rows, :] = value[:edge_rows]
        cells[base + edge_rows : base + 2 * edge_rows, :] = value[cy - edge_rows :]
    for j, x in enumerate(outer):
        acc[j * LANES : (j + 1) * LANES, :] = own_dot(x)

    for d in DIRS[:6]:
        wait_a(*d)
    next_round()
    fill_fringe()
    y = y_rows[...]
    side = jnp.dot(fringe[:, :kf], y, preferred_element_type=F32)
    side = side + jnp.dot(fringe[:, kf:], y, preferred_element_type=F32)
    for x in inner:
        base = x * 2 * edge_rows
        top = cells[base : base + edge_rows, :]
        bottom = cells[base + edge_rows : base + 2 * edge_rows, :]
        a, b = (side[(2 * x + i) * SUB : (2 * x + i + 1) * SUB] for i in range(2))
        top = jnp.concatenate([top[:SUB] + a, top[SUB:]], axis=0)
        bottom = jnp.concatenate([bottom[:SUB], bottom[SUB:] + b], axis=0)
        out[x, :edge_rows] = top.astype(BF16)
        out[x, cy - edge_rows :] = bottom.astype(BF16)
    for j, x in enumerate(outer):
        a, b = (side[(2 * x + i) * SUB : (2 * x + i + 1) * SUB] for i in range(2))
        acc[j * LANES : j * LANES + SUB, :] += a
        acc[(j + 1) * LANES - SUB : (j + 1) * LANES, :] += b

    for dx in (1, -1):
        @pl.when(present(dx, 0))
        def _(dx=dx):
            part = w_halo.at[1 if dx == 1 else 0]
            pltpu.make_async_copy(part, part, w_recv.at[1 if dx == 1 else 0]).wait()

    far = [
        [w_halo[side, :, h * LANES : (h + 1) * LANES].astype(F32) for h in range(STEPS)]
        for side in range(2)
    ]

    def spread(x):
        blocks, left = halo_blocks(x), []
        for lo, hi, base, source, shift in blocks:
            for r in range(lo, hi):
                w = far[source][r + shift]
                if turn(r - x):
                    w = pltpu.roll(w, turn(r - x), 1)
                left.append(w.astype(BF16))
        rows = slice(x * LANES, (x + 1) * LANES)
        right = [
            band[rows, (lo - x + base) * LANES : (hi - x + base) * LANES]
            for lo, hi, base, _, _ in blocks
        ]
        return lax.dot_general(
            jnp.concatenate(left, axis=1),
            right[0] if len(right) == 1 else jnp.concatenate(right, axis=1),
            (((1,), (1,)), ((), ())),
            preferred_element_type=F32,
        ).astype(BF16)

    def halo_blocks(x):
        result = []
        for reach, base in ((STEPS, STEPS), (1, 2 * STEPS + 2)):
            if x < STEPS:
                lo, hi, source, shift = x - reach, 0, 0, STEPS
            else:
                lo, hi, source, shift = cx, x + reach + 1, 1, -cx
            if lo < hi:
                result.append((lo, hi, base, source, shift))
        return result

    low, high_rows = STEPS * LANES, (cx - STEPS) * LANES
    total = jnp.dot(
        wt[:, low:high_rows],
        out[STEPS : cx - STEPS].reshape(high_rows - low, cols),
        preferred_element_type=F32,
    )
    total = total + jnp.dot(
        jnp.concatenate([wt[:, :low], wt[:, high_rows:]], axis=1),
        acc[...].astype(BF16),
        preferred_element_type=F32,
    )
    spread_rows = [spread(x) for x in outer]
    for side in range(2):
        total = total + jnp.dot(
            jnp.concatenate(spread_rows[side * STEPS : (side + 1) * STEPS], axis=1),
            ub[slice(0, STEPS) if side == 0 else slice(cx - STEPS, cx)].reshape(low, cols),
            preferred_element_type=F32,
        )
    for g in range(groups):
        ps[pl.ds(g, picks, stride=groups), :] = total[:, g * LANES : (g + 1) * LANES]

    def halo_dot(x, part):
        blocks, field = [], []
        for lo, hi, base, source, shift in halo_blocks(x):
            blocks.append((lo - x + base, hi - x + base))
            for r in range(lo, hi):
                field += turned(r - x, lambda a, b, r=r: xh[source, r + shift, a:b, part])
        return band_dot(x, blocks, field)

    def reduce_copy(k, tx, ty):
        return pltpu.make_async_remote_copy(
            src_ref=ps.at[pl.ds(pl.multiple_of((tx * ny + ty) * tile, tile), tile)],
            dst_ref=rbuf.at[k - 1], send_sem=r_send, recv_sem=r_recv,
            device_id=(tx, ty), device_id_type=MESH,
        )

    while told[0] < len(rounds):
        next_round()

    near = nx // 4
    for lo, hi in ((near, nx - near + 1), (1, near), (nx - near + 1, nx)):
        @pl.loop(lo, hi)
        def _(i):
            for j in range(ny):
                reduce_copy(i * ny + j, *around(i, j)).start()

    for j in range(1, ny):
        reduce_copy(j, *around(0, j)).start()

    for q in range(chunks):
        part = slice(q * CHUNK, (q + 1) * CHUNK)
        for d in DIRS[6:]:
            wait_a(*d, q)
        for j, x in enumerate(outer):
            value = acc[j * LANES : (j + 1) * LANES, part] + halo_dot(x, part)
            out[x, :, part] = value.astype(BF16)

    for dx in (1, -1):
        @pl.when(present(dx, 0))
        def _(dx=dx):
            w_copy(dx).wait_send()

    for dx, dy in DIRS:
        @pl.when(present(dx, dy))
        def _(dx=dx, dy=dy):
            k_copy(dx, dy).wait_send()
            for c in a_copies(dx, dy):
                c.wait_send()

    pltpu.make_async_copy(rbuf, rbuf, r_recv).wait()
    pltpu.make_async_copy(rbuf, rbuf, r_send).wait()

    total = ps[pl.ds(pl.multiple_of(me * tile, tile), tile), :]
    total = total + jnp.sum(rbuf[...], axis=0)
    for r in range(tile // groups):
        for q in range(groups):
            rep[r : r + 1, q * LANES : (q + 1) * LANES] = total[
                r * groups + q : r * groups + q + 1
            ]


def store_kernel(field, owned, field_out, owned_out, sems):
    parts = sems.shape[0] - 1
    rows = field.shape[0] // parts
    copies = [pltpu.make_async_copy(owned, owned_out, sems.at[parts])]
    for p in range(parts):
        part = pl.ds(p * rows, rows)
        copies.append(pltpu.make_async_copy(field.at[part], field_out.at[part], sems.at[p]))
    for c in copies:
        c.start()
    for c in copies:
        c.wait()


def solution(mesh):
    nx, ny = mesh.shape["gx"], mesh.shape["gy"]
    n = nx * ny

    def per_device(adjoint, conduct_x, conduct_y, pick_weights, owner_order):
        cx, cy, cols = adjoint.shape
        picks = pick_weights.shape[0]
        groups = cols // LANES
        chunks = cols // CHUNK
        ex = cx + 2 * STEPS
        tile = picks // n * groups
        kf = -(-ex * 2 * SUB // LANES) * LANES
        vmem = pl.BlockSpec(memory_space=pltpu.VMEM)
        hbm = pl.BlockSpec(memory_space=pl.ANY)
        dma = pltpu.SemaphoreType.DMA
        span = 2 * STEPS + 4
        field, owned = pl.pallas_call(
            functools.partial(kernel, nx, ny),
            out_shape=(
                pltpu.VMEM((cx, cy, cols), BF16),
                pltpu.VMEM((picks // n, cols), F32),
            ),
            in_specs=[hbm] * 5,
            out_specs=(vmem, vmem),
            scratch_shapes=[
                pltpu.VMEM((cx, cy, cols), BF16),
                pltpu.VMEM((2, STEPS, cy, cols), BF16),
                pltpu.VMEM((2, ex, SUB, cols), BF16),
                pltpu.VMEM((kf, cols), BF16),
                pltpu.VMEM((2, cx + 2 * SUB, 3 * LANES), F32),
                pltpu.VMEM((5 * len(NEAR), cx + 2 * SUB, LANES), F32),
                pltpu.VMEM((LANES * cx, LANES), F32),
                pltpu.VMEM((2 * STEPS + 1, LANES, LANES), BF16),
                pltpu.VMEM((2 * SUB, LANES), F32),
                pltpu.VMEM((cx * cy, span * LANES), BF16),
                pltpu.VMEM((cx * 2 * SUB, 2 * kf), BF16),
                pltpu.VMEM((cx * 4 * SUB, cols), F32),
                pltpu.VMEM((2 * STEPS * cy, cols), F32),
                pltpu.VMEM((1, picks), jnp.int32),
                pltpu.VMEM((picks, cx, cy), BF16),
                pltpu.VMEM((picks * cx, LANES), F32),
                pltpu.VMEM((picks, cx * cy), BF16),
                pltpu.VMEM((2, picks, STEPS * cy), BF16),
                pltpu.VMEM((picks * groups, LANES), F32),
                pltpu.VMEM((n - 1, tile, LANES), F32),
                dma,
                dma,
                dma,
                dma((2,)),
                dma((len(DIRS), chunks)),
                dma((len(DIRS), chunks)),
                dma((len(DIRS),)),
                dma((len(DIRS),)),
                dma((2,)),
                dma((2,)),
                dma,
                dma,
                pltpu.SemaphoreType.REGULAR((len(far_rounds(nx, ny)),)),
            ],
            compiler_params=pltpu.CompilerParams(
                collective_id=0, has_side_effects=True, vmem_limit_bytes=56 << 20
            ),
        )(adjoint, conduct_x, conduct_y, pick_weights, owner_order.reshape(1, picks))
        return pl.pallas_call(
            store_kernel,
            out_shape=(
                jax.ShapeDtypeStruct((cx, cy, cols), BF16),
                jax.ShapeDtypeStruct((picks // n, cols), F32),
            ),
            in_specs=[vmem, vmem],
            out_specs=(hbm, hbm),
            scratch_shapes=[dma((3,))],
        )(*[pltpu.with_memory_space_constraint(v, pltpu.VMEM) for v in (field, owned)])

    return jax.shard_map(
        per_device,
        mesh=mesh,
        in_specs=(P("gx", "gy", None), P("gx", "gy"), P("gx", "gy"), P(None, "gx", "gy"), P()),
        out_specs=(P("gx", "gy", None), P(("gx", "gy"), None)),
        check_vma=False,
    )
```
